512 devices in a mesh: seq: 64 (over z, y), tp: 8 (over x, core).
Axes of the slice: x: 4, y: 4, z: 16, core: 2. Of those that a mesh axis runs over, the one named last changes fastest.
Arguments:
- hidden: bfloat16 [384, 2048], P(None, 'seq'), may hold values from -12 to 12
- ln1_gain: float32 [2048], P('seq'), may hold values from 0.1 to 1.9
- wq: bfloat16 [2048, 2048], P('seq', 'tp'), may hold values from -0.125 to 0.125
- wk: bfloat16 [2048, 1024], P('seq', 'tp'), may hold values from -0.125 to 0.125
- wv: bfloat16 [2048, 1024], P('seq', 'tp'), may hold values from -0.125 to 0.125
- wg: bfloat16 [2048, 2048], P('seq', 'tp'), may hold values from -0.125 to 0.125
- q_gain: float32 [128], replicated, may hold values from 1 to 30
- key_gain: float32 [128], replicated, may hold values from 0.5 to 1.5
- wo: bfloat16 [2048, 2048], P('tp', 'seq'), may hold values from -0.5 to 0.5
- ln2_gain: float32 [2048], P('seq'), may hold values from 0.1 to 1.9
- w_gate: bfloat16 [2048, 6144], P('seq', 'tp'), may hold values from -0.125 to 0.125
- w_up: bfloat16 [2048, 6144], P('seq', 'tp'), may hold values from -0.125 to 0.125
- w_down: bfloat16 [6144, 2048], P('tp', 'seq'), may hold values from -0.078125 to 0.078125
- last_gain: float32 [2048], P('seq'), may hold values from 0.1 to 1.9
- head_weight: bfloat16 [2048, 131072], P(None, ('seq', 'tp')), may hold values from -0.125 to 0.125
- inv_temp: float32 [8], replicated, may hold values from 0.5 to 64
- key_cache: bfloat16 [8, 16384, 1024], P(None, 'seq', 'tp'), may hold values from -40 to 40
- value_cache: bfloat16 [8, 16384, 1024], P(None, 'seq', 'tp'), may hold values from -6 to 6
- lengths: int32 [8], replicated, may hold values from 1 to 16336
- parents: int32 [8, 48], replicated, may hold values from 0 to 46, as said below
- accepted: int32 [8], replicated, may hold values from 0 to 47
Outputs:
- logprobs: float32 [384, 131072], P(None, ('seq', 'tp'))
- next_hidden: bfloat16 [384, 2048], P(None, 'seq')
- updated_key_cache: bfloat16 [8, 16384, 1024], P(None, 'seq', 'tp')
- updated_value_cache: bfloat16 [8, 16384, 1024], P(None, 'seq', 'tp')
The draws below stay inside these ranges and needn't reach their ends.
Inputs may be any that keep to these rules, and one draw needn't show every extreme that they name: parents[r, 0] = 0; for i >= 1, i - 4 <= parents[r, i] < i.
All inputs are finite; a program needn't handle non-finite values.
Results may differ from the reference program's by a relative error of at most 0.012.
Values may be sent and summed in bfloat16 or wider, within the bound.
No kernel may reach another device: no remote copies, remote signals or barrier semaphores. Data moves between devices by JAX's collectives and lax.ppermute only.
A program may use at most 128 MiB of HBM per device.

```python
import math
import jax
import jax.numpy as jnp
from jax import lax

MODEL_DIM = 2048
QUERY_HEADS = 16
KEY_HEADS = 8
HEAD_SIZE = 128
FF = 6144
TREE_TOKENS = 48
REQUEST_COUNT = 8
TOKEN_TOTAL = 384
CACHE_SLOTS = 16384
VOCAB = 131072


def draw_hidden(key, part):
    columns = jnp.arange(MODEL_DIM, dtype=jnp.float32) / MODEL_DIM
    base = jnp.clip(jax.random.normal(key, (REQUEST_COUNT * TREE_TOKENS, MODEL_DIM), jnp.float32), -4.0, 4.0)
    return (base * jnp.exp(columns * math.log(10.0))[None, :] / 3.5).astype(jnp.bfloat16)


def draw_q_gain(key, part):
    base = jax.random.uniform(key, (HEAD_SIZE,), jnp.float32, 1.0, 3.0)
    return base


def draw_inv_temp(key, part):
    lowest, highest = (0.5, 2.0)
    values = jnp.exp(jax.random.uniform(key, (REQUEST_COUNT,), jnp.float32, math.log(lowest), math.log(highest)))
    picked = jax.random.randint(jax.random.fold_in(key, 3), (), 0, REQUEST_COUNT)
    return jnp.where(jnp.arange(REQUEST_COUNT) == picked, highest, values)


def draw_key_cache(key, part):
    shape_everything = (REQUEST_COUNT, CACHE_SLOTS, KEY_HEADS * HEAD_SIZE)
    return jnp.clip(jax.random.normal(key, shape_everything, jnp.float32), -6.0, 6.0).astype(jnp.bfloat16)


def draw_lengths(key, part):
    highest = CACHE_SLOTS - TREE_TOKENS
    values = jax.random.randint(key, (REQUEST_COUNT,), 1, highest + 1)
    picked = jax.random.randint(jax.random.fold_in(key, 7), (), 0, REQUEST_COUNT)
    return jnp.where(jnp.arange(REQUEST_COUNT) == picked, highest, values).astype(jnp.int32)


def draw_parents(key, part):
    node_ids = jnp.arange(TREE_TOKENS, dtype=jnp.int32)
    lowest = jnp.maximum(node_ids - 4, 0)
    highest = jnp.maximum(node_ids, 1)
    drawn = jax.random.randint(key, (REQUEST_COUNT, TREE_TOKENS), lowest[None, :], highest[None, :])
    return jnp.where(node_ids[None, :] == 0, 0, drawn).astype(jnp.int32)


def set_ends(array, rng, least, largest):
    index_at = [jax.random.randint(jax.random.fold_in(rng, axis), (), 0, length) for axis, length in enumerate(array.shape)]
    longest = array.shape.index(max(array.shape))
    next_to = index_at[:longest] + [(index_at[longest] + 1) % array.shape[longest]] + index_at[longest + 1:]
    return array.at[tuple(index_at)].set(least).at[tuple(next_to)].set(largest)


def shard_levels(rng, dims, shards, smallest, top_value):
    factor_of, own = 1.0, jax.random.fold_in(rng, 6)
    for position, parts in shards:
        heights = jnp.exp(jax.random.uniform(jax.random.fold_in(own, position), (parts,), jnp.float32, smallest / len(shards), top_value / len(shards)))
        factor_of = factor_of * jnp.repeat(heights, dims[position] // parts).reshape([-1 if axis == position else 1 for axis in range(len(dims))])
    return factor_of


def gaussian(own_key, extent, scale, limit, shards=(), kind=jnp.bfloat16):
    values = scale * jax.random.normal(own_key, extent, jnp.float32)
    if shards:
        values = values * shard_levels(own_key, extent, shards, -0.22, 0.18)
    return jnp.clip(values, -limit, limit).astype(kind)


def setup_inputs(seed: int = 0) -> dict:
    streams_of = jax.random.split(jax.random.key(seed), 22)
    return {
        "hidden": draw_hidden(jax.random.fold_in(streams_of[21], 71), 0),
        "ln1_gain": jnp.clip(1.0 + 0.18 * jax.random.normal(streams_of[1], (MODEL_DIM,), jnp.float32), 0.1, 1.9),
        "wq": gaussian(streams_of[2], (MODEL_DIM, QUERY_HEADS * HEAD_SIZE), MODEL_DIM ** -0.5, 0.125, ((0, 64), (1, 8))),
        "wk": gaussian(streams_of[3], (MODEL_DIM, KEY_HEADS * HEAD_SIZE), MODEL_DIM ** -0.5, 0.125, ((0, 64), (1, 8))),
        "wv": gaussian(streams_of[4], (MODEL_DIM, KEY_HEADS * HEAD_SIZE), MODEL_DIM ** -0.5, 0.125, ((0, 64), (1, 8))),
        "wg": gaussian(streams_of[5], (MODEL_DIM, QUERY_HEADS * HEAD_SIZE), MODEL_DIM ** -0.5, 0.125, ((0, 64), (1, 8))),
        "q_gain": draw_q_gain(jax.random.fold_in(streams_of[21], 71), 0),
        "key_gain": jnp.clip(jax.random.uniform(streams_of[7], (HEAD_SIZE,), jnp.float32, 0.5, 1.5), 0.5, 1.5),
        "wo": gaussian(streams_of[8], (QUERY_HEADS * HEAD_SIZE, MODEL_DIM), (QUERY_HEADS * HEAD_SIZE // 16) ** -0.5, 0.5, ((0, 8), (1, 64))),
        "ln2_gain": jnp.clip(1.0 + 0.18 * jax.random.normal(streams_of[9], (MODEL_DIM,), jnp.float32), 0.1, 1.9),
        "w_gate": gaussian(streams_of[10], (MODEL_DIM, FF), MODEL_DIM ** -0.5, 0.125, ((0, 64), (1, 8))),
        "w_up": gaussian(streams_of[11], (MODEL_DIM, FF), MODEL_DIM ** -0.5, 0.125, ((0, 64), (1, 8))),
        "w_down": gaussian(streams_of[12], (FF, MODEL_DIM), FF ** -0.5, 0.078125, ((0, 8), (1, 64))),
        "last_gain": jnp.clip(1.0 + 0.18 * jax.random.normal(streams_of[13], (MODEL_DIM,), jnp.float32), 0.1, 1.9),
        "head_weight": gaussian(streams_of[14], (MODEL_DIM, VOCAB), MODEL_DIM ** -0.5, 0.125, ((1, 512),)),
        "inv_temp": draw_inv_temp(jax.random.fold_in(streams_of[21], 71), 0),
        "key_cache": draw_key_cache(jax.random.fold_in(streams_of[21], 71), 0),
        "value_cache": gaussian(streams_of[17], (REQUEST_COUNT, CACHE_SLOTS, KEY_HEADS * HEAD_SIZE), 1.0, 6.0, ((1, 64), (2, 8))),
        "lengths": draw_lengths(jax.random.fold_in(streams_of[21], 71), 0),
        "parents": draw_parents(jax.random.fold_in(streams_of[21], 71), 0),
        "accepted": set_ends(jax.random.randint(streams_of[20], (REQUEST_COUNT,), 0, TREE_TOKENS), jax.random.fold_in(streams_of[20], 1), 0, TREE_TOKENS - 1).astype(jnp.int32),
    }


EPSILON = 1e-06
ROPE_BASE = 1000000.0
NEGATIVE = -1e+30

def ancestry(parents):
    node_count = parents.shape[-1]
    node_ids = jnp.arange(node_count, dtype=jnp.int32)
    reachable = (parents[..., :, None] == node_ids[None, :]).astype(jnp.float32)
    reachable = jnp.maximum(reachable, jnp.eye(node_count, dtype=jnp.float32))
    for turn in range((node_count - 1).bit_length()):
        reachable = jnp.minimum(jnp.einsum('rij,rjk->rik', reachable, reachable, precision=lax.Precision.HIGHEST), 1.0)
    return reachable

def norm_row(values, gain):
    meansq = lax.optimization_barrier(jnp.mean(values * values, axis=-1, keepdims=True))
    return values * lax.rsqrt(meansq + EPSILON) * gain

def apply_rotary(values, places):
    half_dim = values.shape[-1] // 2
    spread = ROPE_BASE ** (-jnp.arange(half_dim, dtype=jnp.float32) / half_dim)
    angles = places.astype(jnp.float32)[:, None] * spread[None, :]
    cosine = jnp.cos(angles)[:, None, :]
    sine = jnp.sin(angles)[:, None, :]
    lower_part = values[..., :half_dim]
    upper_part = values[..., half_dim:]
    return jnp.concatenate([lower_part * cosine - upper_part * sine, upper_part * cosine + lower_part * sine], axis=-1)

def attend_request(item):
    query_rows, cache_keys, cache_values, tree_keys, tree_values, length, parent_links = item
    query_wide = query_rows.astype(jnp.float32)
    cache_scores = jnp.einsum('ikgd,ckd->kgic', query_wide, cache_keys.astype(jnp.float32))
    tree_scores = jnp.einsum('ikgd,jkd->kgij', query_wide, tree_keys.astype(jnp.float32))
    valid_slot = (jnp.arange(cache_keys.shape[0], dtype=jnp.int32) < length)[None, None, None, :]
    valid_node = (parent_links > 0.5)[None, None, :, :]
    row_top = jnp.maximum(lax.optimization_barrier(jnp.max(jnp.where(valid_slot, cache_scores, NEGATIVE), axis=-1)), lax.optimization_barrier(jnp.max(jnp.where(valid_node, tree_scores, NEGATIVE), axis=-1)))
    cache_weights = jnp.where(valid_slot, jnp.exp(cache_scores - row_top[..., None]), 0.0)
    tree_weights = jnp.where(valid_node, jnp.exp(tree_scores - row_top[..., None]), 0.0)
    row_mass = lax.optimization_barrier(jnp.sum(cache_weights, axis=-1)) + lax.optimization_barrier(jnp.sum(tree_weights, axis=-1))
    weighted = jnp.einsum('kgic,ckd->kgid', cache_weights.astype(jnp.bfloat16).astype(jnp.float32), cache_values.astype(jnp.float32))
    weighted = weighted + jnp.einsum('kgij,jkd->kgid', tree_weights.astype(jnp.bfloat16).astype(jnp.float32), tree_values.astype(jnp.float32))
    result = weighted / row_mass[..., None]
    result = jnp.transpose(result, (2, 0, 1, 3))
    return result.reshape(result.shape[0], -1)

def write_request(item):
    old_keys, old_values, fresh_keys, fresh_values, length, tree_node_depth, path_row = item
    slot_ids = jnp.arange(old_keys.shape[0], dtype=jnp.int32)
    target = length + tree_node_depth
    placed = (slot_ids[:, None] == target[None, :]).astype(jnp.float32) * path_row[None, :]
    hits = (lax.optimization_barrier(jnp.sum(placed, axis=1)) > 0.5)[:, None]
    moved_keys = jnp.dot(placed.astype(jnp.bfloat16), fresh_keys, preferred_element_type=jnp.float32).astype(jnp.bfloat16)
    moved_values = jnp.dot(placed.astype(jnp.bfloat16), fresh_values, preferred_element_type=jnp.float32).astype(jnp.bfloat16)
    return (jnp.where(hits, moved_keys, old_keys), jnp.where(hits, moved_values, old_values))

def reference(hidden, ln1_gain, wq, wk, wv, wg, q_gain, key_gain, wo, ln2_gain, w_gate, w_up, w_down, last_gain, head_weight, inv_temp, key_cache, value_cache, lengths, parents, accepted):
    query_group_size = QUERY_HEADS // KEY_HEADS
    parent_links = ancestry(parents)
    tree_node_depth = lax.optimization_barrier(jnp.sum((parent_links > 0.5).astype(jnp.int32), axis=-1)) - 1
    token_position = (lengths[:, None] + tree_node_depth).reshape(-1)
    hidden_wide = hidden.astype(jnp.float32)
    normed1 = norm_row(hidden_wide, ln1_gain).astype(jnp.bfloat16)
    q_sum = jnp.dot(normed1, wq, preferred_element_type=jnp.float32)
    key_sum = jnp.dot(normed1, wk, preferred_element_type=jnp.float32)
    v_sum = jnp.dot(normed1, wv, preferred_element_type=jnp.float32)
    gate = jnp.dot(normed1, wg, preferred_element_type=jnp.float32)
    query_rows_all = apply_rotary(norm_row(q_sum.reshape(TOKEN_TOTAL, QUERY_HEADS, HEAD_SIZE), q_gain), token_position) * HEAD_SIZE ** (-0.5)
    query_rows_all = query_rows_all.astype(jnp.bfloat16)
    draft_keys = apply_rotary(norm_row(key_sum.reshape(TOKEN_TOTAL, KEY_HEADS, HEAD_SIZE), key_gain), token_position).astype(jnp.bfloat16)
    draft_values = v_sum.astype(jnp.bfloat16)
    attention_result = lax.map(attend_request, (query_rows_all.reshape(REQUEST_COUNT, TREE_TOKENS, KEY_HEADS, query_group_size, HEAD_SIZE), key_cache.reshape(REQUEST_COUNT, CACHE_SLOTS, KEY_HEADS, HEAD_SIZE), value_cache.reshape(REQUEST_COUNT, CACHE_SLOTS, KEY_HEADS, HEAD_SIZE), draft_keys.reshape(REQUEST_COUNT, TREE_TOKENS, KEY_HEADS, HEAD_SIZE), draft_values.reshape(REQUEST_COUNT, TREE_TOKENS, KEY_HEADS, HEAD_SIZE), lengths, parent_links))
    attention_result = attention_result.reshape(TOKEN_TOTAL, QUERY_HEADS * HEAD_SIZE)
    gated = (attention_result * jax.nn.sigmoid(gate)).astype(jnp.bfloat16)
    middle = (hidden_wide + jnp.dot(gated, wo, preferred_element_type=jnp.float32)).astype(jnp.bfloat16)
    normed2 = norm_row(middle.astype(jnp.float32), ln2_gain).astype(jnp.bfloat16)
    gate_part = jnp.dot(normed2, w_gate, preferred_element_type=jnp.float32)
    up_part = jnp.dot(normed2, w_up, preferred_element_type=jnp.float32)
    activated = (jax.nn.silu(gate_part) * up_part).astype(jnp.bfloat16)
    next_hidden = (middle.astype(jnp.float32) + jnp.dot(activated, w_down, preferred_element_type=jnp.float32)).astype(jnp.bfloat16)
    normed3 = norm_row(next_hidden.astype(jnp.float32), last_gain).astype(jnp.bfloat16)
    logits = jnp.dot(normed3, head_weight, preferred_element_type=jnp.float32) * jnp.repeat(inv_temp, TREE_TOKENS)[:, None]
    row_top = lax.optimization_barrier(jnp.max(logits, axis=1, keepdims=True))
    logprobs = logits - (row_top + jnp.log(lax.optimization_barrier(jnp.sum(jnp.exp(logits - row_top), axis=1, keepdims=True))))
    accepted_rows = parent_links[jnp.arange(REQUEST_COUNT), accepted]
    updated_key_cache, updated_value_cache = lax.map(write_request, (key_cache, value_cache, draft_keys.reshape(REQUEST_COUNT, TREE_TOKENS, KEY_HEADS * HEAD_SIZE), draft_values.reshape(REQUEST_COUNT, TREE_TOKENS, KEY_HEADS * HEAD_SIZE), lengths, tree_node_depth, accepted_rows))
    return (logprobs, next_hidden, updated_key_cache, updated_value_cache)
```

```python
import jax
import jax.numpy as jnp
from jax import lax
from jax.sharding import Mesh, PartitionSpec as P

EPSILON = 1e-06
ROPE_BASE = 1000000.0
NEGATIVE = -1e30
BF = jnp.bfloat16
F32 = jnp.float32


def ancestry(parents):
    node_count = parents.shape[-1]
    node_ids = jnp.arange(node_count, dtype=jnp.int32)
    reachable = (parents[..., :, None] == node_ids[None, :]).astype(BF)
    reachable = jnp.maximum(reachable, jnp.eye(node_count, dtype=BF))
    for turn in range((node_count - 1).bit_length()):
        reachable = jnp.minimum(
            jnp.einsum("rij,rjk->rik", reachable, reachable, preferred_element_type=F32), 1.0
        ).astype(BF)
    return reachable.astype(F32)


def head_norm(values, gain):
    meansq = jnp.mean(values * values, axis=-1, keepdims=True)
    return values * lax.rsqrt(meansq + EPSILON) * gain


def rotate(values, cosine, sine):
    half = values.shape[-1] // 2
    low, high = values[..., :half], values[..., half:]
    return jnp.concatenate([low * cosine - high * sine, high * cosine + low * sine], axis=-1)


def swap(values, axis):
    return lax.all_to_all(values, axis, 0, 0, tiled=True)


def spread(values, axis, count):
    return swap(jnp.broadcast_to(values[None], (count,) + values.shape), axis)


def split2(values):
    high = values.astype(BF)
    low = (values - high.astype(F32)).astype(BF)
    return high, low


def split3(values):
    high = values.astype(BF)
    rest = values - high.astype(F32)
    mid = rest.astype(BF)
    low = (rest - mid.astype(F32)).astype(BF)
    return high, mid, low


def pack_state(peak, mass, weighted):
    count = peak.shape[0]
    mass_high, mass_low = split2(mass)
    stats = jnp.stack([peak.astype(BF), mass_high, mass_low], axis=1).reshape(count, 6, 24)
    stats = jnp.pad(stats, ((0, 0), (0, 2), (0, 104)))
    return jnp.concatenate([weighted.astype(BF).reshape(count, 48, 128), stats], axis=1)


def merge_state(packed):
    count = packed.shape[0]
    weighted = packed[:, :48].reshape(count, 2, 24, 128).astype(F32)
    stats = packed[:, 48:54, :24].astype(F32).reshape(count, 3, 2, 24)
    peaks, masses = stats[:, 0], stats[:, 1] + stats[:, 2]
    peak = jnp.max(peaks, axis=0)
    factor = jnp.exp(peaks - peak)
    return peak, jnp.sum(masses * factor, axis=0), jnp.sum(weighted * factor[..., None], axis=0)


def on_device(
    hidden, ln1_gain, wq, wk, wv, wg, q_gain, key_gain, wo, ln2_gain, w_gate, w_up, w_down,
    last_gain, head_weight, inv_temp, key_cache, value_cache, lengths, parents, accepted,
):
    z, y, x, c = (lax.axis_index(name) for name in ("z", "y", "x", "c"))
    seq = z * 4 + y
    requests, tree = parents.shape
    slot_count = key_cache.shape[1]
    width = 2048

    token = jnp.arange(384, dtype=jnp.int32)
    token_y = (token // 6) % 4
    place = token_y * 128 + (token // 24) * 6 + token % 6
    scatter = (place[:, None] == jnp.arange(512, dtype=jnp.int32)[None, :]).astype(BF)
    hidden_t = jnp.dot(hidden.T, scatter, preferred_element_type=F32).astype(BF)
    gains = jnp.stack(split3(ln1_gain) + split3(ln2_gain) + split3(last_gain), axis=1)
    gains = jnp.pad(gains, ((0, 0), (96, 128 - 96 - 9)))
    down_t, wo_t = w_down.T, wo.T
    pieces = []
    for part in range(4):
        pieces.append(
            jnp.concatenate(
                [
                    w_gate[:, part * 192 : part * 192 + 192],
                    w_up[:, part * 192 : part * 192 + 192],
                    down_t[:, part * 192 : part * 192 + 192],
                    wo_t[:, part * 64 : part * 64 + 64],
                    wq,
                    wk,
                    wv,
                    wg,
                    hidden_t[:, part * 128 : part * 128 + 128] + gains,
                ],
                axis=1,
            )
        )
    mine = swap(jnp.stack(pieces), "y").reshape(128, 1536)
    ffn = lax.all_gather(mine[:, :640], "z", axis=0, tiled=True)
    proj = mine[:, 640:1408]
    side = mine[:, 1408:]
    side_wide = side.astype(F32)
    ln1_row = side_wide[:, 96:97] + side_wide[:, 97:98] + side_wide[:, 98:99]
    scaled = (side_wide * ln1_row).astype(BF)
    partial = lax.dot_general(scaled, proj, (((0,), (0,)), ((), ())), preferred_element_type=F32)
    sent = jnp.concatenate([partial[:96].astype(BF), side.T[:96]], axis=1).reshape(16, 6, 896)
    got = swap(sent, "z")
    sums = jnp.sum(got[:, :, :768].astype(F32), axis=0)
    rows = got[:, :, 768:]
    rows_wide = rows.astype(F32)
    squares = jnp.sum(rows_wide * rows_wide, axis=(0, 2))
    sums = sums * lax.rsqrt(squares / width + EPSILON)[:, None]

    links = ancestry(parents)
    depth = jnp.sum((links > 0.5).astype(jnp.int32), axis=-1) - 1
    target = lengths[:, None] + depth
    my_places = lax.dynamic_slice(target.reshape(-1), (z * 24 + y * 6,), (6,))
    inverse = ROPE_BASE ** (-jnp.arange(64, dtype=F32) / 64)
    angles = my_places.astype(F32)[:, None] * inverse[None, :]
    cosine, sine = jnp.cos(angles)[:, None, :], jnp.sin(angles)[:, None, :]
    query = rotate(head_norm(sums[:, :256].reshape(6, 2, 128), q_gain), cosine, sine) * 128 ** (-0.5)
    new_key = rotate(head_norm(sums[:, 256:384].reshape(6, 1, 128), key_gain), cosine, sine)
    outgate = jax.nn.sigmoid(sums[:, 512:])
    mine6 = jnp.concatenate(
        [query.reshape(6, 256), new_key.reshape(6, 128), sums[:, 384:512], outgate], axis=1
    ).astype(BF)
    gain_row = side[:, 99:105].T.reshape(1, 768)
    block = jnp.concatenate([mine6, gain_row, jnp.zeros((1, 768), BF)], axis=0)
    gathered = spread(block, "z", 16)
    gain_all = gathered[:, 6].reshape(16, 6, 128).astype(F32)
    ln2_all = gain_all[:, 0] + gain_all[:, 1] + gain_all[:, 2]
    last_all = gain_all[:, 3] + gain_all[:, 4] + gain_all[:, 5]
    tokens = spread(gathered[:, :6].reshape(96, 768), "y", 4).reshape(384, 768)
    order = token_y * 96 + (token // 24) * 6 + token % 6
    gather = (order[:, None] == token[None, :]).astype(BF)
    tokens = jnp.dot(gather, tokens, preferred_element_type=F32).astype(BF)
    queries = tokens[:, :256].reshape(requests, tree, 2, 128)
    tree_keys = tokens[:, 256:384].reshape(requests, tree, 128)
    tree_values = tokens[:, 384:512].reshape(requests, tree, 128)
    gates = tokens[:, 512:]

    slot_ids = seq * slot_count + jnp.arange(slot_count, dtype=jnp.int32)
    valid_slot = (slot_ids[None, :] < lengths[:, None])[:, None, None, :]
    valid_node = ((links > 0.5) & (seq == 0))[:, None, :, :]
    scores = jnp.einsum("rigd,rcd->rgic", queries, key_cache, preferred_element_type=F32)
    tree_scores = jnp.einsum("rigd,rjd->rgij", queries, tree_keys, preferred_element_type=F32)
    peak = jnp.maximum(
        jnp.max(jnp.where(valid_slot, scores, NEGATIVE), axis=-1),
        jnp.max(jnp.where(valid_node, tree_scores, NEGATIVE), axis=-1),
    )
    peak = lax.reduce_precision(peak, 8, 7)
    weights = jnp.where(valid_slot, jnp.exp(scores - peak[..., None]), 0.0)
    tree_weights = jnp.where(valid_node, jnp.exp(tree_scores - peak[..., None]), 0.0)
    mass = jnp.sum(weights, axis=-1) + jnp.sum(tree_weights, axis=-1)
    weighted = jnp.einsum(
        "rgic,rcd->rgid", weights.astype(BF), value_cache, preferred_element_type=F32
    ) + jnp.einsum("rgij,rjd->rgid", tree_weights.astype(BF), tree_values, preferred_element_type=F32)

    def by_z(values):
        split = values.reshape((requests, 2, 2, 24) + values.shape[3:])
        return jnp.swapaxes(split, 1, 2).reshape((16, 2, 24) + values.shape[3:])

    state = merge_state(swap(pack_state(by_z(peak), by_z(mass), by_z(weighted)), "z"))
    packed = pack_state(*(part[None] for part in state))[0]
    both = spread(jnp.concatenate([packed, rows.reshape(96, 128)], axis=0), "y", 4)
    peak, mass, weighted = merge_state(both[:, :56])
    my_gate = lax.dynamic_slice(gates, (z * 24, 0), (24, 256)).reshape(24, 2, 128)
    my_gate = jnp.swapaxes(my_gate, 0, 1).astype(F32)
    gated = (weighted / mass[..., None] * my_gate).astype(BF)
    gated = lax.dynamic_index_in_dim(gated, y // 2, 0, keepdims=False)
    gated = jnp.where(y % 2 == 0, gated[:, :64], gated[:, 64:])
    column = y * 4 + x
    hidden_mine = lax.dynamic_index_in_dim(
        both[:, 56:].reshape(4, 16, 6, 128), column, 1, keepdims=False
    ).reshape(24, 128)

    def reduce_columns(part):
        part = jnp.swapaxes(part.astype(BF).reshape(24, 16, 128), 0, 1)
        part = jnp.sum(swap(part, ("y", "x")).astype(F32), axis=0)
        return part + lax.ppermute(part, "c", [(0, 1), (1, 0)])

    attn = lax.dot_general(gated, ffn[:, 576:], (((1,), (1,)), ((), ())), preferred_element_type=F32)
    middle = (hidden_mine.astype(F32) + reduce_columns(attn)).astype(BF)
    middle_all = spread(middle, ("y", "x"), 16).astype(F32)
    squares_mid = jnp.sum(middle_all * middle_all, axis=(0, 2))
    scale_mid = lax.rsqrt(squares_mid / width + EPSILON)
    normed2 = (middle_all * scale_mid[None, :, None] * ln2_all[:, None, :]).astype(BF)
    normed2 = jnp.swapaxes(normed2, 0, 1).reshape(24, width)
    hidden_units = jnp.dot(normed2, ffn[:, :384], preferred_element_type=F32)
    activated = (jax.nn.silu(hidden_units[:, :192]) * hidden_units[:, 192:]).astype(BF)
    down = lax.dot_general(
        activated, ffn[:, 384:576], (((1,), (1,)), ((), ())), preferred_element_type=F32
    )
    following = (middle.astype(F32) + reduce_columns(down)).astype(BF)

    half = spread(following, "z", 16).reshape(384, 128)
    half = lax.dynamic_slice(half, (c * 192, 0), (192, 128))
    half = spread(spread(half, "y", 4), "x", 4)
    other = lax.ppermute(half, "c", [(0, 1), (1, 0)])
    full = jnp.stack([jnp.where(c == 0, half, other), jnp.where(c == 0, other, half)])
    own = lax.dynamic_slice(full, (0, z % 4, z // 4, 0, 0), (2, 1, 1, 192, 128)).reshape(384, 128)
    next_hidden = lax.dynamic_slice(own, (0, y * 32), (384, 32))
    full = jnp.transpose(full, (0, 3, 2, 1, 4)).reshape(384, width)
    wide = full.astype(F32)
    squares_last = jnp.sum(wide * wide, axis=1)
    normed3 = (
        wide * lax.rsqrt(squares_last / width + EPSILON)[:, None] * last_all.reshape(1, width)
    ).astype(BF)
    logits = jnp.dot(normed3, head_weight, preferred_element_type=F32)
    logits = logits * jnp.repeat(inv_temp, tree)[:, None]
    top = jnp.max(logits, axis=1)
    spot = top + jnp.log(jnp.sum(jnp.exp(logits - top[:, None]), axis=1))
    for axis, count in ((("y", "x", "c"), 32), ("z", 16)):
        spots = spread(spot.reshape(3, 128), axis, count)
        top = jnp.max(spots, axis=0)
        spot = top + jnp.log(jnp.sum(jnp.exp(spots - top), axis=0))
    logprobs = logits - spot.reshape(384, 1)

    accepted_rows = links[jnp.arange(requests), accepted]
    placed = (slot_ids[None, :, None] == target[:, None, :]).astype(F32) * accepted_rows[:, None, :]
    hits = (jnp.sum(placed, axis=2) > 0.5)[:, :, None]
    placed = placed.astype(BF)
    moved_keys = jnp.einsum("rca,rae->rce", placed, tree_keys, preferred_element_type=F32).astype(BF)
    moved_values = jnp.einsum("rca,rae->rce", placed, tree_values, preferred_element_type=F32).astype(BF)
    return (
        logprobs,
        next_hidden,
        jnp.where(hits, moved_keys, key_cache),
        jnp.where(hits, moved_values, value_cache),
    )


def solution(mesh):
    grid = Mesh(mesh.devices.reshape(16, 4, 4, 2), ("z", "y", "x", "c"))
    seq, tp = ("z", "y"), ("x", "c")
    in_specs = (
        P(None, seq), P(seq), P(seq, tp), P(seq, tp), P(seq, tp), P(seq, tp), P(), P(),
        P(tp, seq), P(seq), P(seq, tp), P(seq, tp), P(tp, seq), P(seq),
        P(None, seq + tp), P(), P(None, seq, tp), P(None, seq, tp), P(), P(), P(),
    )
    out_specs = (P(None, seq + tp), P(None, seq), P(None, seq, tp), P(None, seq, tp))
    return jax.shard_map(on_device, mesh=grid, in_specs=in_specs, out_specs=out_specs, check_vma=False)
```

```python
import jax
import jax.numpy as jnp
from jax import lax
from jax.experimental import pallas as pl
from jax.experimental.pallas import tpu as pltpu
from jax.sharding import Mesh, PartitionSpec as P

EPSILON = 1e-06
ROPE_BASE = 1000000.0
NEGATIVE = -1e30
BF = jnp.bfloat16
F32 = jnp.float32


def ancestry(parents):
    node_count = parents.shape[-1]
    node_ids = jnp.arange(node_count, dtype=jnp.int32)
    reachable = (parents[..., :, None] == node_ids[None, :]).astype(BF)
    reachable = jnp.maximum(reachable, jnp.eye(node_count, dtype=BF))
    for turn in range((node_count - 1).bit_length()):
        reachable = jnp.minimum(
            jnp.einsum("rij,rjk->rik", reachable, reachable, preferred_element_type=F32), 1.0
        ).astype(BF)
    return reachable.astype(F32)


def head_norm(values, gain):
    meansq = jnp.mean(values * values, axis=-1, keepdims=True)
    return values * lax.rsqrt(meansq + EPSILON) * gain


def rotate(values, cosine, sine):
    half = values.shape[-1] // 2
    low, high = values[..., :half], values[..., half:]
    return jnp.concatenate([low * cosine - high * sine, high * cosine + low * sine], axis=-1)


def swap(values, axis):
    return lax.all_to_all(values, axis, 0, 0, tiled=True)


def spread(values, axis, count):
    return swap(jnp.broadcast_to(values[None], (count,) + values.shape), axis)


def split2(values):
    high = lax.reduce_precision(values, 8, 7)
    return high.astype(BF), (values - high).astype(BF)


def pack_kernel(hidden_ref, place_ref, gain_ref, gate_ref, up_ref, down_ref, wo_ref, wq_ref, wk_ref, wv_ref, wg_ref, out_ref):
    lanes = lax.broadcasted_iota(jnp.int32, (512, 384), 0)
    chosen = jnp.where(lanes == place_ref[0:1, :], 1.0, 0.0).astype(BF)
    moved = lax.dot_general(
        hidden_ref[...], chosen, (((1,), (1,)), ((), ())), preferred_element_type=F32
    )
    diagonal = lax.broadcasted_iota(jnp.int32, (32, 32), 0) == lax.broadcasted_iota(jnp.int32, (32, 32), 1)
    lane = lax.broadcasted_iota(jnp.int32, (32, 128), 1)
    extra = jnp.zeros((32, 128), F32)
    for which in range(3):
        rest = jnp.sum(jnp.where(diagonal, gain_ref[which : which + 1, :], 0.0), axis=1, keepdims=True)
        for digit in range(3):
            part = rest.astype(BF).astype(F32)
            extra = jnp.where(lane == 96 + which * 3 + digit, part, extra)
            rest = rest - part
    zeros = jnp.zeros((32, 64), BF)
    for y in range(4):
        tile = slice(y * 128, y * 128 + 128)
        start = 512 + y * 64
        side = slice(start, start + 64)
        out_ref[y, :, 0:128] = gate_ref[:, tile]
        out_ref[y, :, 128:256] = up_ref[:, tile]
        out_ref[y, :, 256:384] = down_ref[:, tile]
        out_ref[y, :, 384:640] = wo_ref[...]
        out_ref[y, :, 640:768] = jnp.concatenate([gate_ref[:, side], up_ref[:, side]], axis=1)
        out_ref[y, :, 768:896] = jnp.concatenate([down_ref[:, side], zeros], axis=1)
        out_ref[y, :, 896:1152] = wq_ref[...]
        out_ref[y, :, 1152:1280] = wk_ref[...]
        out_ref[y, :, 1280:1408] = wv_ref[...]
        out_ref[y, :, 1408:1664] = wg_ref[...]
        out_ref[y, :, 1664:1792] = (moved[:, tile] + extra).astype(BF)


def head_kernel(core_ref, temp_ref, tiles_ref, gain_ref, weight_ref, logits_ref, spot_ref, *, flip, width):
    rows = tiles_ref.shape[2]
    squares = jnp.zeros((rows, 128), F32)
    for column in range(16):
        tile = tiles_ref[column % 4, column // 4].astype(F32)
        squares = squares + tile * tile
    scale = lax.rsqrt(jnp.sum(squares, axis=1, keepdims=True) / width + EPSILON)
    total = jnp.zeros((rows, 256), F32)
    for pair in range(8):
        sides = []
        for column in (2 * pair, 2 * pair + 1):
            tile = tiles_ref[column % 4, column // 4].astype(F32)
            sides.append((tile * scale * gain_ref[column : column + 1, :]).astype(BF))
        total = total + jnp.dot(
            jnp.concatenate(sides, axis=1),
            weight_ref[pair * 256 : pair * 256 + 256, :],
            preferred_element_type=F32,
        )
    part = core_ref[0] if not flip else 1 - core_ref[0]
    row = lax.broadcasted_iota(jnp.int32, (rows, 1), 0)
    temps = jnp.zeros((rows, 1), F32)
    for request in range(4):
        here = (row >= request * 48) & (row < request * 48 + 48)
        temps = jnp.where(here, temp_ref[part * 4 + request], temps)
    logits = total * temps
    logits_ref[...] = logits
    top = jnp.max(logits, axis=1, keepdims=True)
    spot = top + jnp.log(jnp.sum(jnp.exp(logits - top), axis=1, keepdims=True))
    across = lax.broadcasted_iota(jnp.int32, (rows, 256), 0) == lax.broadcasted_iota(jnp.int32, (rows, 256), 1)
    spot_ref[...] = jnp.sum(jnp.where(across, spot, 0.0), axis=0, keepdims=True)


def head(core, temps, tiles, gains, weight, flip):
    rows = tiles.shape[2]
    vmem, smem = pl.BlockSpec(memory_space=pltpu.VMEM), pl.BlockSpec(memory_space=pltpu.SMEM)
    return pl.pallas_call(
        lambda *refs: head_kernel(*refs, flip=flip, width=2048),
        out_shape=(
            jax.ShapeDtypeStruct((rows, 256), F32),
            jax.ShapeDtypeStruct((1, 256), F32),
        ),
        in_specs=[smem, smem, vmem, vmem, vmem],
        out_specs=(vmem, vmem),
        cost_estimate=pl.CostEstimate(
            flops=2 * rows * 2048 * 256, bytes_accessed=2 * 2048 * (rows + 256), transcendentals=rows * 256
        ),
        name="head_flip" if flip else "head_own",
    )(core, temps, tiles, gains, weight)


def pack_state(peak, mass, weighted):
    count = peak.shape[0]
    mass_high, mass_low = split2(mass)
    stats = jnp.stack([peak.astype(BF), mass_high, mass_low], axis=1).reshape(count, 6, 24)
    stats = jnp.pad(stats, ((0, 0), (0, 2), (0, 104)))
    return jnp.concatenate([weighted.astype(BF).reshape(count, 48, 128), stats], axis=1)


def merge_state(packed):
    count = packed.shape[0]
    weighted = packed[:, :48].reshape(count, 2, 24, 128).astype(F32)
    stats = packed[:, 48:54, :24].astype(F32).reshape(count, 3, 2, 24)
    peaks, masses = stats[:, 0], stats[:, 1] + stats[:, 2]
    peak = jnp.max(peaks, axis=0)
    factor = jnp.exp(peaks - peak)
    return peak, jnp.sum(masses * factor, axis=0), jnp.sum(weighted * factor[..., None], axis=0)


def on_device(
    hidden, ln1_gain, wq, wk, wv, wg, q_gain, key_gain, wo, ln2_gain, w_gate, w_up, w_down,
    last_gain, head_weight, inv_temp, key_cache, value_cache, lengths, parents, accepted,
):
    z, y, x, c = (lax.axis_index(name) for name in ("z", "y", "x", "c"))
    seq = z * 4 + y
    requests, tree = parents.shape
    slot_count = key_cache.shape[1]
    width = 2048

    token = jnp.arange(384, dtype=jnp.int32)
    token_z = token % 192 // 12
    token_y = token // 192 * 2 + token % 12 // 6
    token_i = token % 6

    place = (token_y * 128 + token_z * 6 + token_i).reshape(1, 384)
    gains = jnp.stack([ln1_gain, ln2_gain, last_gain])
    vmem = pl.BlockSpec(memory_space=pltpu.VMEM)
    pieces = pl.pallas_call(
        pack_kernel,
        out_shape=jax.ShapeDtypeStruct((4, 32, 1792), BF),
        in_specs=[vmem] * 11,
        out_specs=vmem,
        name="pack",
    )(hidden.T, place, gains, w_gate, w_up, w_down.T, wo.T, wq, wk, wv, wg)
    mine = swap(pieces, "y").reshape(128, 1792)
    ffn = lax.all_gather(mine[:, :896], "z", axis=0, tiled=True)
    proj = mine[:, 896:1664]
    side = mine[:, 1664:]
    side_wide = side.astype(F32)
    ln1_row = side_wide[:, 96:97] + side_wide[:, 97:98] + side_wide[:, 98:99]
    scaled = (side_wide * ln1_row).astype(BF)
    partial = lax.dot_general(scaled, proj, (((0,), (0,)), ((), ())), preferred_element_type=F32)
    sent = jnp.concatenate([partial[:96].astype(BF), side.T[:96]], axis=1).reshape(16, 6, 896)
    got = swap(sent, "z")
    sums = jnp.sum(got[:, :, :768].astype(F32), axis=0)
    rows = got[:, :, 768:]
    rows_wide = rows.astype(F32)
    squares = jnp.sum(rows_wide * rows_wide, axis=(0, 2))
    sums = sums * lax.rsqrt(squares / width + EPSILON)[:, None]

    links = ancestry(parents)
    depth = jnp.sum((links > 0.5).astype(jnp.int32), axis=-1) - 1
    target = lengths[:, None] + depth
    first = y // 2 * 192 + z * 12 + y % 2 * 6
    my_places = lax.dynamic_slice(target.reshape(-1), (first,), (6,))
    inverse = ROPE_BASE ** (-jnp.arange(64, dtype=F32) / 64)
    angles = my_places.astype(F32)[:, None] * inverse[None, :]
    cosine, sine = jnp.cos(angles)[:, None, :], jnp.sin(angles)[:, None, :]
    query = rotate(head_norm(sums[:, :256].reshape(6, 2, 128), q_gain), cosine, sine) * 128 ** (-0.5)
    new_key = rotate(head_norm(sums[:, 256:384].reshape(6, 1, 128), key_gain), cosine, sine)
    outgate = jax.nn.sigmoid(sums[:, 512:]).astype(BF)
    block = jnp.concatenate(
        [
            query[:, 0], query[:, 1], new_key[:, 0], sums[:, 384:512],
            side[:, 99:105].T.astype(F32), jnp.zeros((2, 128), F32),
        ],
        axis=0,
    ).astype(BF)
    gathered = spread(block, "z", 16)
    gain_all = gathered[:, 24:30].astype(F32)
    ln2_all = gain_all[:, 0] + gain_all[:, 1] + gain_all[:, 2]
    last_all = gain_all[:, 3] + gain_all[:, 4] + gain_all[:, 5]
    pool = spread(gathered[:, :24].reshape(384, 128), "y", 4).reshape(1536, 128)
    origin = token_y * 384 + token_z * 24 + token_i
    origin = (jnp.arange(4, dtype=jnp.int32)[:, None] * 6 + origin[None, :]).reshape(1536)
    gather = (origin[:, None] == jnp.arange(1536, dtype=jnp.int32)[None, :]).astype(BF)
    tokens = jnp.dot(gather, pool, preferred_element_type=F32).astype(BF).reshape(4, requests, tree, 128)
    queries, tree_keys, tree_values = tokens[:2], tokens[2], tokens[3]

    slot_ids = seq * slot_count + jnp.arange(slot_count, dtype=jnp.int32)
    valid_slot = (slot_ids[None, :] < lengths[:, None])[:, None, None, :]
    valid_node = ((links > 0.5) & (seq == 0))[:, None, :, :]
    scores = jnp.einsum("grid,rcd->rgic", queries, key_cache, preferred_element_type=F32)
    tree_scores = jnp.einsum("grid,rjd->rgij", queries, tree_keys, preferred_element_type=F32)
    peak = jnp.maximum(
        jnp.max(jnp.where(valid_slot, scores, NEGATIVE), axis=-1),
        jnp.max(jnp.where(valid_node, tree_scores, NEGATIVE), axis=-1),
    )
    peak = lax.reduce_precision(peak, 8, 7)
    weights = jnp.where(valid_slot, jnp.exp(scores - peak[..., None]), 0.0)
    tree_weights = jnp.where(valid_node, jnp.exp(tree_scores - peak[..., None]), 0.0)
    mass = jnp.sum(weights, axis=-1) + jnp.sum(tree_weights, axis=-1)
    weighted = jnp.einsum(
        "rgic,rcd->rgid", weights.astype(BF), value_cache, preferred_element_type=F32
    ) + jnp.einsum("rgij,rjd->rgid", tree_weights.astype(BF), tree_values, preferred_element_type=F32)

    def by_z(values):
        rest = values.shape[3:]
        split = values.reshape((2, 4, 2, 4, 12) + rest)
        split = jnp.transpose(split, (1, 3, 2, 0, 4) + tuple(range(5, 5 + len(rest))))
        return split.reshape((16, 2, 24) + rest)

    outgoing = pack_state(by_z(peak), by_z(mass), by_z(weighted))
    state = merge_state(swap(outgoing, "z"))
    packed = pack_state(*(part[None] for part in state))[0]
    shared = jnp.concatenate([packed, rows.reshape(96, 128), outgate[:, :128], outgate[:, 128:]], axis=0)
    shared, ffn = lax.optimization_barrier((shared, ffn))
    both = spread(shared, "y", 4)
    peak, mass, weighted = merge_state(both[:, :56])
    my_gate = jnp.swapaxes(both[:, 152:].reshape(4, 2, 6, 128), 0, 1).reshape(2, 24, 128).astype(F32)
    gated = (weighted / mass[..., None] * my_gate).astype(BF)
    hidden_rows = jnp.swapaxes(both[:, 56:152].reshape(4, 16, 6, 128), 0, 1).reshape(16, 24, 128)

    attn = lax.dot_general(
        jnp.concatenate([gated[0], gated[1]], axis=1),
        ffn[:, 384:640],
        (((1,), (1,)), ((), ())),
        preferred_element_type=F32,
    )
    attn = jnp.sum(spread(attn.astype(BF), ("x", "c"), 8).astype(F32), axis=0)
    hidden_rows = jnp.swapaxes(hidden_rows, 0, 1).reshape(24, width)
    middle = (hidden_rows.astype(F32) + attn).astype(BF)
    middle_wide = middle.astype(F32)
    squares_mid = jnp.sum(middle_wide * middle_wide, axis=1)
    normed2 = (
        middle_wide * lax.rsqrt(squares_mid / width + EPSILON)[:, None] * ln2_all.reshape(1, width)
    ).astype(BF)
    units = jnp.dot(normed2, ffn[:, :256], preferred_element_type=F32)
    sides = jnp.dot(normed2, ffn[:, 640:768], preferred_element_type=F32)
    act = (jax.nn.silu(units[:, :128]) * units[:, 128:]).astype(BF)
    act_side = (jax.nn.silu(sides[:, :64]) * sides[:, 64:]).astype(BF)
    contract = (((1,), (1,)), ((), ()))
    down = lax.dot_general(act, ffn[:, 256:384], contract, preferred_element_type=F32) + lax.dot_general(
        act_side, ffn[:, 768:832], contract, preferred_element_type=F32
    )
    down = jnp.transpose(down.astype(BF).reshape(2, 12, 16, 128), (2, 0, 1, 3)).reshape(32, 12, 128)
    down = jnp.sum(swap(down, ("y", "x", "c")).astype(F32), axis=0)
    middle_mine = lax.dynamic_slice(middle, (c * 12, (y * 4 + x) * 128), (12, 128))
    following = (middle_mine.astype(F32) + down).astype(BF)

    half = spread(following, "z", 16).reshape(192, 128)
    half = spread(spread(half, "y", 4), "x", 4)
    other = lax.ppermute(half, "c", [(0, 1), (1, 0)])
    core = c.reshape(1)
    own_logits, own_spot = head(core, inv_temp, half, last_all, head_weight, False)
    other_logits, other_spot = head(core, inv_temp, other, last_all, head_weight, True)

    def in_order(mine_part, other_part):
        return jnp.concatenate(
            [jnp.where(c == 0, mine_part, other_part), jnp.where(c == 0, other_part, mine_part)], axis=0
        )

    def own_columns(tiles):
        return lax.dynamic_slice(tiles, (z % 4, z // 4, 0, 0), (1, 1, 192, 128)).reshape(192, 128)

    own = in_order(own_columns(half), own_columns(other))
    next_hidden = lax.dynamic_slice(own, (0, y * 32), (384, 32))
    spot = in_order(own_spot, other_spot).reshape(1, 512)
    for axis, count in ((("y", "x", "c"), 32), ("z", 16)):
        spots = spread(spot, axis, count)
        top = jnp.max(spots, axis=0)
        spot = top + jnp.log(jnp.sum(jnp.exp(spots - top), axis=0))
    spot = spot.reshape(2, 256)[:, :192].reshape(384, 1)
    logprobs = in_order(own_logits, other_logits) - spot

    accepted_rows = links[jnp.arange(requests), accepted]
    placed = (slot_ids[None, :, None] == target[:, None, :]).astype(F32) * accepted_rows[:, None, :]
    hits = (jnp.sum(placed, axis=2) > 0.5)[:, :, None]
    placed = placed.astype(BF)
    moved_keys = jnp.einsum("rca,rae->rce", placed, tree_keys, preferred_element_type=F32).astype(BF)
    moved_values = jnp.einsum("rca,rae->rce", placed, tree_values, preferred_element_type=F32).astype(BF)
    return (
        logprobs,
        next_hidden,
        jnp.where(hits, moved_keys, key_cache),
        jnp.where(hits, moved_values, value_cache),
    )


def solution(mesh):
    grid = Mesh(mesh.devices.reshape(16, 4, 4, 2), ("z", "y", "x", "c"))
    seq, tp = ("z", "y"), ("x", "c")
    in_specs = (
        P(None, seq), P(seq), P(seq, tp), P(seq, tp), P(seq, tp), P(seq, tp), P(), P(),
        P(tp, seq), P(seq), P(seq, tp), P(seq, tp), P(tp, seq), P(seq),
        P(None, seq + tp), P(), P(None, seq, tp), P(None, seq, tp), P(), P(), P(),
    )
    out_specs = (P(None, seq + tp), P(None, seq), P(None, seq, tp), P(None, seq, tp))
    return jax.shard_map(on_device, mesh=grid, in_specs=in_specs, out_specs=out_specs, check_vma=False)
```

```python
import jax
import jax.numpy as jnp
from jax import lax
from jax.experimental import pallas as pl
from jax.experimental.pallas import tpu as pltpu
from jax.sharding import Mesh, PartitionSpec as P

EPSILON = 1e-06
ROPE_BASE = 1000000.0
NEGATIVE = -1e30
BF = jnp.bfloat16
F32 = jnp.float32


def ancestry(parents):
    node_count = parents.shape[-1]
    node_ids = jnp.arange(node_count, dtype=jnp.int32)
    reachable = (parents[..., :, None] == node_ids[None, :]).astype(BF)
    reachable = jnp.maximum(reachable, jnp.eye(node_count, dtype=BF))
    for turn in range((node_count - 1).bit_length()):
        reachable = jnp.minimum(
            jnp.einsum("rij,rjk->rik", reachable, reachable, preferred_element_type=F32), 1.0
        ).astype(BF)
    return reachable.astype(F32)


def head_norm(values, gain):
    meansq = jnp.mean(values * values, axis=-1, keepdims=True)
    return values * lax.rsqrt(meansq + EPSILON) * gain


def rotate(values, cosine, sine):
    half = values.shape[-1] // 2
    low, high = values[..., :half], values[..., half:]
    return jnp.concatenate([low * cosine - high * sine, high * cosine + low * sine], axis=-1)


def swap(values, axis):
    return lax.all_to_all(values, axis, 0, 0, tiled=True)


def spread(values, axis, count):
    return swap(jnp.broadcast_to(values[None], (count,) + values.shape), axis)


def split2(values):
    high = lax.reduce_precision(values, 8, 7)
    return high.astype(BF), (values - high).astype(BF)


def pack_kernel(hidden_ref, ln1_ref, ln2_ref, last_ref, wq_ref, wk_ref, wv_ref, wg_ref, out_ref):
    lane = lax.broadcasted_iota(jnp.int32, (1, 512), 1)
    first = lane // 128
    local = lane - first * 128
    first_z = local // 6
    token = first // 2 * 192 + first_z * 12 + first % 2 * 6 + (local - first_z * 6)
    token = jnp.where(local < 96, token, -1)
    chosen = lax.broadcasted_iota(jnp.int32, (384, 512), 0) == token
    moved = jnp.dot(
        hidden_ref[...], jnp.where(chosen, 1.0, 0.0).astype(BF), preferred_element_type=F32
    )
    diagonal = lax.broadcasted_iota(jnp.int32, (32, 32), 0) == lax.broadcasted_iota(jnp.int32, (32, 32), 1)
    lane = lax.broadcasted_iota(jnp.int32, (32, 128), 1)
    extra = jnp.zeros((32, 128), F32)
    for which, gain_ref in enumerate((ln1_ref, ln2_ref, last_ref)):
        rest = jnp.sum(jnp.where(diagonal, gain_ref[...], 0.0), axis=1, keepdims=True)
        for digit in range(3):
            part = rest.astype(BF).astype(F32)
            extra = jnp.where(lane == 96 + which * 3 + digit, part, extra)
            rest = rest - part
    for y in range(4):
        out_ref[y, :, 0:256] = wq_ref[...]
        out_ref[y, :, 256:384] = wk_ref[...]
        out_ref[y, :, 384:512] = wv_ref[...]
        out_ref[y, :, 512:768] = wg_ref[...]
        out_ref[y, :, 768:896] = (moved[:, y * 128 : y * 128 + 128] + extra).astype(BF)


def head_kernel(core_ref, temp_ref, tiles_ref, gain_ref, weight_ref, logits_ref, spot_ref, *, flip, width):
    rows = tiles_ref.shape[2]
    squares = jnp.zeros((rows, 128), F32)
    for column in range(16):
        tile = tiles_ref[column // 4, column % 4].astype(F32)
        squares = squares + tile * tile
    scale = lax.rsqrt(jnp.sum(squares, axis=1, keepdims=True) / width + EPSILON)
    total = jnp.zeros((rows, 256), F32)
    for pair in range(8):
        sides, rights = [], []
        for column in (2 * pair, 2 * pair + 1):
            for quarter in range(4):
                start = (column // 4 * 4 + quarter) * 128 + column % 4 * 32
                rights.append(weight_ref[start : start + 32, :])
            tile = tiles_ref[column // 4, column % 4].astype(F32)
            sides.append((tile * scale * gain_ref[column : column + 1, :]).astype(BF))
        total = total + jnp.dot(
            jnp.concatenate(sides, axis=1),
            jnp.concatenate(rights, axis=0),
            preferred_element_type=F32,
        )
    part = core_ref[0] if not flip else 1 - core_ref[0]
    row = lax.broadcasted_iota(jnp.int32, (rows, 1), 0)
    temps = jnp.zeros((rows, 1), F32)
    for request in range(4):
        here = (row >= request * 48) & (row < request * 48 + 48)
        temps = jnp.where(here, temp_ref[part * 4 + request], temps)
    logits = total * temps
    logits_ref[...] = logits
    top = jnp.max(logits, axis=1, keepdims=True)
    spot = top + jnp.log(jnp.sum(jnp.exp(logits - top), axis=1, keepdims=True))
    across = lax.broadcasted_iota(jnp.int32, (rows, 256), 0) == lax.broadcasted_iota(jnp.int32, (rows, 256), 1)
    spot_ref[...] = jnp.sum(jnp.where(across, spot, 0.0), axis=0, keepdims=True)


def head(core, temps, tiles, gains, weight, flip):
    rows = tiles.shape[2]
    vmem, smem = pl.BlockSpec(memory_space=pltpu.VMEM), pl.BlockSpec(memory_space=pltpu.SMEM)
    return pl.pallas_call(
        lambda *refs: head_kernel(*refs, flip=flip, width=2048),
        out_shape=(
            jax.ShapeDtypeStruct((rows, 256), F32),
            jax.ShapeDtypeStruct((1, 256), F32),
        ),
        in_specs=[smem, smem, vmem, vmem, vmem],
        out_specs=(vmem, vmem),
        cost_estimate=pl.CostEstimate(
            flops=2 * rows * 2048 * 256, bytes_accessed=2 * 2048 * (rows + 256), transcendentals=rows * 256
        ),
        name="head_flip" if flip else "head_own",
    )(core, temps, tiles, gains, weight)


def pack_state(peak, mass, weighted):
    count = peak.shape[0]
    mass_high, mass_low = split2(mass)
    stats = jnp.stack([peak.astype(BF), mass_high, mass_low], axis=1).reshape(count, 6, 24)
    stats = jnp.pad(stats, ((0, 0), (0, 2), (0, 104)))
    return jnp.concatenate([weighted.astype(BF).reshape(count, 48, 128), stats], axis=1)


def merge_state(packed):
    count = packed.shape[0]
    weighted = packed[:, :48].reshape(count, 2, 24, 128).astype(F32)
    stats = packed[:, 48:54, :24].astype(F32).reshape(count, 3, 2, 24)
    peaks, masses = stats[:, 0], stats[:, 1] + stats[:, 2]
    peak = jnp.max(peaks, axis=0)
    factor = jnp.exp(peaks - peak)
    return peak, jnp.sum(masses * factor, axis=0), jnp.sum(weighted * factor[..., None], axis=0)


def on_device(
    hidden, ln1_gain, wq, wk, wv, wg, q_gain, key_gain, wo, ln2_gain, w_gate, w_up, w_down,
    last_gain, head_weight, inv_temp, key_cache, value_cache, lengths, parents, accepted,
):
    z, y, x, c = (lax.axis_index(name) for name in ("z", "y", "x", "c"))
    seq = z * 4 + y
    requests, tree = parents.shape
    slot_count = key_cache.shape[1]
    width = 2048

    token = jnp.arange(384, dtype=jnp.int32)
    token_z = token % 192 // 12
    token_y = token // 192 * 2 + token % 12 // 6
    token_i = token % 6

    ffn = jnp.concatenate([w_gate, w_up, w_down.T, wo.T], axis=1)
    ffn = lax.all_gather(ffn, "z", axis=0, tiled=True)
    vmem = pl.BlockSpec(memory_space=pltpu.VMEM)
    pieces = pl.pallas_call(
        pack_kernel,
        out_shape=jax.ShapeDtypeStruct((4, 32, 896), BF),
        in_specs=[vmem] * 8,
        out_specs=vmem,
        name="pack",
    )(hidden.T, *(gain.reshape(1, 32) for gain in (ln1_gain, ln2_gain, last_gain)), wq, wk, wv, wg)
    mine = swap(pieces, "y").reshape(128, 896)
    proj, side = mine[:, :768], mine[:, 768:]
    side_wide = side.astype(F32)
    ln1_row = side_wide[:, 96:97] + side_wide[:, 97:98] + side_wide[:, 98:99]
    scaled = (side_wide * ln1_row).astype(BF)
    partial = lax.dot_general(scaled, proj, (((0,), (0,)), ((), ())), preferred_element_type=F32)
    sent = jnp.concatenate([partial[:96].astype(BF), side.T[:96]], axis=1).reshape(16, 6, 896)
    got = swap(sent, "z")
    sums = jnp.sum(got[:, :, :768].astype(F32), axis=0)
    rows = got[:, :, 768:]
    rows_wide = rows.astype(F32)
    squares = jnp.sum(rows_wide * rows_wide, axis=(0, 2))
    sums = sums * lax.rsqrt(squares / width + EPSILON)[:, None]

    links = ancestry(parents)
    depth = jnp.sum((links > 0.5).astype(jnp.int32), axis=-1) - 1
    target = lengths[:, None] + depth
    first = y // 2 * 192 + z * 12 + y % 2 * 6
    my_places = lax.dynamic_slice(target.reshape(-1), (first,), (6,))
    inverse = ROPE_BASE ** (-jnp.arange(64, dtype=F32) / 64)
    angles = my_places.astype(F32)[:, None] * inverse[None, :]
    cosine, sine = jnp.cos(angles)[:, None, :], jnp.sin(angles)[:, None, :]
    query = rotate(head_norm(sums[:, :256].reshape(6, 2, 128), q_gain), cosine, sine) * 128 ** (-0.5)
    new_key = rotate(head_norm(sums[:, 256:384].reshape(6, 1, 128), key_gain), cosine, sine)
    outgate = jax.nn.sigmoid(sums[:, 512:]).astype(BF)
    block = jnp.concatenate(
        [
            query[:, 0], query[:, 1], new_key[:, 0], sums[:, 384:512],
            side[:, 99:105].T.astype(F32), jnp.zeros((2, 128), F32),
        ],
        axis=0,
    ).astype(BF)
    gathered = spread(block, "z", 16)
    gain_all = gathered[:, 24:30].astype(F32)
    ln2_mine = gain_all[:, 0] + gain_all[:, 1] + gain_all[:, 2]
    ln2_mine = lax.dynamic_slice(ln2_mine, (0, y * 32), (16, 32)).reshape(1, 512)
    last_all = gain_all[:, 3] + gain_all[:, 4] + gain_all[:, 5]
    last_all = jnp.swapaxes(last_all.reshape(4, 4, 4, 32), 1, 2).reshape(16, 128)
    pool = spread(gathered[:, :24].reshape(384, 128), "y", 4).reshape(1536, 128)
    origin = token_y * 384 + token_z * 24 + token_i
    origin = (jnp.arange(4, dtype=jnp.int32)[:, None] * 6 + origin[None, :]).reshape(1536)
    gather = (origin[:, None] == jnp.arange(1536, dtype=jnp.int32)[None, :]).astype(BF)
    tokens = jnp.dot(gather, pool, preferred_element_type=F32).astype(BF).reshape(4, requests, tree, 128)
    queries, tree_keys, tree_values = tokens[:2], tokens[2], tokens[3]

    slot_ids = seq * slot_count + jnp.arange(slot_count, dtype=jnp.int32)
    valid_slot = (slot_ids[None, :] < lengths[:, None])[:, None, None, :]
    valid_node = ((links > 0.5) & (seq == 0))[:, None, :, :]
    scores = jnp.einsum("grid,rcd->rgic", queries, key_cache, preferred_element_type=F32)
    tree_scores = jnp.einsum("grid,rjd->rgij", queries, tree_keys, preferred_element_type=F32)
    peak = jnp.maximum(
        jnp.max(jnp.where(valid_slot, scores, NEGATIVE), axis=-1),
        jnp.max(jnp.where(valid_node, tree_scores, NEGATIVE), axis=-1),
    )
    peak = lax.reduce_precision(peak, 8, 7)
    weights = jnp.where(valid_slot, jnp.exp(scores - peak[..., None]), 0.0)
    tree_weights = jnp.where(valid_node, jnp.exp(tree_scores - peak[..., None]), 0.0)
    mass = jnp.sum(weights, axis=-1) + jnp.sum(tree_weights, axis=-1)
    weighted = jnp.einsum(
        "rgic,rcd->rgid", weights.astype(BF), value_cache, preferred_element_type=F32
    ) + jnp.einsum("rgij,rjd->rgid", tree_weights.astype(BF), tree_values, preferred_element_type=F32)

    def by_z(values):
        rest = values.shape[3:]
        split = values.reshape((2, 4, 2, 4, 12) + rest)
        split = jnp.transpose(split, (1, 3, 2, 0, 4) + tuple(range(5, 5 + len(rest))))
        return split.reshape((16, 2, 24) + rest)

    outgoing = pack_state(by_z(peak), by_z(mass), by_z(weighted))
    outgoing, ffn = lax.optimization_barrier((outgoing, ffn))
    state = merge_state(swap(outgoing, "z"))
    packed = pack_state(*(part[None] for part in state))
    residual = jnp.transpose(rows.reshape(4, 4, 6, 4, 32), (3, 0, 2, 1, 4)).reshape(4, 24, 128)
    outgates = jnp.concatenate([outgate[:, :128], outgate[:, 128:]], axis=0)
    shared = jnp.concatenate(
        [jnp.broadcast_to(packed, (4, 56, 128)), residual, jnp.broadcast_to(outgates[None], (4, 12, 128))],
        axis=1,
    )
    both = swap(shared, "y")
    peak, mass, weighted = merge_state(both[:, :56])
    my_gate = jnp.swapaxes(both[:, 80:].reshape(4, 2, 6, 128), 0, 1).reshape(2, 24, 128).astype(F32)
    gated = (weighted / mass[..., None] * my_gate).astype(BF)
    hidden_rows = jnp.swapaxes(both[:, 56:80].reshape(4, 4, 6, 128), 1, 2).reshape(24, 512)

    contract = (((1,), (1,)), ((), ()))
    attn = lax.dot_general(
        jnp.concatenate([gated[0], gated[1]], axis=1),
        ffn[:, 2304:],
        contract,
        preferred_element_type=F32,
    )
    attn = jnp.sum(spread(attn.astype(BF), ("x", "c"), 8).astype(F32), axis=0)
    middle = (hidden_rows.astype(F32) + attn).astype(BF)
    middle_wide = middle.astype(F32)
    squares_mid = split2(jnp.sum(middle_wide * middle_wide, axis=1, keepdims=True))
    units = jnp.dot(
        (middle_wide * ln2_mine).astype(BF), ffn[:, :1536], preferred_element_type=F32
    ).astype(BF)
    squares_mid = jnp.pad(jnp.concatenate(squares_mid, axis=1), ((0, 0), (0, 126)))
    units = spread(jnp.concatenate([units, squares_mid], axis=1), "y", 4)
    units = jnp.sum(units.astype(F32), axis=0)
    scale_mid = lax.rsqrt((units[:, 1536:1537] + units[:, 1537:1538]) / width + EPSILON)
    act = (jax.nn.silu(units[:, :768] * scale_mid) * (units[:, 768:1536] * scale_mid)).astype(BF)
    down = lax.dot_general(act, ffn[:, 1536:2304], contract, preferred_element_type=F32)
    down = jnp.transpose(down.astype(BF).reshape(2, 12, 4, 128), (2, 0, 1, 3)).reshape(8, 12, 128)
    down = jnp.sum(swap(down, ("x", "c")).astype(F32), axis=0)
    middle_mine = lax.dynamic_slice(middle, (c * 12, x * 128), (12, 128))
    following = (middle_mine.astype(F32) + down).astype(BF)

    half = spread(following, "z", 16).reshape(192, 128)
    half = spread(spread(half, "y", 4), "x", 4)
    other = lax.ppermute(half, "c", [(0, 1), (1, 0)])
    core = c.reshape(1)
    own_logits, own_spot = head(core, inv_temp, half, last_all, head_weight, False)
    other_logits, other_spot = head(core, inv_temp, other, last_all, head_weight, True)

    def in_order(mine_part, other_part):
        return jnp.concatenate(
            [jnp.where(c == 0, mine_part, other_part), jnp.where(c == 0, other_part, mine_part)], axis=0
        )

    def own_columns(tiles):
        return lax.dynamic_slice(tiles, (z // 4, y, 0, 0), (1, 1, 192, 128)).reshape(192, 128)

    own = in_order(own_columns(half), own_columns(other))
    next_hidden = lax.dynamic_slice(own, (0, z % 4 * 32), (384, 32))
    spot = in_order(own_spot, other_spot).reshape(1, 512)
    for axis, count in ((("y", "x", "c"), 32), ("z", 16)):
        spots = spread(spot, axis, count)
        top = jnp.max(spots, axis=0)
        spot = top + jnp.log(jnp.sum(jnp.exp(spots - top), axis=0))
    spot = spot.reshape(2, 256)[:, :192].reshape(384, 1)
    logprobs = in_order(own_logits, other_logits) - spot

    accepted_rows = links[jnp.arange(requests), accepted]
    placed = (slot_ids[None, :, None] == target[:, None, :]).astype(F32) * accepted_rows[:, None, :]
    hits = (jnp.sum(placed, axis=2) > 0.5)[:, :, None]
    placed = placed.astype(BF)
    moved_keys = jnp.einsum("rca,rae->rce", placed, tree_keys, preferred_element_type=F32).astype(BF)
    moved_values = jnp.einsum("rca,rae->rce", placed, tree_values, preferred_element_type=F32).astype(BF)
    return (
        logprobs,
        next_hidden,
        jnp.where(hits, moved_keys, key_cache),
        jnp.where(hits, moved_values, value_cache),
    )


def solution(mesh):
    grid = Mesh(mesh.devices.reshape(16, 4, 4, 2), ("z", "y", "x", "c"))
    seq, tp = ("z", "y"), ("x", "c")
    in_specs = (
        P(None, seq), P(seq), P(seq, tp), P(seq, tp), P(seq, tp), P(seq, tp), P(), P(),
        P(tp, seq), P(seq), P(seq, tp), P(seq, tp), P(tp, seq), P(seq),
        P(None, seq + tp), P(), P(None, seq, tp), P(None, seq, tp), P(), P(), P(),
    )
    out_specs = (P(None, seq + tp), P(None, seq), P(None, seq, tp), P(None, seq, tp))
    return jax.shard_map(on_device, mesh=grid, in_specs=in_specs, out_specs=out_specs, check_vma=False)
```

```python
import jax
import jax.numpy as jnp
from jax import lax
from jax.experimental import pallas as pl
from jax.experimental.pallas import tpu as pltpu
from jax.sharding import Mesh, PartitionSpec as P

EPSILON = 1e-06
ROPE_BASE = 1000000.0
NEGATIVE = -1e30
BF = jnp.bfloat16
F32 = jnp.float32


def ancestry(parents):
    node_count = parents.shape[-1]
    node_ids = jnp.arange(node_count, dtype=jnp.int32)
    reachable = (parents[..., :, None] == node_ids[None, :]).astype(BF)
    reachable = jnp.maximum(reachable, jnp.eye(node_count, dtype=BF))
    for turn in range((node_count - 1).bit_length()):
        reachable = jnp.minimum(
            jnp.einsum("rij,rjk->rik", reachable, reachable, preferred_element_type=F32), 1.0
        ).astype(BF)
    return reachable.astype(F32)


def head_norm(values, gain):
    meansq = jnp.mean(values * values, axis=-1, keepdims=True)
    return values * lax.rsqrt(meansq + EPSILON) * gain


def rotate(values, cosine, sine):
    half = values.shape[-1] // 2
    low, high = values[..., :half], values[..., half:]
    return jnp.concatenate([low * cosine - high * sine, high * cosine + low * sine], axis=-1)


def swap(values, axis):
    return lax.all_to_all(values, axis, 0, 0, tiled=True)


def spread(values, axis, count):
    return swap(jnp.broadcast_to(values[None], (count,) + values.shape), axis)


def split2(values):
    high = lax.reduce_precision(values, 8, 7)
    return high.astype(BF), (values - high).astype(BF)


def pack_kernel(hidden_ref, ln1_ref, ln2_ref, last_ref, wq_ref, wk_ref, wv_ref, wg_ref, out_ref):
    lane = lax.broadcasted_iota(jnp.int32, (1, 512), 1)
    first = lane // 128
    local = lane - first * 128
    first_z = local // 6
    token = first // 2 * 192 + first_z * 12 + first % 2 * 6 + (local - first_z * 6)
    token = jnp.where(local < 96, token, -1)
    chosen = lax.broadcasted_iota(jnp.int32, (384, 512), 0) == token
    moved = jnp.dot(
        hidden_ref[...], jnp.where(chosen, 1.0, 0.0).astype(BF), preferred_element_type=F32
    )
    diagonal = lax.broadcasted_iota(jnp.int32, (32, 32), 0) == lax.broadcasted_iota(jnp.int32, (32, 32), 1)
    lane = lax.broadcasted_iota(jnp.int32, (32, 128), 1)
    extra = jnp.zeros((32, 128), F32)
    for which, gain_ref in enumerate((ln1_ref, ln2_ref, last_ref)):
        rest = jnp.sum(jnp.where(diagonal, gain_ref[...], 0.0), axis=1, keepdims=True)
        for digit in range(3):
            part = rest.astype(BF).astype(F32)
            extra = jnp.where(lane == 96 + which * 3 + digit, part, extra)
            rest = rest - part
    for y in range(4):
        out_ref[y, :, 0:256] = wq_ref[...]
        out_ref[y, :, 256:384] = wk_ref[...]
        out_ref[y, :, 384:512] = wv_ref[...]
        out_ref[y, :, 512:768] = wg_ref[...]
        out_ref[y, :, 768:896] = (moved[:, y * 128 : y * 128 + 128] + extra).astype(BF)


def head_kernel(core_ref, temp_ref, tiles_ref, gain_ref, weight_ref, logits_ref, spot_ref, *, flip, width):
    rows = tiles_ref.shape[1]
    squares = jnp.zeros((rows, 128), F32)
    for column in range(16):
        tile = tiles_ref[column % 4 * 4 + column // 4].astype(F32)
        squares = squares + tile * tile
    scale = lax.rsqrt(jnp.sum(squares, axis=1, keepdims=True) / width + EPSILON)
    total = jnp.zeros((rows, 256), F32)
    for pair in range(8):
        sides, rights = [], []
        for column in (2 * pair, 2 * pair + 1):
            for quarter in range(4):
                start = (column // 4 * 4 + quarter) * 128 + column % 4 * 32
                rights.append(weight_ref[start : start + 32, :])
            tile = tiles_ref[column % 4 * 4 + column // 4].astype(F32)
            sides.append((tile * scale * gain_ref[column : column + 1, :]).astype(BF))
        total = total + jnp.dot(
            jnp.concatenate(sides, axis=1),
            jnp.concatenate(rights, axis=0),
            preferred_element_type=F32,
        )
    part = core_ref[0] if not flip else 1 - core_ref[0]
    row = lax.broadcasted_iota(jnp.int32, (rows, 1), 0)
    temps = jnp.zeros((rows, 1), F32)
    for request in range(4):
        here = (row >= request * 48) & (row < request * 48 + 48)
        temps = jnp.where(here, temp_ref[part * 4 + request], temps)
    logits = total * temps
    logits_ref[...] = logits
    top = jnp.max(logits, axis=1, keepdims=True)
    spot = top + jnp.log(jnp.sum(jnp.exp(logits - top), axis=1, keepdims=True))
    across = lax.broadcasted_iota(jnp.int32, (rows, 256), 0) == lax.broadcasted_iota(jnp.int32, (rows, 256), 1)
    spot_ref[...] = jnp.sum(jnp.where(across, spot, 0.0), axis=0, keepdims=True)


def head(core, temps, tiles, gains, weight, flip):
    rows = tiles.shape[1]
    vmem, smem = pl.BlockSpec(memory_space=pltpu.VMEM), pl.BlockSpec(memory_space=pltpu.SMEM)
    return pl.pallas_call(
        lambda *refs: head_kernel(*refs, flip=flip, width=2048),
        out_shape=(
            jax.ShapeDtypeStruct((rows, 256), F32),
            jax.ShapeDtypeStruct((1, 256), F32),
        ),
        in_specs=[smem, smem, vmem, vmem, vmem],
        out_specs=(vmem, vmem),
        cost_estimate=pl.CostEstimate(
            flops=2 * rows * 2048 * 256, bytes_accessed=2 * 2048 * (rows + 256), transcendentals=rows * 256
        ),
        name="head_flip" if flip else "head_own",
    )(core, temps, tiles, gains, weight)


def pack_state(peak, mass, weighted):
    count = peak.shape[0]
    mass_high, mass_low = split2(mass)
    stats = jnp.stack([peak.astype(BF), mass_high, mass_low], axis=1).reshape(count, 6, 24)
    stats = jnp.pad(stats, ((0, 0), (0, 2), (0, 104)))
    return jnp.concatenate([weighted.astype(BF).reshape(count, 48, 128), stats], axis=1)


def merge_state(packed):
    count = packed.shape[0]
    weighted = packed[:, :48].reshape(count, 2, 24, 128).astype(F32)
    stats = packed[:, 48:54, :24].astype(F32).reshape(count, 3, 2, 24)
    peaks, masses = stats[:, 0], stats[:, 1] + stats[:, 2]
    peak = jnp.max(peaks, axis=0)
    factor = jnp.exp(peaks - peak)
    return peak, jnp.sum(masses * factor, axis=0), jnp.sum(weighted * factor[..., None], axis=0)


def on_device(
    hidden, ln1_gain, wq, wk, wv, wg, q_gain, key_gain, wo, ln2_gain, w_gate, w_up, w_down,
    last_gain, head_weight, inv_temp, key_cache, value_cache, lengths, parents, accepted,
):
    z, y, x, c = (lax.axis_index(name) for name in ("z", "y", "x", "c"))
    seq = z * 4 + y
    requests, tree = parents.shape
    slot_count = key_cache.shape[1]
    width = 2048

    token = jnp.arange(384, dtype=jnp.int32)
    token_z = token % 192 // 12
    token_y = token // 192 * 2 + token % 12 // 6
    token_i = token % 6

    ffn = jnp.concatenate([w_gate, w_up, w_down.T, wo.T], axis=1)
    ffn = lax.all_gather(ffn, "z", axis=0, tiled=True)
    vmem = pl.BlockSpec(memory_space=pltpu.VMEM)
    pieces = pl.pallas_call(
        pack_kernel,
        out_shape=jax.ShapeDtypeStruct((4, 32, 896), BF),
        in_specs=[vmem] * 8,
        out_specs=vmem,
        name="pack",
    )(hidden.T, *(gain.reshape(1, 32) for gain in (ln1_gain, ln2_gain, last_gain)), wq, wk, wv, wg)
    mine = swap(pieces, "y").reshape(128, 896)
    proj, side = mine[:, :768], mine[:, 768:]
    side_wide = side.astype(F32)
    ln1_row = side_wide[:, 96:97] + side_wide[:, 97:98] + side_wide[:, 98:99]
    scaled = (side_wide * ln1_row).astype(BF)
    partial = lax.dot_general(scaled, proj, (((0,), (0,)), ((), ())), preferred_element_type=F32)
    sent = jnp.concatenate([partial[:96].astype(BF), side.T[:96]], axis=1).reshape(16, 6, 896)
    got = swap(sent, "z")
    sums = jnp.sum(got[:, :, :768].astype(F32), axis=0)
    rows = got[:, :, 768:]
    rows_wide = rows.astype(F32)
    squares = jnp.sum(rows_wide * rows_wide, axis=(0, 2))
    sums = sums * lax.rsqrt(squares / width + EPSILON)[:, None]

    links = ancestry(parents)
    depth = jnp.sum((links > 0.5).astype(jnp.int32), axis=-1) - 1
    target = lengths[:, None] + depth
    first = y // 2 * 192 + z * 12 + y % 2 * 6
    my_places = lax.dynamic_slice(target.reshape(-1), (first,), (6,))
    inverse = ROPE_BASE ** (-jnp.arange(64, dtype=F32) / 64)
    angles = my_places.astype(F32)[:, None] * inverse[None, :]
    cosine, sine = jnp.cos(angles)[:, None, :], jnp.sin(angles)[:, None, :]
    query = rotate(head_norm(sums[:, :256].reshape(6, 2, 128), q_gain), cosine, sine) * 128 ** (-0.5)
    new_key = rotate(head_norm(sums[:, 256:384].reshape(6, 1, 128), key_gain), cosine, sine)
    outgate = jax.nn.sigmoid(sums[:, 512:]).astype(BF)
    block = jnp.concatenate(
        [
            query[:, 0], query[:, 1], new_key[:, 0], sums[:, 384:512],
            side[:, 99:105].T.astype(F32), jnp.zeros((2, 128), F32),
        ],
        axis=0,
    ).astype(BF)
    gathered = spread(block, "z", 16)
    gain_all = gathered[:, 24:30].astype(F32)
    ln2_mine = gain_all[:, 0] + gain_all[:, 1] + gain_all[:, 2]
    ln2_mine = lax.dynamic_slice(ln2_mine, (0, y * 32), (16, 32)).reshape(1, 512)
    last_all = gain_all[:, 3] + gain_all[:, 4] + gain_all[:, 5]
    last_all = jnp.swapaxes(last_all.reshape(4, 4, 4, 32), 1, 2).reshape(16, 128)
    pool = spread(gathered[:, :24].reshape(384, 128), "y", 4).reshape(1536, 128)
    origin = token_y * 384 + token_z * 24 + token_i
    origin = (jnp.arange(4, dtype=jnp.int32)[:, None] * 6 + origin[None, :]).reshape(1536)
    gather = (origin[:, None] == jnp.arange(1536, dtype=jnp.int32)[None, :]).astype(BF)
    tokens = jnp.dot(gather, pool, preferred_element_type=F32).astype(BF).reshape(4, requests, tree, 128)
    queries, tree_keys, tree_values = tokens[:2], tokens[2], tokens[3]

    slot_ids = seq * slot_count + jnp.arange(slot_count, dtype=jnp.int32)
    valid_slot = (slot_ids[None, :] < lengths[:, None])[:, None, None, :]
    valid_node = ((links > 0.5) & (seq == 0))[:, None, :, :]
    scores = jnp.einsum("grid,rcd->rgic", queries, key_cache, preferred_element_type=F32)
    tree_scores = jnp.einsum("grid,rjd->rgij", queries, tree_keys, preferred_element_type=F32)
    peak = jnp.maximum(
        jnp.max(jnp.where(valid_slot, scores, NEGATIVE), axis=-1),
        jnp.max(jnp.where(valid_node, tree_scores, NEGATIVE), axis=-1),
    )
    peak = lax.reduce_precision(peak, 8, 7)
    weights = jnp.where(valid_slot, jnp.exp(scores - peak[..., None]), 0.0)
    tree_weights = jnp.where(valid_node, jnp.exp(tree_scores - peak[..., None]), 0.0)
    mass = jnp.sum(weights, axis=-1) + jnp.sum(tree_weights, axis=-1)
    weighted = jnp.einsum(
        "rgic,rcd->rgid", weights.astype(BF), value_cache, preferred_element_type=F32
    ) + jnp.einsum("rgij,rjd->rgid", tree_weights.astype(BF), tree_values, preferred_element_type=F32)

    def by_z(values):
        rest = values.shape[3:]
        split = values.reshape((2, 4, 2, 4, 12) + rest)
        split = jnp.transpose(split, (1, 3, 2, 0, 4) + tuple(range(5, 5 + len(rest))))
        return split.reshape((16, 2, 24) + rest)

    outgoing = pack_state(by_z(peak), by_z(mass), by_z(weighted))
    accepted_rows = links[jnp.arange(requests), accepted]
    placed = (slot_ids[None, :, None] == target[:, None, :]).astype(F32) * accepted_rows[:, None, :]
    hits = (jnp.sum(placed, axis=2) > 0.5)[:, :, None]
    placed = placed.astype(BF)
    moved_keys = jnp.einsum("rca,rae->rce", placed, tree_keys, preferred_element_type=F32).astype(BF)
    moved_values = jnp.einsum("rca,rae->rce", placed, tree_values, preferred_element_type=F32).astype(BF)
    updated_keys = jnp.where(hits, moved_keys, key_cache)
    updated_values = jnp.where(hits, moved_values, value_cache)

    arrived, ffn, updated_keys, updated_values = lax.optimization_barrier(
        (swap(outgoing, "z"), ffn, updated_keys, updated_values)
    )
    state = merge_state(arrived)
    packed = pack_state(*(part[None] for part in state))
    residual = jnp.transpose(rows.reshape(4, 4, 6, 4, 32), (3, 0, 2, 1, 4)).reshape(4, 24, 128)
    outgates = jnp.concatenate([outgate[:, :128], outgate[:, 128:]], axis=0)
    shared = jnp.concatenate(
        [jnp.broadcast_to(packed, (4, 56, 128)), residual, jnp.broadcast_to(outgates[None], (4, 12, 128))],
        axis=1,
    )
    both = swap(shared, "y")
    peak, mass, weighted = merge_state(both[:, :56])
    my_gate = jnp.swapaxes(both[:, 80:].reshape(4, 2, 6, 128), 0, 1).reshape(2, 24, 128).astype(F32)
    gated = (weighted / mass[..., None] * my_gate).astype(BF)
    hidden_rows = jnp.swapaxes(both[:, 56:80].reshape(4, 4, 6, 128), 1, 2).reshape(24, 512)

    contract = (((1,), (1,)), ((), ()))
    attn = lax.dot_general(
        jnp.concatenate([gated[0], gated[1]], axis=1),
        ffn[:, 2304:],
        contract,
        preferred_element_type=F32,
    )
    attn = jnp.sum(spread(attn.astype(BF), ("x", "c"), 8).astype(F32), axis=0)
    middle = (hidden_rows.astype(F32) + attn).astype(BF)
    middle_wide = middle.astype(F32)
    squares_mid = split2(jnp.sum(middle_wide * middle_wide, axis=1, keepdims=True))
    units = jnp.dot(
        (middle_wide * ln2_mine).astype(BF), ffn[:, :1536], preferred_element_type=F32
    ).astype(BF)
    squares_mid = jnp.pad(jnp.concatenate(squares_mid, axis=1), ((0, 0), (0, 126)))
    units = spread(jnp.concatenate([units, squares_mid], axis=1), "y", 4)
    units = jnp.sum(units.astype(F32), axis=0)
    scale_mid = lax.rsqrt((units[:, 1536:1537] + units[:, 1537:1538]) / width + EPSILON)
    act = (jax.nn.silu(units[:, :768] * scale_mid) * (units[:, 768:1536] * scale_mid)).astype(BF)
    down = lax.dot_general(act, ffn[:, 1536:2304], contract, preferred_element_type=F32)
    down = jnp.transpose(down.astype(BF).reshape(2, 12, 4, 128), (2, 0, 1, 3)).reshape(8, 12, 128)
    down = jnp.sum(swap(down, ("x", "c")).astype(F32), axis=0)
    middle_mine = lax.dynamic_slice(middle, (c * 12, x * 128), (12, 128))
    following = (middle_mine.astype(F32) + down).astype(BF)

    half = spread(following, "z", 16).reshape(192, 128)
    half = spread(half, ("y", "x"), 16)
    other = lax.ppermute(half, "c", [(0, 1), (1, 0)])
    core = c.reshape(1)
    own_logits, own_spot = head(core, inv_temp, half, last_all, head_weight, False)
    other_logits, other_spot = head(core, inv_temp, other, last_all, head_weight, True)

    def in_order(mine_part, other_part):
        return jnp.concatenate(
            [jnp.where(c == 0, mine_part, other_part), jnp.where(c == 0, other_part, mine_part)], axis=0
        )

    def own_columns(tiles):
        return lax.dynamic_slice(tiles, (y * 4 + z // 4, 0, 0), (1, 192, 128)).reshape(192, 128)

    own = in_order(own_columns(half), own_columns(other))
    next_hidden = lax.dynamic_slice(own, (0, z % 4 * 32), (384, 32))
    spot = in_order(own_spot, other_spot).reshape(1, 512)
    for axis, count in ((("y", "x", "c"), 32), ("z", 16)):
        spots = spread(spot, axis, count)
        top = jnp.max(spots, axis=0)
        spot = top + jnp.log(jnp.sum(jnp.exp(spots - top), axis=0))
    spot = spot.reshape(2, 256)[:, :192].reshape(384, 1)
    logprobs = in_order(own_logits, other_logits) - spot

    return logprobs, next_hidden, updated_keys, updated_values


def solution(mesh):
    grid = Mesh(mesh.devices.reshape(16, 4, 4, 2), ("z", "y", "x", "c"))
    seq, tp = ("z", "y"), ("x", "c")
    in_specs = (
        P(None, seq), P(seq), P(seq, tp), P(seq, tp), P(seq, tp), P(seq, tp), P(), P(),
        P(tp, seq), P(seq), P(seq, tp), P(seq, tp), P(tp, seq), P(seq),
        P(None, seq + tp), P(), P(None, seq, tp), P(None, seq, tp), P(), P(), P(),
    )
    out_specs = (P(None, seq + tp), P(None, seq), P(None, seq, tp), P(None, seq, tp))
    return jax.shard_map(on_device, mesh=grid, in_specs=in_specs, out_specs=out_specs, check_vma=False)
```

```python
import jax
import jax.numpy as jnp
from jax import lax
from jax.experimental import pallas as pl
from jax.experimental.pallas import tpu as pltpu
from jax.sharding import Mesh, PartitionSpec as P

EPSILON = 1e-06
ROPE_BASE = 1000000.0
NEGATIVE = -1e30
BF = jnp.bfloat16
F32 = jnp.float32


def ancestry(parents):
    node_count = parents.shape[-1]
    node_ids = jnp.arange(node_count, dtype=jnp.int32)
    reachable = (parents[..., :, None] == node_ids[None, :]).astype(BF)
    reachable = jnp.maximum(reachable, jnp.eye(node_count, dtype=BF))
    for turn in range((node_count - 1).bit_length()):
        reachable = jnp.minimum(
            jnp.einsum("rij,rjk->rik", reachable, reachable, preferred_element_type=F32), 1.0
        ).astype(BF)
    return reachable.astype(F32)


def head_norm(values, gain):
    meansq = jnp.mean(values * values, axis=-1, keepdims=True)
    return values * lax.rsqrt(meansq + EPSILON) * gain


def rotate(values, cosine, sine):
    half = values.shape[-1] // 2
    low, high = values[..., :half], values[..., half:]
    return jnp.concatenate([low * cosine - high * sine, high * cosine + low * sine], axis=-1)


def swap(values, axis):
    return lax.all_to_all(values, axis, 0, 0, tiled=True)


def spread(values, axis, count):
    return swap(jnp.broadcast_to(values[None], (count,) + values.shape), axis)


def split2(values):
    high = lax.reduce_precision(values, 8, 7)
    return high.astype(BF), (values - high).astype(BF)


def pack_kernel(hidden_ref, ln1_ref, ln2_ref, last_ref, wq_ref, wk_ref, wv_ref, wg_ref, out_ref):
    lane = lax.broadcasted_iota(jnp.int32, (1, 512), 1)
    first = lane // 128
    local = lane - first * 128
    token = jnp.where(local < 96, first * 96 + local, -1)
    chosen = lax.broadcasted_iota(jnp.int32, (384, 512), 0) == token
    moved = jnp.dot(
        hidden_ref[...], jnp.where(chosen, 1.0, 0.0).astype(BF), preferred_element_type=F32
    )
    diagonal = lax.broadcasted_iota(jnp.int32, (32, 32), 0) == lax.broadcasted_iota(jnp.int32, (32, 32), 1)
    lane = lax.broadcasted_iota(jnp.int32, (32, 128), 1)
    extra = jnp.zeros((32, 128), F32)
    for which, gain_ref in enumerate((ln1_ref, ln2_ref, last_ref)):
        rest = jnp.sum(jnp.where(diagonal, gain_ref[...], 0.0), axis=1, keepdims=True)
        for digit in range(3):
            part = rest.astype(BF).astype(F32)
            extra = jnp.where(lane == 96 + which * 3 + digit, part, extra)
            rest = rest - part
    for y in range(4):
        out_ref[y, :, 0:256] = wq_ref[...]
        out_ref[y, :, 256:384] = wk_ref[...]
        out_ref[y, :, 384:512] = wv_ref[...]
        out_ref[y, :, 512:768] = wg_ref[...]
        out_ref[y, :, 768:896] = (moved[:, y * 128 : y * 128 + 128] + extra).astype(BF)


def head_kernel(core_ref, temp_ref, tiles_ref, gain_ref, weight_ref, logits_ref, spot_ref, *, flip, width):
    rows = tiles_ref.shape[1]
    squares = jnp.zeros((rows, 128), F32)
    for column in range(16):
        tile = tiles_ref[column % 4 * 4 + column // 4].astype(F32)
        squares = squares + tile * tile
    scale = lax.rsqrt(jnp.sum(squares, axis=1, keepdims=True) / width + EPSILON)
    total = jnp.zeros((rows, 256), F32)
    for pair in range(8):
        sides, rights = [], []
        for column in (2 * pair, 2 * pair + 1):
            for quarter in range(4):
                start = (column // 4 * 4 + quarter) * 128 + column % 4 * 32
                rights.append(weight_ref[start : start + 32, :])
            tile = tiles_ref[column % 4 * 4 + column // 4].astype(F32)
            sides.append((tile * scale * gain_ref[column : column + 1, :]).astype(BF))
        total = total + jnp.dot(
            jnp.concatenate(sides, axis=1),
            jnp.concatenate(rights, axis=0),
            preferred_element_type=F32,
        )
    part = core_ref[0] if not flip else 1 - core_ref[0]
    row = lax.broadcasted_iota(jnp.int32, (rows, 1), 0)
    temps = jnp.zeros((rows, 1), F32)
    for request in range(4):
        here = (row >= request * 48) & (row < request * 48 + 48)
        temps = jnp.where(here, temp_ref[part * 4 + request], temps)
    logits = total * temps
    logits_ref[...] = logits
    top = jnp.max(logits, axis=1, keepdims=True)
    spot = top + jnp.log(jnp.sum(jnp.exp(logits - top), axis=1, keepdims=True))
    across = lax.broadcasted_iota(jnp.int32, (rows, 256), 0) == lax.broadcasted_iota(jnp.int32, (rows, 256), 1)
    spot_ref[...] = jnp.sum(jnp.where(across, spot, 0.0), axis=0, keepdims=True)


def head(core, temps, tiles, gains, weight, flip):
    rows = tiles.shape[1]
    vmem, smem = pl.BlockSpec(memory_space=pltpu.VMEM), pl.BlockSpec(memory_space=pltpu.SMEM)
    return pl.pallas_call(
        lambda *refs: head_kernel(*refs, flip=flip, width=2048),
        out_shape=(
            jax.ShapeDtypeStruct((rows, 256), F32),
            jax.ShapeDtypeStruct((1, 256), F32),
        ),
        in_specs=[smem, smem, vmem, vmem, vmem],
        out_specs=(vmem, vmem),
        cost_estimate=pl.CostEstimate(
            flops=2 * rows * 2048 * 256, bytes_accessed=2 * 2048 * (rows + 256), transcendentals=rows * 256
        ),
        name="head_flip" if flip else "head_own",
    )(core, temps, tiles, gains, weight)


def pack_state(peak, mass, weighted):
    count = peak.shape[0]
    mass_high, mass_low = split2(mass)
    stats = jnp.stack([peak.astype(BF), mass_high, mass_low], axis=1).reshape(count, 6, 6)
    stats = jnp.pad(stats, ((0, 0), (0, 0), (0, 122)))
    return jnp.concatenate([weighted.astype(BF).reshape(count, 12, 128), stats], axis=1)


def merge_state(packed):
    count = packed.shape[0]
    weighted = packed[:, :12].reshape(count, 2, 6, 128).astype(F32)
    stats = packed[:, 12:, :6].astype(F32).reshape(count, 3, 2, 6)
    peaks, masses = stats[:, 0], stats[:, 1] + stats[:, 2]
    factor = jnp.exp(peaks - jnp.max(peaks, axis=0))
    return jnp.sum(masses * factor, axis=0), jnp.sum(weighted * factor[..., None], axis=0)


def on_device(
    hidden, ln1_gain, wq, wk, wv, wg, q_gain, key_gain, wo, ln2_gain, w_gate, w_up, w_down,
    last_gain, head_weight, inv_temp, key_cache, value_cache, lengths, parents, accepted,
):
    z, y, x, c = (lax.axis_index(name) for name in ("z", "y", "x", "c"))
    seq = z * 4 + y
    requests, tree = parents.shape
    slot_count = key_cache.shape[1]
    width = 2048


    ffn = jnp.concatenate([w_gate, w_up, w_down.T, wo.T], axis=1)
    ffn = lax.all_gather(ffn, "z", axis=0, tiled=True)
    vmem = pl.BlockSpec(memory_space=pltpu.VMEM)
    pieces = pl.pallas_call(
        pack_kernel,
        out_shape=jax.ShapeDtypeStruct((4, 32, 896), BF),
        in_specs=[vmem] * 8,
        out_specs=vmem,
        name="pack",
    )(hidden.T, *(gain.reshape(1, 32) for gain in (ln1_gain, ln2_gain, last_gain)), wq, wk, wv, wg)
    mine = swap(pieces, "y").reshape(128, 896)
    proj, side = mine[:, :768], mine[:, 768:]
    side_wide = side.astype(F32)
    ln1_row = side_wide[:, 96:97] + side_wide[:, 97:98] + side_wide[:, 98:99]
    scaled = (side_wide * ln1_row).astype(BF)
    partial = lax.dot_general(scaled, proj, (((0,), (0,)), ((), ())), preferred_element_type=F32)
    sent = jnp.concatenate([partial[:96].astype(BF), side.T[:96]], axis=1).reshape(16, 6, 896)
    got = swap(sent, "z")
    sums = jnp.sum(got[:, :, :768].astype(F32), axis=0)
    rows = got[:, :, 768:]
    rows_wide = rows.astype(F32)
    squares = jnp.sum(rows_wide * rows_wide, axis=(0, 2))
    sums = sums * lax.rsqrt(squares / width + EPSILON)[:, None]

    links = ancestry(parents)
    depth = jnp.sum((links > 0.5).astype(jnp.int32), axis=-1) - 1
    target = lengths[:, None] + depth
    first = y * 96 + z * 6
    my_places = lax.dynamic_slice(target.reshape(-1), (first,), (6,))
    inverse = ROPE_BASE ** (-jnp.arange(64, dtype=F32) / 64)
    angles = my_places.astype(F32)[:, None] * inverse[None, :]
    cosine, sine = jnp.cos(angles)[:, None, :], jnp.sin(angles)[:, None, :]
    query = rotate(head_norm(sums[:, :256].reshape(6, 2, 128), q_gain), cosine, sine) * 128 ** (-0.5)
    new_key = rotate(head_norm(sums[:, 256:384].reshape(6, 1, 128), key_gain), cosine, sine)
    outgate = jax.nn.sigmoid(sums[:, 512:]).astype(BF)
    block = jnp.concatenate(
        [
            query[:, 0], query[:, 1], new_key[:, 0], sums[:, 384:512],
            side[:, 99:105].T.astype(F32), jnp.zeros((2, 128), F32),
        ],
        axis=0,
    ).astype(BF)
    caches = jnp.stack([key_cache, value_cache])
    parts = []
    for shift in range(4):
        part = lax.dynamic_slice(
            caches, (0, (y + shift) % 4 * 2, 0, 0), (2, 2, slot_count, 128)
        )
        if shift:
            part = lax.ppermute(part, "y", [(i, (i + shift) % 4) for i in range(4)])
        parts.append(part)
    moved = jnp.concatenate(parts, axis=2)
    gathered, moved = lax.optimization_barrier((spread(block, "z", 16), moved))
    gain_all = gathered[:, 24:30].astype(F32)
    ln2_mine = gain_all[:, 0] + gain_all[:, 1] + gain_all[:, 2]
    ln2_mine = lax.dynamic_slice(ln2_mine, (0, y * 32), (16, 32)).reshape(1, 512)
    last_all = gain_all[:, 3] + gain_all[:, 4] + gain_all[:, 5]
    last_all = jnp.swapaxes(last_all.reshape(4, 4, 4, 32), 1, 2).reshape(16, 128)
    spot96 = jnp.arange(96, dtype=jnp.int32)
    origin = jnp.arange(4, dtype=jnp.int32)[:, None] * 6 + (spot96 // 6 * 24 + spot96 % 6)[None, :]
    gather = (origin.reshape(384, 1) == jnp.arange(384, dtype=jnp.int32)[None, :]).astype(BF)
    tokens = jnp.dot(gather, gathered[:, :24].reshape(384, 128), preferred_element_type=F32).astype(BF)
    queries = tokens[:192].reshape(2, 2, tree, 128)
    tree_keys = tokens[192:288].reshape(2, tree, 128)
    tree_values = tokens[288:].reshape(2, tree, 128)

    keys, values = moved[0], moved[1]
    my_lengths = lax.dynamic_slice(lengths, (2 * y,), (2,))
    my_links = lax.dynamic_slice(links, (2 * y, 0, 0), (2, tree, tree))
    source = (y - jnp.arange(4, dtype=jnp.int32)) % 4 + z * 4
    row_slots = (source[:, None] * slot_count + jnp.arange(slot_count, dtype=jnp.int32)).reshape(-1)
    valid_slot = (row_slots[None, :] < my_lengths[:, None])[:, None, None, :]
    valid_node = ((my_links > 0.5) & (z == 0))[:, None, :, :]
    scores = jnp.einsum("grid,rcd->rgic", queries, keys, preferred_element_type=F32)
    tree_scores = jnp.einsum("grid,rjd->rgij", queries, tree_keys, preferred_element_type=F32)
    peak = jnp.maximum(
        jnp.max(jnp.where(valid_slot, scores, NEGATIVE), axis=-1),
        jnp.max(jnp.where(valid_node, tree_scores, NEGATIVE), axis=-1),
    )
    peak = lax.reduce_precision(peak, 8, 7)
    weights = jnp.where(valid_slot, jnp.exp(scores - peak[..., None]), 0.0)
    tree_weights = jnp.where(valid_node, jnp.exp(tree_scores - peak[..., None]), 0.0)
    mass = jnp.sum(weights, axis=-1) + jnp.sum(tree_weights, axis=-1)
    weighted = jnp.einsum(
        "rgic,rcd->rgid", weights.astype(BF), values, preferred_element_type=F32
    ) + jnp.einsum("rgij,rjd->rgid", tree_weights.astype(BF), tree_values, preferred_element_type=F32)

    def by_z(values):
        rest = values.shape[3:]
        return jnp.swapaxes(values.reshape((2, 2, 8, 6) + rest), 1, 2).reshape((16, 2, 6) + rest)

    outgoing = pack_state(by_z(peak), by_z(mass), by_z(weighted))
    arrived, ffn = lax.optimization_barrier((swap(outgoing, "z"), ffn))
    mass, weighted = merge_state(arrived)
    my_gate = jnp.swapaxes(outgate.reshape(6, 2, 128), 0, 1).astype(F32)
    gated = (weighted / mass[..., None] * my_gate).astype(BF).reshape(12, 128)
    residual = jnp.transpose(rows.reshape(4, 4, 6, 4, 32), (3, 0, 2, 1, 4)).reshape(4, 24, 128)
    same = jnp.concatenate([gated, tokens[192:]], axis=0)
    both = swap(jnp.concatenate([residual, jnp.broadcast_to(same[None], (4, 204, 128))], axis=1), "y")
    hidden_rows = jnp.swapaxes(both[:, :24].reshape(4, 4, 6, 128), 1, 2).reshape(24, 512)
    gated = jnp.swapaxes(both[:, 24:36].reshape(4, 2, 6, 128), 0, 1).reshape(2, 24, 128)
    tree_keys = both[:, 36:132].reshape(requests, tree, 128)
    tree_values = both[:, 132:].reshape(requests, tree, 128)

    slot_ids = seq * slot_count + jnp.arange(slot_count, dtype=jnp.int32)
    accepted_rows = links[jnp.arange(requests), accepted]
    placed = (slot_ids[None, :, None] == target[:, None, :]).astype(F32) * accepted_rows[:, None, :]
    hits = (jnp.sum(placed, axis=2) > 0.5)[:, :, None]
    placed = placed.astype(BF)
    moved_keys = jnp.einsum("rca,rae->rce", placed, tree_keys, preferred_element_type=F32).astype(BF)
    moved_values = jnp.einsum("rca,rae->rce", placed, tree_values, preferred_element_type=F32).astype(BF)
    updated_keys = jnp.where(hits, moved_keys, key_cache)
    updated_values = jnp.where(hits, moved_values, value_cache)

    contract = (((1,), (1,)), ((), ()))
    attn = lax.dot_general(
        jnp.concatenate([gated[0], gated[1]], axis=1),
        ffn[:, 2304:],
        contract,
        preferred_element_type=F32,
    )
    attn, updated_keys, updated_values = lax.optimization_barrier(
        (spread(attn.astype(BF), ("x", "c"), 8), updated_keys, updated_values)
    )
    attn = jnp.sum(attn.astype(F32), axis=0)
    middle = (hidden_rows.astype(F32) + attn).astype(BF)
    middle_wide = middle.astype(F32)
    squares_mid = split2(jnp.sum(middle_wide * middle_wide, axis=1, keepdims=True))
    units = jnp.dot(
        (middle_wide * ln2_mine).astype(BF), ffn[:, :1536], preferred_element_type=F32
    ).astype(BF)
    squares_mid = jnp.pad(jnp.concatenate(squares_mid, axis=1), ((0, 0), (0, 126)))
    units = spread(jnp.concatenate([units, squares_mid], axis=1), "y", 4)
    units = jnp.sum(units.astype(F32), axis=0)
    scale_mid = lax.rsqrt((units[:, 1536:1537] + units[:, 1537:1538]) / width + EPSILON)
    act = (jax.nn.silu(units[:, :768] * scale_mid) * (units[:, 768:1536] * scale_mid)).astype(BF)
    down = lax.dot_general(act, ffn[:, 1536:2304], contract, preferred_element_type=F32)
    down = jnp.transpose(down.astype(BF).reshape(2, 12, 4, 128), (2, 0, 1, 3)).reshape(8, 12, 128)
    down = jnp.sum(swap(down, ("x", "c")).astype(F32), axis=0)
    middle_mine = lax.dynamic_slice(middle, (c * 12, x * 128), (12, 128))
    following = (middle_mine.astype(F32) + down).astype(BF)

    half = spread(following, "z", 16).reshape(16, 2, 6, 128)
    half = jnp.swapaxes(half, 0, 1).reshape(192, 128)
    half = spread(half, ("y", "x"), 16)
    other = lax.ppermute(half, "c", [(0, 1), (1, 0)])
    core = c.reshape(1)
    own_logits, own_spot = head(core, inv_temp, half, last_all, head_weight, False)
    other_logits, other_spot = head(core, inv_temp, other, last_all, head_weight, True)

    def in_order(mine_part, other_part):
        return jnp.concatenate(
            [jnp.where(c == 0, mine_part, other_part), jnp.where(c == 0, other_part, mine_part)], axis=0
        )

    def own_columns(tiles):
        return lax.dynamic_slice(tiles, (y * 4 + z // 4, 0, 0), (1, 192, 128)).reshape(192, 128)

    own = in_order(own_columns(half), own_columns(other))
    next_hidden = lax.dynamic_slice(own, (0, z % 4 * 32), (384, 32))
    spot = in_order(own_spot, other_spot).reshape(1, 512)
    for axis, count in ((("y", "x", "c"), 32), ("z", 16)):
        spots = spread(spot, axis, count)
        top = jnp.max(spots, axis=0)
        spot = top + jnp.log(jnp.sum(jnp.exp(spots - top), axis=0))
    spot = spot.reshape(2, 256)[:, :192].reshape(384, 1)
    logprobs = in_order(own_logits, other_logits) - spot

    return logprobs, next_hidden, updated_keys, updated_values


def solution(mesh):
    grid = Mesh(mesh.devices.reshape(16, 4, 4, 2), ("z", "y", "x", "c"))
    seq, tp = ("z", "y"), ("x", "c")
    in_specs = (
        P(None, seq), P(seq), P(seq, tp), P(seq, tp), P(seq, tp), P(seq, tp), P(), P(),
        P(tp, seq), P(seq), P(seq, tp), P(seq, tp), P(tp, seq), P(seq),
        P(None, seq + tp), P(), P(None, seq, tp), P(None, seq, tp), P(), P(), P(),
    )
    out_specs = (P(None, seq + tp), P(None, seq), P(None, seq, tp), P(None, seq, tp))
    return jax.shard_map(on_device, mesh=grid, in_specs=in_specs, out_specs=out_specs, check_vma=False)
```

```python
import jax
import jax.numpy as jnp
from jax import lax
from jax.experimental import pallas as pl
from jax.experimental.pallas import tpu as pltpu
from jax.sharding import Mesh, PartitionSpec as P

EPSILON = 1e-06
ROPE_BASE = 1000000.0
NEGATIVE = -1e30
BF = jnp.bfloat16
F32 = jnp.float32


def ancestry(parents):
    node_count = parents.shape[-1]
    node_ids = jnp.arange(node_count, dtype=jnp.int32)
    reachable = (parents[..., :, None] == node_ids[None, :]).astype(BF)
    reachable = jnp.maximum(reachable, jnp.eye(node_count, dtype=BF))
    for turn in range((node_count - 1).bit_length()):
        reachable = jnp.minimum(
            jnp.einsum("rij,rjk->rik", reachable, reachable, preferred_element_type=F32), 1.0
        ).astype(BF)
    return reachable.astype(F32)


def head_norm(values, gain):
    meansq = jnp.mean(values * values, axis=-1, keepdims=True)
    return values * lax.rsqrt(meansq + EPSILON) * gain


def rotate(values, cosine, sine):
    half = values.shape[-1] // 2
    low, high = values[..., :half], values[..., half:]
    return jnp.concatenate([low * cosine - high * sine, high * cosine + low * sine], axis=-1)


def swap(values, axis):
    return lax.all_to_all(values, axis, 0, 0, tiled=True)


def spread(values, axis, count):
    return swap(jnp.broadcast_to(values[None], (count,) + values.shape), axis)


def split2(values):
    high = lax.reduce_precision(values, 8, 7)
    return high.astype(BF), (values - high).astype(BF)


def pack_kernel(hidden_ref, ln1_ref, ln2_ref, last_ref, wq_ref, wk_ref, wv_ref, wg_ref, out_ref):
    lane = lax.broadcasted_iota(jnp.int32, (1, 512), 1)
    first = lane // 128
    local = lane - first * 128
    token = jnp.where(local < 96, first * 96 + local, -1)
    chosen = lax.broadcasted_iota(jnp.int32, (384, 512), 0) == token
    moved = jnp.dot(
        hidden_ref[...], jnp.where(chosen, 1.0, 0.0).astype(BF), preferred_element_type=F32
    )
    diagonal = lax.broadcasted_iota(jnp.int32, (32, 32), 0) == lax.broadcasted_iota(jnp.int32, (32, 32), 1)
    lane = lax.broadcasted_iota(jnp.int32, (32, 128), 1)
    extra = jnp.zeros((32, 128), F32)
    for which, gain_ref in enumerate((ln1_ref, ln2_ref, last_ref)):
        rest = jnp.sum(jnp.where(diagonal, gain_ref[...], 0.0), axis=1, keepdims=True)
        for digit in range(3):
            part = rest.astype(BF).astype(F32)
            extra = jnp.where(lane == 96 + which * 3 + digit, part, extra)
            rest = rest - part
    for y in range(4):
        out_ref[y, :, 0:256] = wq_ref[...]
        out_ref[y, :, 256:384] = wk_ref[...]
        out_ref[y, :, 384:512] = wv_ref[...]
        out_ref[y, :, 512:768] = wg_ref[...]
        out_ref[y, :, 768:896] = (moved[:, y * 128 : y * 128 + 128] + extra).astype(BF)


def head_kernel(core_ref, temp_ref, tiles_ref, gain_ref, weight_ref, logits_ref, spot_ref, *, flip, width):
    rows = tiles_ref.shape[1]
    squares = jnp.zeros((rows, 128), F32)
    for column in range(16):
        tile = tiles_ref[column % 4 * 4 + column // 4].astype(F32)
        squares = squares + tile * tile
    scale = lax.rsqrt(jnp.sum(squares, axis=1, keepdims=True) / width + EPSILON)
    total = jnp.zeros((rows, 256), F32)
    for pair in range(8):
        sides, rights = [], []
        for column in (2 * pair, 2 * pair + 1):
            for quarter in range(4):
                start = (column // 4 * 4 + quarter) * 128 + column % 4 * 32
                rights.append(weight_ref[start : start + 32, :])
            tile = tiles_ref[column % 4 * 4 + column // 4].astype(F32)
            sides.append((tile * scale * gain_ref[column : column + 1, :]).astype(BF))
        total = total + jnp.dot(
            jnp.concatenate(sides, axis=1),
            jnp.concatenate(rights, axis=0),
            preferred_element_type=F32,
        )
    part = core_ref[0] if not flip else 1 - core_ref[0]
    row = lax.broadcasted_iota(jnp.int32, (rows, 1), 0)
    temps = jnp.zeros((rows, 1), F32)
    for request in range(4):
        here = (row >= request * 48) & (row < request * 48 + 48)
        temps = jnp.where(here, temp_ref[part * 4 + request], temps)
    logits = total * temps
    logits_ref[...] = logits
    top = jnp.max(logits, axis=1, keepdims=True)
    spot = top + jnp.log(jnp.sum(jnp.exp(logits - top), axis=1, keepdims=True))
    across = lax.broadcasted_iota(jnp.int32, (rows, 256), 0) == lax.broadcasted_iota(jnp.int32, (rows, 256), 1)
    spot_ref[...] = jnp.sum(jnp.where(across, spot, 0.0), axis=0, keepdims=True)


def head(core, temps, tiles, gains, weight, flip):
    rows = tiles.shape[1]
    vmem, smem = pl.BlockSpec(memory_space=pltpu.VMEM), pl.BlockSpec(memory_space=pltpu.SMEM)
    return pl.pallas_call(
        lambda *refs: head_kernel(*refs, flip=flip, width=2048),
        out_shape=(
            jax.ShapeDtypeStruct((rows, 256), F32),
            jax.ShapeDtypeStruct((1, 256), F32),
        ),
        in_specs=[smem, smem, vmem, vmem, vmem],
        out_specs=(vmem, vmem),
        cost_estimate=pl.CostEstimate(
            flops=2 * rows * 2048 * 256, bytes_accessed=2 * 2048 * (rows + 256), transcendentals=rows * 256
        ),
        name="head_flip" if flip else "head_own",
    )(core, temps, tiles, gains, weight)


def pack_state(peak, mass, weighted):
    count = peak.shape[0]
    mass_high, mass_low = split2(mass)
    stats = jnp.stack([peak.astype(BF), mass_high, mass_low], axis=1).reshape(count, 6, 6)
    stats = jnp.pad(stats, ((0, 0), (0, 0), (0, 122)))
    return jnp.concatenate([weighted.astype(BF).reshape(count, 12, 128), stats], axis=1)


def merge_state(packed):
    count = packed.shape[0]
    weighted = packed[:, :12].reshape(count, 2, 6, 128).astype(F32)
    stats = packed[:, 12:, :6].astype(F32).reshape(count, 3, 2, 6)
    peaks, masses = stats[:, 0], stats[:, 1] + stats[:, 2]
    factor = jnp.exp(peaks - jnp.max(peaks, axis=0))
    return jnp.sum(masses * factor, axis=0), jnp.sum(weighted * factor[..., None], axis=0)


def on_device(
    hidden, ln1_gain, wq, wk, wv, wg, q_gain, key_gain, wo, ln2_gain, w_gate, w_up, w_down,
    last_gain, head_weight, inv_temp, key_cache, value_cache, lengths, parents, accepted,
):
    z, y, x, c = (lax.axis_index(name) for name in ("z", "y", "x", "c"))
    seq = z * 4 + y
    requests, tree = parents.shape
    slot_count = key_cache.shape[1]
    width = 2048


    ffn = jnp.concatenate([w_gate, w_up, w_down.T, wo.T], axis=1)
    ffn = lax.all_gather(ffn, "z", axis=0, tiled=True)
    vmem = pl.BlockSpec(memory_space=pltpu.VMEM)
    pieces = pl.pallas_call(
        pack_kernel,
        out_shape=jax.ShapeDtypeStruct((4, 32, 896), BF),
        in_specs=[vmem] * 8,
        out_specs=vmem,
        name="pack",
    )(hidden.T, *(gain.reshape(1, 32) for gain in (ln1_gain, ln2_gain, last_gain)), wq, wk, wv, wg)
    mine = swap(pieces, "y").reshape(128, 896)
    proj, side = mine[:, :768], mine[:, 768:]
    side_wide = side.astype(F32)
    ln1_row = side_wide[:, 96:97] + side_wide[:, 97:98] + side_wide[:, 98:99]
    scaled = (side_wide * ln1_row).astype(BF)
    partial = lax.dot_general(scaled, proj, (((0,), (0,)), ((), ())), preferred_element_type=F32)
    sent = jnp.concatenate([partial[:96].astype(BF), side.T[:96]], axis=1).reshape(16, 6, 896)
    caches = jnp.stack([key_cache, value_cache])
    parts = [
        lax.dynamic_slice(caches, (0, (y + shift) % 4 * 2, 0, 0), (2, 2, slot_count, 128))
        for shift in range(4)
    ]
    sent, parts = lax.optimization_barrier((sent, parts))
    got = swap(sent, "z")
    for shift in range(1, 4):
        parts[shift] = lax.ppermute(parts[shift], "y", [(i, (i + shift) % 4) for i in range(4)])
    moved = jnp.concatenate(parts, axis=2)
    sums = jnp.sum(got[:, :, :768].astype(F32), axis=0)
    rows = got[:, :, 768:]
    rows_wide = rows.astype(F32)
    squares = jnp.sum(rows_wide * rows_wide, axis=(0, 2))
    sums = sums * lax.rsqrt(squares / width + EPSILON)[:, None]

    links = ancestry(parents)
    depth = jnp.sum((links > 0.5).astype(jnp.int32), axis=-1) - 1
    target = lengths[:, None] + depth
    first = y * 96 + z * 6
    my_places = lax.dynamic_slice(target.reshape(-1), (first,), (6,))
    inverse = ROPE_BASE ** (-jnp.arange(64, dtype=F32) / 64)
    angles = my_places.astype(F32)[:, None] * inverse[None, :]
    cosine, sine = jnp.cos(angles)[:, None, :], jnp.sin(angles)[:, None, :]
    query = rotate(head_norm(sums[:, :256].reshape(6, 2, 128), q_gain), cosine, sine) * 128 ** (-0.5)
    new_key = rotate(head_norm(sums[:, 256:384].reshape(6, 1, 128), key_gain), cosine, sine)
    outgate = jax.nn.sigmoid(sums[:, 512:]).astype(BF)
    block = jnp.concatenate(
        [
            query[:, 0], query[:, 1], new_key[:, 0], sums[:, 384:512],
            side[:, 99:105].T.astype(F32), jnp.zeros((2, 128), F32),
        ],
        axis=0,
    ).astype(BF)
    block, moved = lax.optimization_barrier((block, moved))
    gathered = spread(block, "z", 16)
    gain_all = gathered[:, 24:30].astype(F32)
    ln2_mine = gain_all[:, 0] + gain_all[:, 1] + gain_all[:, 2]
    ln2_mine = lax.dynamic_slice(ln2_mine, (0, y * 32), (16, 32)).reshape(1, 512)
    last_all = gain_all[:, 3] + gain_all[:, 4] + gain_all[:, 5]
    last_all = jnp.swapaxes(last_all.reshape(4, 4, 4, 32), 1, 2).reshape(16, 128)
    spot96 = jnp.arange(96, dtype=jnp.int32)
    origin = jnp.arange(4, dtype=jnp.int32)[:, None] * 6 + (spot96 // 6 * 24 + spot96 % 6)[None, :]
    gather = (origin.reshape(384, 1) == jnp.arange(384, dtype=jnp.int32)[None, :]).astype(BF)
    tokens = jnp.dot(gather, gathered[:, :24].reshape(384, 128), preferred_element_type=F32).astype(BF)
    queries = tokens[:192].reshape(2, 2, tree, 128)
    tree_keys = tokens[192:288].reshape(2, tree, 128)
    tree_values = tokens[288:].reshape(2, tree, 128)

    keys, values = moved[0], moved[1]
    my_lengths = lax.dynamic_slice(lengths, (2 * y,), (2,))
    my_links = lax.dynamic_slice(links, (2 * y, 0, 0), (2, tree, tree))
    source = (y - jnp.arange(4, dtype=jnp.int32)) % 4 + z * 4
    row_slots = (source[:, None] * slot_count + jnp.arange(slot_count, dtype=jnp.int32)).reshape(-1)
    valid_slot = (row_slots[None, :] < my_lengths[:, None])[:, None, None, :]
    valid_node = ((my_links > 0.5) & (z == 0))[:, None, :, :]
    scores = jnp.einsum("grid,rcd->rgic", queries, keys, preferred_element_type=F32)
    tree_scores = jnp.einsum("grid,rjd->rgij", queries, tree_keys, preferred_element_type=F32)
    peak = jnp.maximum(
        jnp.max(jnp.where(valid_slot, scores, NEGATIVE), axis=-1),
        jnp.max(jnp.where(valid_node, tree_scores, NEGATIVE), axis=-1),
    )
    peak = lax.reduce_precision(peak, 8, 7)
    weights = jnp.where(valid_slot, jnp.exp(scores - peak[..., None]), 0.0)
    tree_weights = jnp.where(valid_node, jnp.exp(tree_scores - peak[..., None]), 0.0)
    mass = jnp.sum(weights, axis=-1) + jnp.sum(tree_weights, axis=-1)
    weighted = jnp.einsum(
        "rgic,rcd->rgid", weights.astype(BF), values, preferred_element_type=F32
    ) + jnp.einsum("rgij,rjd->rgid", tree_weights.astype(BF), tree_values, preferred_element_type=F32)

    def by_z(values):
        rest = values.shape[3:]
        return jnp.swapaxes(values.reshape((2, 2, 8, 6) + rest), 1, 2).reshape((16, 2, 6) + rest)

    outgoing = pack_state(by_z(peak), by_z(mass), by_z(weighted))
    arrived, ffn = lax.optimization_barrier((swap(outgoing, "z"), ffn))
    mass, weighted = merge_state(arrived)
    my_gate = jnp.swapaxes(outgate.reshape(6, 2, 128), 0, 1).astype(F32)
    gated = (weighted / mass[..., None] * my_gate).astype(BF).reshape(12, 128)
    residual = jnp.transpose(rows.reshape(4, 4, 6, 4, 32), (3, 0, 2, 1, 4)).reshape(4, 24, 128)
    same = jnp.concatenate([gated, tokens[192:]], axis=0)
    both = swap(jnp.concatenate([residual, jnp.broadcast_to(same[None], (4, 204, 128))], axis=1), "y")
    hidden_rows = jnp.swapaxes(both[:, :24].reshape(4, 4, 6, 128), 1, 2).reshape(24, 512)
    gated = jnp.swapaxes(both[:, 24:36].reshape(4, 2, 6, 128), 0, 1).reshape(2, 24, 128)
    tree_keys = both[:, 36:132].reshape(requests, tree, 128)
    tree_values = both[:, 132:].reshape(requests, tree, 128)

    slot_ids = seq * slot_count + jnp.arange(slot_count, dtype=jnp.int32)
    accepted_rows = links[jnp.arange(requests), accepted]
    placed = (slot_ids[None, :, None] == target[:, None, :]).astype(F32) * accepted_rows[:, None, :]
    hits = (jnp.sum(placed, axis=2) > 0.5)[:, :, None]
    placed = placed.astype(BF)
    moved_keys = jnp.einsum("rca,rae->rce", placed, tree_keys, preferred_element_type=F32).astype(BF)
    moved_values = jnp.einsum("rca,rae->rce", placed, tree_values, preferred_element_type=F32).astype(BF)
    updated_keys = jnp.where(hits, moved_keys, key_cache)
    updated_values = jnp.where(hits, moved_values, value_cache)

    contract = (((1,), (1,)), ((), ()))
    attn = lax.dot_general(
        jnp.concatenate([gated[0], gated[1]], axis=1),
        ffn[:, 2304:],
        contract,
        preferred_element_type=F32,
    )
    attn, updated_keys, updated_values = lax.optimization_barrier(
        (spread(attn.astype(BF), ("x", "c"), 8), updated_keys, updated_values)
    )
    attn = jnp.sum(attn.astype(F32), axis=0)
    middle = (hidden_rows.astype(F32) + attn).astype(BF)
    middle_wide = middle.astype(F32)
    squares_mid = split2(jnp.sum(middle_wide * middle_wide, axis=1, keepdims=True))
    units = jnp.dot(
        (middle_wide * ln2_mine).astype(BF), ffn[:, :1536], preferred_element_type=F32
    ).astype(BF)
    squares_mid = jnp.pad(jnp.concatenate(squares_mid, axis=1), ((0, 0), (0, 126)))
    units = spread(jnp.concatenate([units, squares_mid], axis=1), "y", 4)
    units = jnp.sum(units.astype(F32), axis=0)
    scale_mid = lax.rsqrt((units[:, 1536:1537] + units[:, 1537:1538]) / width + EPSILON)
    act = (jax.nn.silu(units[:, :768] * scale_mid) * (units[:, 768:1536] * scale_mid)).astype(BF)
    down = lax.dot_general(act, ffn[:, 1536:2304], contract, preferred_element_type=F32)
    down = jnp.transpose(down.astype(BF).reshape(2, 12, 4, 128), (2, 0, 1, 3)).reshape(8, 12, 128)
    down = jnp.sum(swap(down, ("x", "c")).astype(F32), axis=0)
    middle_mine = lax.dynamic_slice(middle, (c * 12, x * 128), (12, 128))
    following = (middle_mine.astype(F32) + down).astype(BF)

    half = spread(following, "z", 16).reshape(16, 2, 6, 128)
    half = jnp.swapaxes(half, 0, 1).reshape(192, 128)
    half = spread(half, ("y", "x"), 16)
    other = lax.ppermute(half, "c", [(0, 1), (1, 0)])
    core = c.reshape(1)
    own_logits, own_spot = head(core, inv_temp, half, last_all, head_weight, False)
    other_logits, other_spot = head(core, inv_temp, other, last_all, head_weight, True)

    def in_order(mine_part, other_part):
        return jnp.concatenate(
            [jnp.where(c == 0, mine_part, other_part), jnp.where(c == 0, other_part, mine_part)], axis=0
        )

    def own_columns(tiles):
        return lax.dynamic_slice(tiles, (y * 4 + z // 4, 0, 0), (1, 192, 128)).reshape(192, 128)

    own = in_order(own_columns(half), own_columns(other))
    next_hidden = lax.dynamic_slice(own, (0, z % 4 * 32), (384, 32))
    spot = in_order(own_spot, other_spot).reshape(1, 512)
    for axis, count in ((("y", "x", "c"), 32), ("z", 16)):
        spots = spread(spot, axis, count)
        top = jnp.max(spots, axis=0)
        spot = top + jnp.log(jnp.sum(jnp.exp(spots - top), axis=0))
    spot = spot.reshape(2, 256)[:, :192].reshape(384, 1)
    logprobs = in_order(own_logits, other_logits) - spot

    return logprobs, next_hidden, updated_keys, updated_values


def solution(mesh):
    grid = Mesh(mesh.devices.reshape(16, 4, 4, 2), ("z", "y", "x", "c"))
    seq, tp = ("z", "y"), ("x", "c")
    in_specs = (
        P(None, seq), P(seq), P(seq, tp), P(seq, tp), P(seq, tp), P(seq, tp), P(), P(),
        P(tp, seq), P(seq), P(seq, tp), P(seq, tp), P(tp, seq), P(seq),
        P(None, seq + tp), P(), P(None, seq, tp), P(None, seq, tp), P(), P(), P(),
    )
    out_specs = (P(None, seq + tp), P(None, seq), P(None, seq, tp), P(None, seq, tp))
    return jax.shard_map(on_device, mesh=grid, in_specs=in_specs, out_specs=out_specs, check_vma=False)
```

```python
import jax
import jax.numpy as jnp
from jax import lax
from jax.experimental import pallas as pl
from jax.experimental.pallas import tpu as pltpu
from jax.sharding import Mesh, PartitionSpec as P

EPSILON = 1e-06
ROPE_BASE = 1000000.0
NEGATIVE = -1e30
BF = jnp.bfloat16
F32 = jnp.float32


def ancestry(parents):
    node_count = parents.shape[-1]
    node_ids = jnp.arange(node_count, dtype=jnp.int32)
    reachable = (parents[..., :, None] == node_ids[None, :]).astype(BF)
    reachable = jnp.maximum(reachable, jnp.eye(node_count, dtype=BF))
    for turn in range((node_count - 1).bit_length()):
        reachable = jnp.minimum(
            jnp.einsum("rij,rjk->rik", reachable, reachable, preferred_element_type=F32), 1.0
        ).astype(BF)
    return reachable.astype(F32)


def head_norm(values, gain):
    meansq = jnp.mean(values * values, axis=-1, keepdims=True)
    return values * lax.rsqrt(meansq + EPSILON) * gain


def rotate(values, cosine, sine):
    half = values.shape[-1] // 2
    low, high = values[..., :half], values[..., half:]
    return jnp.concatenate([low * cosine - high * sine, high * cosine + low * sine], axis=-1)


def swap(values, axis):
    return lax.all_to_all(values, axis, 0, 0, tiled=True)


def spread(values, axis, count):
    return swap(jnp.broadcast_to(values[None], (count,) + values.shape), axis)


def split2(values):
    high = lax.reduce_precision(values, 8, 7)
    return high.astype(BF), (values - high).astype(BF)


def pack_kernel(hidden_ref, ln1_ref, ln2_ref, last_ref, wq_ref, wk_ref, wv_ref, wg_ref, out_ref):
    lane = lax.broadcasted_iota(jnp.int32, (1, 512), 1)
    first = lane // 128
    local = lane - first * 128
    token = jnp.where(local < 96, first * 96 + local, -1)
    chosen = lax.broadcasted_iota(jnp.int32, (384, 512), 0) == token
    moved = jnp.dot(
        hidden_ref[...], jnp.where(chosen, 1.0, 0.0).astype(BF), preferred_element_type=F32
    )
    diagonal = lax.broadcasted_iota(jnp.int32, (32, 32), 0) == lax.broadcasted_iota(jnp.int32, (32, 32), 1)
    lane = lax.broadcasted_iota(jnp.int32, (32, 128), 1)
    extra = jnp.zeros((32, 128), F32)
    for which, gain_ref in enumerate((ln1_ref, ln2_ref, last_ref)):
        rest = jnp.sum(jnp.where(diagonal, gain_ref[...], 0.0), axis=1, keepdims=True)
        for digit in range(3):
            part = rest.astype(BF).astype(F32)
            extra = jnp.where(lane == 96 + which * 3 + digit, part, extra)
            rest = rest - part
    for y in range(4):
        out_ref[y, :, 0:256] = wq_ref[...]
        out_ref[y, :, 256:384] = wk_ref[...]
        out_ref[y, :, 384:512] = wv_ref[...]
        out_ref[y, :, 512:768] = wg_ref[...]
        out_ref[y, :, 768:896] = (moved[:, y * 128 : y * 128 + 128] + extra).astype(BF)


def head_kernel(core_ref, temp_ref, tiles_ref, gain_ref, weight_ref, logits_ref, spot_ref, *, flip, width):
    rows = tiles_ref.shape[1]
    squares = jnp.zeros((rows, 128), F32)
    for column in range(16):
        tile = tiles_ref[column % 4 * 4 + column // 4].astype(F32)
        squares = squares + tile * tile
    scale = lax.rsqrt(jnp.sum(squares, axis=1, keepdims=True) / width + EPSILON)
    total = jnp.zeros((rows, 256), F32)
    for pair in range(8):
        sides, rights = [], []
        for column in (2 * pair, 2 * pair + 1):
            for quarter in range(4):
                start = (column // 4 * 4 + quarter) * 128 + column % 4 * 32
                rights.append(weight_ref[start : start + 32, :])
            tile = tiles_ref[column % 4 * 4 + column // 4].astype(F32)
            sides.append((tile * scale * gain_ref[column : column + 1, :]).astype(BF))
        total = total + jnp.dot(
            jnp.concatenate(sides, axis=1),
            jnp.concatenate(rights, axis=0),
            preferred_element_type=F32,
        )
    part = core_ref[0] if not flip else 1 - core_ref[0]
    row = lax.broadcasted_iota(jnp.int32, (rows, 1), 0)
    temps = jnp.zeros((rows, 1), F32)
    for request in range(4):
        here = (row >= request * 48) & (row < request * 48 + 48)
        temps = jnp.where(here, temp_ref[part * 4 + request], temps)
    logits = total * temps
    logits_ref[...] = logits
    top = jnp.max(logits, axis=1, keepdims=True)
    spot = top + jnp.log(jnp.sum(jnp.exp(logits - top), axis=1, keepdims=True))
    across = lax.broadcasted_iota(jnp.int32, (rows, 256), 0) == lax.broadcasted_iota(jnp.int32, (rows, 256), 1)
    spot_ref[...] = jnp.sum(jnp.where(across, spot, 0.0), axis=0, keepdims=True)


def head(core, temps, tiles, gains, weight, flip):
    rows = tiles.shape[1]
    vmem, smem = pl.BlockSpec(memory_space=pltpu.VMEM), pl.BlockSpec(memory_space=pltpu.SMEM)
    return pl.pallas_call(
        lambda *refs: head_kernel(*refs, flip=flip, width=2048),
        out_shape=(
            jax.ShapeDtypeStruct((rows, 256), F32),
            jax.ShapeDtypeStruct((1, 256), F32),
        ),
        in_specs=[smem, smem, vmem, vmem, vmem],
        out_specs=(vmem, vmem),
        cost_estimate=pl.CostEstimate(
            flops=2 * rows * 2048 * 256, bytes_accessed=2 * 2048 * (rows + 256), transcendentals=rows * 256
        ),
        name="head_flip" if flip else "head_own",
    )(core, temps, tiles, gains, weight)


def pack_state(peak, mass, weighted):
    count = peak.shape[0]
    mass_high, mass_low = split2(mass)
    stats = jnp.stack([peak.astype(BF), mass_high, mass_low], axis=1).reshape(count, 6, 6)
    stats = jnp.pad(stats, ((0, 0), (0, 0), (0, 122)))
    return jnp.concatenate([weighted.astype(BF).reshape(count, 12, 128), stats], axis=1)


def merge_state(packed):
    count = packed.shape[0]
    weighted = packed[:, :12].reshape(count, 2, 6, 128).astype(F32)
    stats = packed[:, 12:, :6].astype(F32).reshape(count, 3, 2, 6)
    peaks, masses = stats[:, 0], stats[:, 1] + stats[:, 2]
    factor = jnp.exp(peaks - jnp.max(peaks, axis=0))
    return jnp.sum(masses * factor, axis=0), jnp.sum(weighted * factor[..., None], axis=0)


def on_device(
    hidden, ln1_gain, wq, wk, wv, wg, q_gain, key_gain, wo, ln2_gain, w_gate, w_up, w_down,
    last_gain, head_weight, inv_temp, key_cache, value_cache, lengths, parents, accepted,
):
    z, y, x, c = (lax.axis_index(name) for name in ("z", "y", "x", "c"))
    seq = z * 4 + y
    requests, tree = parents.shape
    slot_count = key_cache.shape[1]
    width = 2048


    ffn = jnp.concatenate([w_gate, w_up, w_down.T, wo.T], axis=1)
    ffn = lax.all_gather(ffn, "z", axis=0, tiled=True)
    vmem = pl.BlockSpec(memory_space=pltpu.VMEM)
    pieces = pl.pallas_call(
        pack_kernel,
        out_shape=jax.ShapeDtypeStruct((4, 32, 896), BF),
        in_specs=[vmem] * 8,
        out_specs=vmem,
        name="pack",
    )(hidden.T, *(gain.reshape(1, 32) for gain in (ln1_gain, ln2_gain, last_gain)), wq, wk, wv, wg)
    mine = swap(pieces, "y").reshape(128, 896)
    proj, side = mine[:, :768], mine[:, 768:]
    side_wide = side.astype(F32)
    ln1_row = side_wide[:, 96:97] + side_wide[:, 97:98] + side_wide[:, 98:99]
    scaled = (side_wide * ln1_row).astype(BF)
    partial = lax.dot_general(scaled, proj, (((0,), (0,)), ((), ())), preferred_element_type=F32)
    sent = jnp.concatenate([partial[:96].astype(BF), side.T[:96]], axis=1).reshape(16, 6, 896)
    caches = jnp.stack([key_cache, value_cache])
    parts = [
        lax.dynamic_slice(caches, (0, (y + shift) % 4 * 2, 0, 0), (2, 2, slot_count, 128))
        for shift in range(4)
    ]
    sent, parts = lax.optimization_barrier((sent, parts))
    got = swap(sent, "z")
    for shift in range(1, 4):
        parts[shift] = lax.ppermute(parts[shift], "y", [(i, (i + shift) % 4) for i in range(4)])
    sums = jnp.sum(got[:, :, :768].astype(F32), axis=0)
    rows = got[:, :, 768:]
    rows_wide = rows.astype(F32)
    squares = jnp.sum(rows_wide * rows_wide, axis=(0, 2))
    sums = sums * lax.rsqrt(squares / width + EPSILON)[:, None]

    links = ancestry(parents)
    depth = jnp.sum((links > 0.5).astype(jnp.int32), axis=-1) - 1
    target = lengths[:, None] + depth
    first = y * 96 + z * 6
    my_places = lax.dynamic_slice(target.reshape(-1), (first,), (6,))
    inverse = ROPE_BASE ** (-jnp.arange(64, dtype=F32) / 64)
    angles = my_places.astype(F32)[:, None] * inverse[None, :]
    cosine, sine = jnp.cos(angles)[:, None, :], jnp.sin(angles)[:, None, :]
    query = rotate(head_norm(sums[:, :256].reshape(6, 2, 128), q_gain), cosine, sine) * 128 ** (-0.5)
    new_key = rotate(head_norm(sums[:, 256:384].reshape(6, 1, 128), key_gain), cosine, sine)
    outgate = jax.nn.sigmoid(sums[:, 512:]).astype(BF)
    block = jnp.concatenate(
        [
            query[:, 0], query[:, 1], new_key[:, 0], sums[:, 384:512],
            side[:, 99:105].T.astype(F32), jnp.zeros((2, 128), F32),
        ],
        axis=0,
    ).astype(BF)
    block, parts[1], parts[3] = lax.optimization_barrier((block, parts[1], parts[3]))
    gathered, moved = lax.optimization_barrier((spread(block, "z", 16), jnp.concatenate(parts, axis=2)))
    gain_all = gathered[:, 24:30].astype(F32)
    ln2_mine = gain_all[:, 0] + gain_all[:, 1] + gain_all[:, 2]
    ln2_mine = lax.dynamic_slice(ln2_mine, (0, y * 32), (16, 32)).reshape(1, 512)
    last_all = gain_all[:, 3] + gain_all[:, 4] + gain_all[:, 5]
    last_all = jnp.swapaxes(last_all.reshape(4, 4, 4, 32), 1, 2).reshape(16, 128)
    spot96 = jnp.arange(96, dtype=jnp.int32)
    origin = jnp.arange(4, dtype=jnp.int32)[:, None] * 6 + (spot96 // 6 * 24 + spot96 % 6)[None, :]
    gather = (origin.reshape(384, 1) == jnp.arange(384, dtype=jnp.int32)[None, :]).astype(BF)
    tokens = jnp.dot(gather, gathered[:, :24].reshape(384, 128), preferred_element_type=F32).astype(BF)
    queries = tokens[:192].reshape(2, 2, tree, 128)
    tree_keys = tokens[192:288].reshape(2, tree, 128)
    tree_values = tokens[288:].reshape(2, tree, 128)

    keys, values = moved[0], moved[1]
    my_lengths = lax.dynamic_slice(lengths, (2 * y,), (2,))
    my_links = lax.dynamic_slice(links, (2 * y, 0, 0), (2, tree, tree))
    source = (y - jnp.arange(4, dtype=jnp.int32)) % 4 + z * 4
    row_slots = (source[:, None] * slot_count + jnp.arange(slot_count, dtype=jnp.int32)).reshape(-1)
    valid_slot = (row_slots[None, :] < my_lengths[:, None])[:, None, None, :]
    valid_node = ((my_links > 0.5) & (z == 0))[:, None, :, :]
    scores = jnp.einsum("grid,rcd->rgic", queries, keys, preferred_element_type=F32)
    tree_scores = jnp.einsum("grid,rjd->rgij", queries, tree_keys, preferred_element_type=F32)
    peak = jnp.maximum(
        jnp.max(jnp.where(valid_slot, scores, NEGATIVE), axis=-1),
        jnp.max(jnp.where(valid_node, tree_scores, NEGATIVE), axis=-1),
    )
    peak = lax.reduce_precision(peak, 8, 7)
    weights = jnp.where(valid_slot, jnp.exp(scores - peak[..., None]), 0.0)
    tree_weights = jnp.where(valid_node, jnp.exp(tree_scores - peak[..., None]), 0.0)
    mass = jnp.sum(weights, axis=-1) + jnp.sum(tree_weights, axis=-1)
    weighted = jnp.einsum(
        "rgic,rcd->rgid", weights.astype(BF), values, preferred_element_type=F32
    ) + jnp.einsum("rgij,rjd->rgid", tree_weights.astype(BF), tree_values, preferred_element_type=F32)

    def by_z(values):
        rest = values.shape[3:]
        return jnp.swapaxes(values.reshape((2, 2, 8, 6) + rest), 1, 2).reshape((16, 2, 6) + rest)

    outgoing = pack_state(by_z(peak), by_z(mass), by_z(weighted))
    mass, weighted = merge_state(swap(outgoing, "z"))
    my_gate = jnp.swapaxes(outgate.reshape(6, 2, 128), 0, 1).astype(F32)
    gated = (weighted / mass[..., None] * my_gate).astype(BF).reshape(12, 128)
    residual = jnp.transpose(rows.reshape(4, 4, 6, 4, 32), (3, 0, 2, 1, 4)).reshape(4, 24, 128)
    same = jnp.concatenate([gated, tokens[192:]], axis=0)
    both = swap(jnp.concatenate([residual, jnp.broadcast_to(same[None], (4, 204, 128))], axis=1), "y")
    hidden_rows = jnp.swapaxes(both[:, :24].reshape(4, 4, 6, 128), 1, 2).reshape(24, 512)
    gated = jnp.swapaxes(both[:, 24:36].reshape(4, 2, 6, 128), 0, 1).reshape(2, 24, 128)

    contract = (((1,), (1,)), ((), ()))
    attn = lax.dot_general(
        jnp.concatenate([gated[0], gated[1]], axis=1),
        ffn[:, 2304:],
        contract,
        preferred_element_type=F32,
    )
    attn, fresh = lax.optimization_barrier((attn.astype(BF), both[:, 36:]))
    tree_keys = fresh[:, :96].reshape(requests, tree, 128)
    tree_values = fresh[:, 96:].reshape(requests, tree, 128)

    slot_ids = seq * slot_count + jnp.arange(slot_count, dtype=jnp.int32)
    accepted_rows = links[jnp.arange(requests), accepted]
    placed = (slot_ids[None, :, None] == target[:, None, :]).astype(F32) * accepted_rows[:, None, :]
    hits = (jnp.sum(placed, axis=2) > 0.5)[:, :, None]
    placed = placed.astype(BF)
    moved_keys = jnp.einsum("rca,rae->rce", placed, tree_keys, preferred_element_type=F32).astype(BF)
    moved_values = jnp.einsum("rca,rae->rce", placed, tree_values, preferred_element_type=F32).astype(BF)
    updated_keys = jnp.where(hits, moved_keys, key_cache)
    updated_values = jnp.where(hits, moved_values, value_cache)

    attn, updated_keys, updated_values = lax.optimization_barrier(
        (spread(attn, ("x", "c"), 8), updated_keys, updated_values)
    )
    attn = jnp.sum(attn.astype(F32), axis=0)
    middle = (hidden_rows.astype(F32) + attn).astype(BF)
    middle_wide = middle.astype(F32)
    squares_mid = split2(jnp.sum(middle_wide * middle_wide, axis=1, keepdims=True))
    units = jnp.dot(
        (middle_wide * ln2_mine).astype(BF), ffn[:, :1536], preferred_element_type=F32
    ).astype(BF)
    squares_mid = jnp.pad(jnp.concatenate(squares_mid, axis=1), ((0, 0), (0, 126)))
    units = spread(jnp.concatenate([units, squares_mid], axis=1), "y", 4)
    units = jnp.sum(units.astype(F32), axis=0)
    scale_mid = lax.rsqrt((units[:, 1536:1537] + units[:, 1537:1538]) / width + EPSILON)
    act = (jax.nn.silu(units[:, :768] * scale_mid) * (units[:, 768:1536] * scale_mid)).astype(BF)
    down = lax.dot_general(act, ffn[:, 1536:2304], contract, preferred_element_type=F32)
    down = jnp.transpose(down.astype(BF).reshape(2, 12, 4, 128), (2, 0, 1, 3)).reshape(8, 12, 128)
    down = jnp.sum(swap(down, ("x", "c")).astype(F32), axis=0)
    middle_mine = lax.dynamic_slice(middle, (c * 12, x * 128), (12, 128))
    following = (middle_mine.astype(F32) + down).astype(BF)

    half = spread(following, "z", 16).reshape(16, 2, 6, 128)
    half = jnp.swapaxes(half, 0, 1).reshape(192, 128)
    half = spread(half, ("y", "x"), 16)
    other = lax.ppermute(half, "c", [(0, 1), (1, 0)])
    core = c.reshape(1)
    own_logits, own_spot = head(core, inv_temp, half, last_all, head_weight, False)
    other_logits, other_spot = head(core, inv_temp, other, last_all, head_weight, True)

    def in_order(mine_part, other_part):
        return jnp.concatenate(
            [jnp.where(c == 0, mine_part, other_part), jnp.where(c == 0, other_part, mine_part)], axis=0
        )

    def own_columns(tiles):
        return lax.dynamic_slice(tiles, (y * 4 + z // 4, 0, 0), (1, 192, 128)).reshape(192, 128)

    own = in_order(own_columns(half), own_columns(other))
    next_hidden = lax.dynamic_slice(own, (0, z % 4 * 32), (384, 32))
    spot = in_order(own_spot, other_spot).reshape(1, 512)
    for axis, count in ((("y", "x", "c"), 32), ("z", 16)):
        spots = spread(spot, axis, count)
        top = jnp.max(spots, axis=0)
        spot = top + jnp.log(jnp.sum(jnp.exp(spots - top), axis=0))
    spot = spot.reshape(2, 256)[:, :192].reshape(384, 1)
    logprobs = in_order(own_logits, other_logits) - spot

    return logprobs, next_hidden, updated_keys, updated_values


def solution(mesh):
    grid = Mesh(mesh.devices.reshape(16, 4, 4, 2), ("z", "y", "x", "c"))
    seq, tp = ("z", "y"), ("x", "c")
    in_specs = (
        P(None, seq), P(seq), P(seq, tp), P(seq, tp), P(seq, tp), P(seq, tp), P(), P(),
        P(tp, seq), P(seq), P(seq, tp), P(seq, tp), P(tp, seq), P(seq),
        P(None, seq + tp), P(), P(None, seq, tp), P(None, seq, tp), P(), P(), P(),
    )
    out_specs = (P(None, seq + tp), P(None, seq), P(None, seq, tp), P(None, seq, tp))
    return jax.shard_map(on_device, mesh=grid, in_specs=in_specs, out_specs=out_specs, check_vma=False)
```

```python
import jax
import jax.numpy as jnp
from jax import lax
from jax.experimental import pallas as pl
from jax.experimental.pallas import tpu as pltpu
from jax.sharding import Mesh, PartitionSpec as P

EPSILON = 1e-06
ROPE_BASE = 1000000.0
NEGATIVE = -1e30
BF = jnp.bfloat16
F32 = jnp.float32


def ancestry(parents):
    node_count = parents.shape[-1]
    node_ids = jnp.arange(node_count, dtype=jnp.int32)
    reachable = (parents[..., :, None] == node_ids[None, :]).astype(BF)
    reachable = jnp.maximum(reachable, jnp.eye(node_count, dtype=BF))
    for turn in range((node_count - 1).bit_length()):
        reachable = jnp.minimum(
            jnp.einsum("rij,rjk->rik", reachable, reachable, preferred_element_type=F32), 1.0
        ).astype(BF)
    return reachable.astype(F32)


def head_norm(values, gain):
    meansq = jnp.mean(values * values, axis=-1, keepdims=True)
    return values * lax.rsqrt(meansq + EPSILON) * gain


def rotate(values, cosine, sine):
    half = values.shape[-1] // 2
    low, high = values[..., :half], values[..., half:]
    return jnp.concatenate([low * cosine - high * sine, high * cosine + low * sine], axis=-1)


def swap(values, axis):
    return lax.all_to_all(values, axis, 0, 0, tiled=True)


def spread(values, axis, count):
    return swap(jnp.broadcast_to(values[None], (count,) + values.shape), axis)


def split2(values):
    high = lax.reduce_precision(values, 8, 7)
    return high.astype(BF), (values - high).astype(BF)


def pack_kernel(hidden_ref, ln1_ref, ln2_ref, last_ref, wq_ref, wk_ref, wv_ref, wg_ref, out_ref):
    lane = lax.broadcasted_iota(jnp.int32, (1, 512), 1)
    first = lane // 128
    local = lane - first * 128
    token = jnp.where(local < 96, first * 96 + local, -1)
    chosen = lax.broadcasted_iota(jnp.int32, (384, 512), 0) == token
    moved = jnp.dot(
        hidden_ref[...], jnp.where(chosen, 1.0, 0.0).astype(BF), preferred_element_type=F32
    )
    diagonal = lax.broadcasted_iota(jnp.int32, (32, 32), 0) == lax.broadcasted_iota(jnp.int32, (32, 32), 1)
    lane = lax.broadcasted_iota(jnp.int32, (32, 128), 1)
    extra = jnp.zeros((32, 128), F32)
    for which, gain_ref in enumerate((ln1_ref, ln2_ref, last_ref)):
        rest = jnp.sum(jnp.where(diagonal, gain_ref[...], 0.0), axis=1, keepdims=True)
        for digit in range(3):
            part = rest.astype(BF).astype(F32)
            extra = jnp.where(lane == 96 + which * 3 + digit, part, extra)
            rest = rest - part
    for y in range(4):
        out_ref[y, :, 0:256] = wq_ref[...]
        out_ref[y, :, 256:384] = wk_ref[...]
        out_ref[y, :, 384:512] = wv_ref[...]
        out_ref[y, :, 512:768] = wg_ref[...]
        out_ref[y, :, 768:896] = (moved[:, y * 128 : y * 128 + 128] + extra).astype(BF)


def head_kernel(core_ref, temp_ref, tiles_ref, gain_ref, weight_ref, *refs, flip, width):
    logits_ref, spot_ref = refs[-2:]
    rows = tiles_ref.shape[1]
    squares = jnp.zeros((rows, 128), F32)
    for column in range(16):
        tile = tiles_ref[column % 4 * 4 + column // 4].astype(F32)
        squares = squares + tile * tile
    scale = lax.rsqrt(jnp.sum(squares, axis=1, keepdims=True) / width + EPSILON)
    total = jnp.zeros((rows, 256), F32)
    for pair in range(8):
        sides, rights = [], []
        for column in (2 * pair, 2 * pair + 1):
            for quarter in range(4):
                start = (column // 4 * 4 + quarter) * 128 + column % 4 * 32
                rights.append(weight_ref[start : start + 32, :])
            tile = tiles_ref[column % 4 * 4 + column // 4].astype(F32)
            sides.append((tile * scale * gain_ref[column : column + 1, :]).astype(BF))
        total = total + jnp.dot(
            jnp.concatenate(sides, axis=1),
            jnp.concatenate(rights, axis=0),
            preferred_element_type=F32,
        )
    part = core_ref[0] if not flip else 1 - core_ref[0]
    row = lax.broadcasted_iota(jnp.int32, (rows, 1), 0)
    temps = jnp.zeros((rows, 1), F32)
    for request in range(4):
        here = (row >= request * 48) & (row < request * 48 + 48)
        temps = jnp.where(here, temp_ref[part * 4 + request], temps)
    logits = total * temps
    logits_ref[...] = logits
    top = jnp.max(logits, axis=1, keepdims=True)
    spot = top + jnp.log(jnp.sum(jnp.exp(logits - top), axis=1, keepdims=True))
    across = lax.broadcasted_iota(jnp.int32, (rows, 256), 0) == lax.broadcasted_iota(jnp.int32, (rows, 256), 1)
    mine = jnp.sum(jnp.where(across, spot, 0.0), axis=0, keepdims=True)
    if not flip:
        spot_ref[...] = mine
    else:
        first = refs[0][...]
        low, high = jnp.where(part == 1, first, mine), jnp.where(part == 1, mine, first)
        for copy in range(spot_ref.shape[0]):
            spot_ref[copy, :, 0:256] = low
            spot_ref[copy, :, 256:512] = high


def head(core, temps, tiles, gains, weight, first=None):
    rows = tiles.shape[1]
    flip = first is not None
    vmem, smem = pl.BlockSpec(memory_space=pltpu.VMEM), pl.BlockSpec(memory_space=pltpu.SMEM)
    extra = (first,) if flip else ()
    return pl.pallas_call(
        lambda *refs: head_kernel(*refs, flip=flip, width=2048),
        out_shape=(
            jax.ShapeDtypeStruct((rows, 256), F32),
            jax.ShapeDtypeStruct((32, 1, 512) if flip else (1, 256), F32),
        ),
        in_specs=[smem, smem, vmem, vmem, vmem] + [vmem] * len(extra),
        out_specs=(vmem, vmem),
        cost_estimate=pl.CostEstimate(
            flops=2 * rows * 2048 * 256, bytes_accessed=2 * 2048 * (rows + 256), transcendentals=rows * 256
        ),
        name="head_flip" if flip else "head_own",
    )(core, temps, tiles, gains, weight, *extra)


def pack_state(peak, mass, weighted):
    count = peak.shape[0]
    mass_high, mass_low = split2(mass)
    stats = jnp.stack([peak.astype(BF), mass_high, mass_low], axis=1).reshape(count, 6, 6)
    stats = jnp.pad(stats, ((0, 0), (0, 0), (0, 122)))
    return jnp.concatenate([weighted.astype(BF).reshape(count, 12, 128), stats], axis=1)


def merge_state(packed):
    count = packed.shape[0]
    weighted = packed[:, :12].reshape(count, 2, 6, 128).astype(F32)
    stats = packed[:, 12:, :6].astype(F32).reshape(count, 3, 2, 6)
    peaks, masses = stats[:, 0], stats[:, 1] + stats[:, 2]
    factor = jnp.exp(peaks - jnp.max(peaks, axis=0))
    return jnp.sum(masses * factor, axis=0), jnp.sum(weighted * factor[..., None], axis=0)


def on_device(
    hidden, ln1_gain, wq, wk, wv, wg, q_gain, key_gain, wo, ln2_gain, w_gate, w_up, w_down,
    last_gain, head_weight, inv_temp, key_cache, value_cache, lengths, parents, accepted,
):
    z, y, x, c = (lax.axis_index(name) for name in ("z", "y", "x", "c"))
    seq = z * 4 + y
    requests, tree = parents.shape
    slot_count = key_cache.shape[1]
    width = 2048


    ffn = jnp.concatenate([w_gate, w_up, w_down.T, wo.T], axis=1)
    ffn = lax.all_gather(ffn, "z", axis=0, tiled=True)
    vmem = pl.BlockSpec(memory_space=pltpu.VMEM)
    pieces = pl.pallas_call(
        pack_kernel,
        out_shape=jax.ShapeDtypeStruct((4, 32, 896), BF),
        in_specs=[vmem] * 8,
        out_specs=vmem,
        name="pack",
    )(hidden.T, *(gain.reshape(1, 32) for gain in (ln1_gain, ln2_gain, last_gain)), wq, wk, wv, wg)
    mine = swap(pieces, "y").reshape(128, 896)
    proj, side = mine[:, :768], mine[:, 768:]
    side_wide = side.astype(F32)
    ln1_row = side_wide[:, 96:97] + side_wide[:, 97:98] + side_wide[:, 98:99]
    scaled = (side_wide * ln1_row).astype(BF)
    partial = lax.dot_general(scaled, proj, (((0,), (0,)), ((), ())), preferred_element_type=F32)
    partial = partial[:96].astype(BF)

    def by_tile(values):
        split = values.reshape(16, 6, values.shape[1] // 128, 128)
        return jnp.swapaxes(split, 1, 2).reshape(16, -1, 128)

    sent = by_tile(jnp.concatenate([partial[:, :512], side.T[:96]], axis=1))
    caches = jnp.stack([key_cache, value_cache])
    parts = [
        lax.dynamic_slice(caches, (0, (y + shift) % 4 * 2, 0, 0), (2, 2, slot_count, 128))
        for shift in range(4)
    ]
    sent, parts = lax.optimization_barrier((sent, parts))
    got = swap(sent, "z")
    for shift in range(1, 4):
        parts[shift] = lax.ppermute(parts[shift], "y", [(i, (i + shift) % 4) for i in range(4)])
    sums = jnp.sum(got[:, :24].astype(F32), axis=0).reshape(4, 6, 128)
    rows = got[:, 24:]
    rows_wide = rows.astype(F32)
    squares = jnp.sum(rows_wide * rows_wide, axis=(0, 2))
    scale1 = lax.rsqrt(squares / width + EPSILON)[:, None]
    sums = sums * scale1

    links = ancestry(parents)
    depth = jnp.sum((links > 0.5).astype(jnp.int32), axis=-1) - 1
    target = lengths[:, None] + depth
    first = y * 96 + z * 6
    my_places = lax.dynamic_slice(target.reshape(-1), (first,), (6,))
    inverse = ROPE_BASE ** (-jnp.arange(64, dtype=F32) / 64)
    angles = my_places.astype(F32)[:, None] * inverse[None, :]
    cosine, sine = jnp.cos(angles), jnp.sin(angles)
    query = rotate(head_norm(sums[:2], q_gain), cosine, sine) * 128 ** (-0.5)
    new_key = rotate(head_norm(sums[2], key_gain), cosine, sine)
    block = jnp.concatenate(
        [
            query.reshape(12, 128), new_key, sums[3],
            side[:, 99:105].T.astype(F32), jnp.zeros((2, 128), F32),
        ],
        axis=0,
    ).astype(BF)
    block, parts[1], parts[3] = lax.optimization_barrier((block, parts[1], parts[3]))
    gathered, moved = lax.optimization_barrier((spread(block, "z", 16), jnp.concatenate(parts, axis=2)))
    gain_all = gathered[:, 24:30].astype(F32)
    ln2_mine = gain_all[:, 0] + gain_all[:, 1] + gain_all[:, 2]
    ln2_mine = lax.dynamic_slice(ln2_mine, (0, y * 32), (16, 32)).reshape(1, 512)
    last_all = gain_all[:, 3] + gain_all[:, 4] + gain_all[:, 5]
    last_all = jnp.swapaxes(last_all.reshape(4, 4, 4, 32), 1, 2).reshape(16, 128)
    spot96 = jnp.arange(96, dtype=jnp.int32)
    origin = jnp.arange(4, dtype=jnp.int32)[:, None] * 6 + (spot96 // 6 * 24 + spot96 % 6)[None, :]
    gather = (origin.reshape(384, 1) == jnp.arange(384, dtype=jnp.int32)[None, :]).astype(BF)
    tokens = jnp.dot(gather, gathered[:, :24].reshape(384, 128), preferred_element_type=F32).astype(BF)
    queries = tokens[:192].reshape(2, 2, tree, 128)
    tree_keys = tokens[192:288].reshape(2, tree, 128)
    tree_values = tokens[288:].reshape(2, tree, 128)

    keys, values = moved[0], moved[1]
    my_lengths = lax.dynamic_slice(lengths, (2 * y,), (2,))
    my_links = lax.dynamic_slice(links, (2 * y, 0, 0), (2, tree, tree))
    source = (y - jnp.arange(4, dtype=jnp.int32)) % 4 + z * 4
    row_slots = (source[:, None] * slot_count + jnp.arange(slot_count, dtype=jnp.int32)).reshape(-1)
    valid_slot = (row_slots[None, :] < my_lengths[:, None])[:, None, None, :]
    valid_node = ((my_links > 0.5) & (z == 0))[:, None, :, :]
    scores = jnp.einsum("grid,rcd->rgic", queries, keys, preferred_element_type=F32)
    tree_scores = jnp.einsum("grid,rjd->rgij", queries, tree_keys, preferred_element_type=F32)
    peak = jnp.maximum(
        jnp.max(jnp.where(valid_slot, scores, NEGATIVE), axis=-1),
        jnp.max(jnp.where(valid_node, tree_scores, NEGATIVE), axis=-1),
    )
    peak = lax.reduce_precision(peak, 8, 7)
    weights = jnp.where(valid_slot, jnp.exp(scores - peak[..., None]), 0.0)
    tree_weights = jnp.where(valid_node, jnp.exp(tree_scores - peak[..., None]), 0.0)
    mass = jnp.sum(weights, axis=-1) + jnp.sum(tree_weights, axis=-1)
    weighted = jnp.einsum(
        "rgic,rcd->rgid", weights.astype(BF), values, preferred_element_type=F32
    ) + jnp.einsum("rgij,rjd->rgid", tree_weights.astype(BF), tree_values, preferred_element_type=F32)

    def by_z(values):
        rest = values.shape[3:]
        return jnp.swapaxes(values.reshape((2, 2, 8, 6) + rest), 1, 2).reshape((16, 2, 6) + rest)

    outgoing = pack_state(by_z(peak), by_z(mass), by_z(weighted))
    outgoing = jnp.concatenate([outgoing, by_tile(partial[:, 512:])], axis=1)
    arrived, last_all = lax.optimization_barrier((swap(outgoing, "z"), last_all))
    mass, weighted = merge_state(arrived[:, :18])
    gate = jnp.sum(arrived[:, 18:].astype(F32), axis=0).reshape(2, 6, 128)
    gated = weighted / mass[..., None] * jax.nn.sigmoid(gate * scale1)
    gated = gated.astype(BF).reshape(12, 128)
    residual = jnp.transpose(rows.reshape(4, 4, 6, 4, 32), (3, 0, 2, 1, 4)).reshape(4, 24, 128)
    same = jnp.concatenate([gated, tokens[192:]], axis=0)
    both = swap(jnp.concatenate([residual, jnp.broadcast_to(same[None], (4, 204, 128))], axis=1), "y")
    hidden_rows = jnp.swapaxes(both[:, :24].reshape(4, 4, 6, 128), 1, 2).reshape(24, 512)
    gated = jnp.swapaxes(both[:, 24:36].reshape(4, 2, 6, 128), 0, 1).reshape(2, 24, 128)

    contract = (((1,), (1,)), ((), ()))
    attn = lax.dot_general(
        jnp.concatenate([gated[0], gated[1]], axis=1),
        ffn[:, 2304:],
        contract,
        preferred_element_type=F32,
    )
    attn, fresh = lax.optimization_barrier((attn.astype(BF), both[:, 36:]))
    tree_keys = fresh[:, :96].reshape(requests, tree, 128)
    tree_values = fresh[:, 96:].reshape(requests, tree, 128)

    slot_ids = seq * slot_count + jnp.arange(slot_count, dtype=jnp.int32)
    accepted_rows = links[jnp.arange(requests), accepted]
    placed = (slot_ids[None, :, None] == target[:, None, :]).astype(F32) * accepted_rows[:, None, :]
    hits = (jnp.sum(placed, axis=2) > 0.5)[:, :, None]
    placed = placed.astype(BF)
    moved_keys = jnp.einsum("rca,rae->rce", placed, tree_keys, preferred_element_type=F32).astype(BF)
    moved_values = jnp.einsum("rca,rae->rce", placed, tree_values, preferred_element_type=F32).astype(BF)
    updated_keys = jnp.where(hits, moved_keys, key_cache)
    updated_values = jnp.where(hits, moved_values, value_cache)

    attn, updated_keys, updated_values = lax.optimization_barrier(
        (spread(attn, ("x", "c"), 8), updated_keys, updated_values)
    )
    attn = jnp.sum(attn.astype(F32), axis=0)
    middle = (hidden_rows.astype(F32) + attn).astype(BF)
    middle_wide = middle.astype(F32)
    squares_mid = split2(jnp.sum(middle_wide * middle_wide, axis=1, keepdims=True))
    units = jnp.dot(
        (middle_wide * ln2_mine).astype(BF), ffn[:, :1536], preferred_element_type=F32
    ).astype(BF)
    squares_mid = jnp.pad(jnp.concatenate(squares_mid, axis=1), ((0, 0), (0, 126)))
    units = spread(jnp.concatenate([units, squares_mid], axis=1), "y", 4)
    units = jnp.sum(units.astype(F32), axis=0)
    scale_mid = lax.rsqrt((units[:, 1536:1537] + units[:, 1537:1538]) / width + EPSILON)
    act = (jax.nn.silu(units[:, :768] * scale_mid) * (units[:, 768:1536] * scale_mid)).astype(BF)
    down = lax.dot_general(act, ffn[:, 1536:2304], contract, preferred_element_type=F32)
    down = jnp.transpose(down.astype(BF).reshape(2, 12, 4, 128), (2, 0, 1, 3)).reshape(8, 12, 128)
    down = jnp.sum(swap(down, ("x", "c")).astype(F32), axis=0)
    middle_mine = lax.dynamic_slice(middle, (c * 12, x * 128), (12, 128))
    following = (middle_mine.astype(F32) + down).astype(BF)

    half = spread(following, "z", 16).reshape(16, 2, 6, 128)
    half = jnp.swapaxes(half, 0, 1).reshape(192, 128)
    half = spread(half, ("y", "x"), 16)
    other = lax.ppermute(half, "c", [(0, 1), (1, 0)])
    core = c.reshape(1)
    own_logits, own_spot = head(core, inv_temp, half, last_all, head_weight)
    other_logits, spots = head(core, inv_temp, other, last_all, head_weight, own_spot)

    def in_order(mine_part, other_part):
        return jnp.concatenate(
            [jnp.where(c == 0, mine_part, other_part), jnp.where(c == 0, other_part, mine_part)], axis=0
        )

    def own_columns(tiles):
        return lax.dynamic_slice(tiles, (y * 4 + z // 4, 0, 0), (1, 192, 128)).reshape(192, 128)

    own = in_order(own_columns(half), own_columns(other))
    next_hidden = lax.dynamic_slice(own, (0, z % 4 * 32), (384, 32))
    spots = swap(spots, ("y", "x", "c"))
    top = jnp.max(spots, axis=0)
    spot = top + jnp.log(jnp.sum(jnp.exp(spots - top), axis=0))
    spots = spread(spot, "z", 16)
    top = jnp.max(spots, axis=0)
    spot = top + jnp.log(jnp.sum(jnp.exp(spots - top), axis=0))
    spot = spot.reshape(2, 256)[:, :192].reshape(384, 1)
    logprobs = in_order(own_logits, other_logits) - spot

    return logprobs, next_hidden, updated_keys, updated_values


def solution(mesh):
    grid = Mesh(mesh.devices.reshape(16, 4, 4, 2), ("z", "y", "x", "c"))
    seq, tp = ("z", "y"), ("x", "c")
    in_specs = (
        P(None, seq), P(seq), P(seq, tp), P(seq, tp), P(seq, tp), P(seq, tp), P(), P(),
        P(tp, seq), P(seq), P(seq, tp), P(seq, tp), P(tp, seq), P(seq),
        P(None, seq + tp), P(), P(None, seq, tp), P(None, seq, tp), P(), P(), P(),
    )
    out_specs = (P(None, seq + tp), P(None, seq), P(None, seq, tp), P(None, seq, tp))
    return jax.shard_map(on_device, mesh=grid, in_specs=in_specs, out_specs=out_specs, check_vma=False)
```

```python
import jax
import jax.numpy as jnp
from jax import lax
from jax.experimental import pallas as pl
from jax.experimental.pallas import tpu as pltpu
from jax.sharding import Mesh, PartitionSpec as P

EPSILON = 1e-06
ROPE_BASE = 1000000.0
NEGATIVE = -1e30
BF = jnp.bfloat16
F32 = jnp.float32


def ancestry(parents):
    node_count = parents.shape[-1]
    node_ids = jnp.arange(node_count, dtype=jnp.int32)
    reachable = (parents[..., :, None] == node_ids[None, :]).astype(BF)
    reachable = jnp.maximum(reachable, jnp.eye(node_count, dtype=BF))
    for turn in range((node_count - 1).bit_length()):
        reachable = jnp.minimum(
            jnp.einsum("rij,rjk->rik", reachable, reachable, preferred_element_type=F32), 1.0
        ).astype(BF)
    return reachable.astype(F32)


def head_norm(values, gain):
    meansq = jnp.mean(values * values, axis=-1, keepdims=True)
    return values * lax.rsqrt(meansq + EPSILON) * gain


def rotate(values, cosine, sine):
    half = values.shape[-1] // 2
    low, high = values[..., :half], values[..., half:]
    return jnp.concatenate([low * cosine - high * sine, high * cosine + low * sine], axis=-1)


def swap(values, axis):
    return lax.all_to_all(values, axis, 0, 0, tiled=True)


def spread(values, axis, count):
    return swap(jnp.broadcast_to(values[None], (count,) + values.shape), axis)


def split2(values):
    high = lax.reduce_precision(values, 8, 7)
    return high.astype(BF), (values - high).astype(BF)


def pack_kernel(hidden_ref, ln1_ref, ln2_ref, last_ref, wq_ref, wk_ref, wv_ref, wg_ref, out_ref):
    lane = lax.broadcasted_iota(jnp.int32, (1, 512), 1)
    first = lane // 128
    local = lane - first * 128
    token = jnp.where(local < 96, first * 96 + local, -1)
    chosen = lax.broadcasted_iota(jnp.int32, (384, 512), 0) == token
    moved = jnp.dot(
        hidden_ref[...], jnp.where(chosen, 1.0, 0.0).astype(BF), preferred_element_type=F32
    )
    diagonal = lax.broadcasted_iota(jnp.int32, (32, 32), 0) == lax.broadcasted_iota(jnp.int32, (32, 32), 1)
    lane = lax.broadcasted_iota(jnp.int32, (32, 128), 1)
    extra = jnp.zeros((32, 128), F32)
    for which, gain_ref in enumerate((ln1_ref, ln2_ref, last_ref)):
        rest = jnp.sum(jnp.where(diagonal, gain_ref[...], 0.0), axis=1, keepdims=True)
        for digit in range(3):
            part = rest.astype(BF).astype(F32)
            extra = jnp.where(lane == 96 + which * 3 + digit, part, extra)
            rest = rest - part
    for y in range(4):
        out_ref[y, :, 0:256] = wq_ref[...]
        out_ref[y, :, 256:384] = wk_ref[...]
        out_ref[y, :, 384:512] = wv_ref[...]
        out_ref[y, :, 512:768] = wg_ref[...]
        out_ref[y, :, 768:896] = (moved[:, y * 128 : y * 128 + 128] + extra).astype(BF)


def head_kernel(core_ref, temp_ref, tiles_ref, gain_ref, weight_ref, *refs, flip, width):
    logits_ref, spot_ref = refs[-2:]
    rows = tiles_ref.shape[1]
    squares = jnp.zeros((rows, 128), F32)
    for column in range(16):
        tile = tiles_ref[column % 4 * 4 + column // 4].astype(F32)
        squares = squares + tile * tile
    scale = lax.rsqrt(jnp.sum(squares, axis=1, keepdims=True) / width + EPSILON)
    total = jnp.zeros((rows, 256), F32)
    for pair in range(8):
        sides, rights = [], []
        for column in (2 * pair, 2 * pair + 1):
            for quarter in range(4):
                start = (column // 4 * 4 + quarter) * 128 + column % 4 * 32
                rights.append(weight_ref[start : start + 32, :])
            tile = tiles_ref[column % 4 * 4 + column // 4].astype(F32)
            sides.append((tile * scale * gain_ref[column : column + 1, :]).astype(BF))
        total = total + jnp.dot(
            jnp.concatenate(sides, axis=1),
            jnp.concatenate(rights, axis=0),
            preferred_element_type=F32,
        )
    part = core_ref[0] if not flip else 1 - core_ref[0]
    row = lax.broadcasted_iota(jnp.int32, (rows, 1), 0)
    temps = jnp.zeros((rows, 1), F32)
    for request in range(4):
        here = (row >= request * 48) & (row < request * 48 + 48)
        temps = jnp.where(here, temp_ref[part * 4 + request], temps)
    logits = total * temps
    logits_ref[...] = logits
    top = jnp.max(logits, axis=1, keepdims=True)
    spot = top + jnp.log(jnp.sum(jnp.exp(logits - top), axis=1, keepdims=True))
    across = lax.broadcasted_iota(jnp.int32, (rows, 256), 0) == lax.broadcasted_iota(jnp.int32, (rows, 256), 1)
    mine = jnp.sum(jnp.where(across, spot, 0.0), axis=0, keepdims=True)
    if not flip:
        spot_ref[...] = mine
    else:
        first = refs[0][...]
        low, high = jnp.where(part == 1, first, mine), jnp.where(part == 1, mine, first)
        for copy in range(spot_ref.shape[0]):
            spot_ref[copy, :, 0:256] = low
            spot_ref[copy, :, 256:512] = high


def head(core, temps, tiles, gains, weight, first=None):
    rows = tiles.shape[1]
    flip = first is not None
    vmem, smem = pl.BlockSpec(memory_space=pltpu.VMEM), pl.BlockSpec(memory_space=pltpu.SMEM)
    extra = (first,) if flip else ()
    return pl.pallas_call(
        lambda *refs: head_kernel(*refs, flip=flip, width=2048),
        out_shape=(
            jax.ShapeDtypeStruct((rows, 256), F32),
            jax.ShapeDtypeStruct((32, 1, 512) if flip else (1, 256), F32),
        ),
        in_specs=[smem, smem, vmem, vmem, vmem] + [vmem] * len(extra),
        out_specs=(vmem, vmem),
        cost_estimate=pl.CostEstimate(
            flops=2 * rows * 2048 * 256, bytes_accessed=2 * 2048 * (rows + 256), transcendentals=rows * 256
        ),
        name="head_flip" if flip else "head_own",
    )(core, temps, tiles, gains, weight, *extra)


def pack_state(peak, mass, weighted):
    count = peak.shape[0]
    mass_high, mass_low = split2(mass)
    stats = jnp.stack([peak.astype(BF), mass_high, mass_low], axis=1).reshape(count, 6, 6)
    stats = jnp.pad(stats, ((0, 0), (0, 0), (0, 122)))
    return jnp.concatenate([weighted.astype(BF).reshape(count, 12, 128), stats], axis=1)


def merge_state(packed):
    count = packed.shape[0]
    weighted = packed[:, :12].reshape(count, 2, 6, 128).astype(F32)
    stats = packed[:, 12:, :6].astype(F32).reshape(count, 3, 2, 6)
    peaks, masses = stats[:, 0], stats[:, 1] + stats[:, 2]
    factor = jnp.exp(peaks - jnp.max(peaks, axis=0))
    return jnp.sum(masses * factor, axis=0), jnp.sum(weighted * factor[..., None], axis=0)


def on_device(
    hidden, ln1_gain, wq, wk, wv, wg, q_gain, key_gain, wo, ln2_gain, w_gate, w_up, w_down,
    last_gain, head_weight, inv_temp, key_cache, value_cache, lengths, parents, accepted,
):
    z, y, x, c = (lax.axis_index(name) for name in ("z", "y", "x", "c"))
    seq = z * 4 + y
    requests, tree = parents.shape
    slot_count = key_cache.shape[1]
    width = 2048


    ffn = jnp.concatenate([w_gate, w_up, w_down.T, wo.T], axis=1)
    ffn = lax.all_gather(ffn, "z", axis=0, tiled=True)
    vmem = pl.BlockSpec(memory_space=pltpu.VMEM)
    pieces = pl.pallas_call(
        pack_kernel,
        out_shape=jax.ShapeDtypeStruct((4, 32, 896), BF),
        in_specs=[vmem] * 8,
        out_specs=vmem,
        name="pack",
    )(hidden.T, *(gain.reshape(1, 32) for gain in (ln1_gain, ln2_gain, last_gain)), wq, wk, wv, wg)
    mine = swap(pieces, "y").reshape(128, 896)
    proj, side = mine[:, :768], mine[:, 768:]
    side_wide = side.astype(F32)
    ln1_row = side_wide[:, 96:97] + side_wide[:, 97:98] + side_wide[:, 98:99]
    scaled = (side_wide * ln1_row).astype(BF)
    partial = lax.dot_general(scaled, proj, (((0,), (0,)), ((), ())), preferred_element_type=F32)
    partial = partial[:96].astype(BF)

    def by_tile(values):
        split = values.reshape(16, 6, values.shape[1] // 128, 128)
        return jnp.swapaxes(split, 1, 2).reshape(16, -1, 128)

    sent = by_tile(jnp.concatenate([partial[:, :512], side.T[:96]], axis=1))
    caches = jnp.stack([key_cache, value_cache])
    parts = [
        lax.dynamic_slice(caches, (0, (y ^ shift) * 2, 0, 0), (2, 2, slot_count, 128))
        for shift in range(4)
    ]
    sent, parts = lax.optimization_barrier((sent, parts))
    got = swap(sent, "z")
    for shift in range(1, 4):
        parts[shift] = lax.ppermute(parts[shift], "y", [(i, i ^ shift) for i in range(4)])
    sums = jnp.sum(got[:, :24].astype(F32), axis=0).reshape(4, 6, 128)
    rows = got[:, 24:]
    rows_wide = rows.astype(F32)
    squares = jnp.sum(rows_wide * rows_wide, axis=(0, 2))
    scale1 = lax.rsqrt(squares / width + EPSILON)[:, None]
    sums = sums * scale1

    links = ancestry(parents)
    depth = jnp.sum((links > 0.5).astype(jnp.int32), axis=-1) - 1
    target = lengths[:, None] + depth
    first = y * 96 + z * 6
    my_places = lax.dynamic_slice(target.reshape(-1), (first,), (6,))
    inverse = ROPE_BASE ** (-jnp.arange(64, dtype=F32) / 64)
    angles = my_places.astype(F32)[:, None] * inverse[None, :]
    cosine, sine = jnp.cos(angles), jnp.sin(angles)
    query = rotate(head_norm(sums[:2], q_gain), cosine, sine) * 128 ** (-0.5)
    new_key = rotate(head_norm(sums[2], key_gain), cosine, sine)
    block = jnp.concatenate(
        [
            query.reshape(12, 128), new_key, sums[3],
            side[:, 99:105].T.astype(F32), jnp.zeros((2, 128), F32),
        ],
        axis=0,
    ).astype(BF)
    block, parts[1], parts[3] = lax.optimization_barrier((block, parts[1], parts[3]))
    gathered, moved = lax.optimization_barrier((spread(block, "z", 16), jnp.concatenate(parts, axis=2)))
    gain_all = gathered[:, 24:30].astype(F32)
    ln2_mine = gain_all[:, 0] + gain_all[:, 1] + gain_all[:, 2]
    ln2_mine = lax.dynamic_slice(ln2_mine, (0, y * 32), (16, 32)).reshape(1, 512)
    last_all = gain_all[:, 3] + gain_all[:, 4] + gain_all[:, 5]
    last_all = jnp.swapaxes(last_all.reshape(4, 4, 4, 32), 1, 2).reshape(16, 128)
    spot96 = jnp.arange(96, dtype=jnp.int32)
    origin = jnp.arange(4, dtype=jnp.int32)[:, None] * 6 + (spot96 // 6 * 24 + spot96 % 6)[None, :]
    gather = (origin.reshape(384, 1) == jnp.arange(384, dtype=jnp.int32)[None, :]).astype(BF)
    tokens = jnp.dot(gather, gathered[:, :24].reshape(384, 128), preferred_element_type=F32).astype(BF)
    queries = tokens[:192].reshape(2, 2, tree, 128)
    tree_keys = tokens[192:288].reshape(2, tree, 128)
    tree_values = tokens[288:].reshape(2, tree, 128)

    keys, values = moved[0], moved[1]
    my_lengths = lax.dynamic_slice(lengths, (2 * y,), (2,))
    my_links = lax.dynamic_slice(links, (2 * y, 0, 0), (2, tree, tree))
    source = (y ^ jnp.arange(4, dtype=jnp.int32)) + z * 4
    row_slots = (source[:, None] * slot_count + jnp.arange(slot_count, dtype=jnp.int32)).reshape(-1)
    valid_slot = (row_slots[None, :] < my_lengths[:, None])[:, None, None, :]
    valid_node = ((my_links > 0.5) & (z == 0))[:, None, :, :]
    scores = jnp.einsum("grid,rcd->rgic", queries, keys, preferred_element_type=F32)
    tree_scores = jnp.einsum("grid,rjd->rgij", queries, tree_keys, preferred_element_type=F32)
    peak = jnp.maximum(
        jnp.max(jnp.where(valid_slot, scores, NEGATIVE), axis=-1),
        jnp.max(jnp.where(valid_node, tree_scores, NEGATIVE), axis=-1),
    )
    peak = lax.reduce_precision(peak, 8, 7)
    weights = jnp.where(valid_slot, jnp.exp(scores - peak[..., None]), 0.0)
    tree_weights = jnp.where(valid_node, jnp.exp(tree_scores - peak[..., None]), 0.0)
    mass = jnp.sum(weights, axis=-1) + jnp.sum(tree_weights, axis=-1)
    weighted = jnp.einsum(
        "rgic,rcd->rgid", weights.astype(BF), values, preferred_element_type=F32
    ) + jnp.einsum("rgij,rjd->rgid", tree_weights.astype(BF), tree_values, preferred_element_type=F32)

    def by_z(values):
        rest = values.shape[3:]
        return jnp.swapaxes(values.reshape((2, 2, 8, 6) + rest), 1, 2).reshape((16, 2, 6) + rest)

    outgoing = pack_state(by_z(peak), by_z(mass), by_z(weighted))
    outgoing = jnp.concatenate([outgoing, by_tile(partial[:, 512:])], axis=1)
    arrived, last_all = lax.optimization_barrier((swap(outgoing, "z"), last_all))
    mass, weighted = merge_state(arrived[:, :18])
    gate = jnp.sum(arrived[:, 18:].astype(F32), axis=0).reshape(2, 6, 128)
    gated = weighted / mass[..., None] * jax.nn.sigmoid(gate * scale1)
    gated = gated.astype(BF).reshape(12, 128)
    residual = jnp.transpose(rows.reshape(4, 4, 6, 4, 32), (3, 0, 2, 1, 4)).reshape(4, 24, 128)
    same = jnp.concatenate([gated, tokens[192:]], axis=0)
    both = swap(jnp.concatenate([residual, jnp.broadcast_to(same[None], (4, 204, 128))], axis=1), "y")
    hidden_rows = jnp.swapaxes(both[:, :24].reshape(4, 4, 6, 128), 1, 2).reshape(24, 512)
    gated = jnp.swapaxes(both[:, 24:36].reshape(4, 2, 6, 128), 0, 1).reshape(2, 24, 128)

    contract = (((1,), (1,)), ((), ()))
    attn = lax.dot_general(
        jnp.concatenate([gated[0], gated[1]], axis=1),
        ffn[:, 2304:],
        contract,
        preferred_element_type=F32,
    )
    attn = jnp.broadcast_to(attn.astype(BF)[None], (8, 24, 512))
    attn, fresh = lax.optimization_barrier((attn, both[:, 36:]))
    tree_keys = fresh[:, :96].reshape(requests, tree, 128)
    tree_values = fresh[:, 96:].reshape(requests, tree, 128)

    slot_ids = seq * slot_count + jnp.arange(slot_count, dtype=jnp.int32)
    accepted_rows = links[jnp.arange(requests), accepted]
    placed = (slot_ids[None, :, None] == target[:, None, :]).astype(F32) * accepted_rows[:, None, :]
    hits = (jnp.sum(placed, axis=2) > 0.5)[:, :, None]
    placed = placed.astype(BF)
    moved_keys = jnp.einsum("rca,rae->rce", placed, tree_keys, preferred_element_type=F32).astype(BF)
    moved_values = jnp.einsum("rca,rae->rce", placed, tree_values, preferred_element_type=F32).astype(BF)
    updated_keys = jnp.where(hits, moved_keys, key_cache)
    updated_values = jnp.where(hits, moved_values, value_cache)

    attn, updated_keys, updated_values = lax.optimization_barrier(
        (swap(attn, ("x", "c")), updated_keys, updated_values)
    )
    attn = jnp.sum(attn.astype(F32), axis=0)
    middle = (hidden_rows.astype(F32) + attn).astype(BF)
    middle_wide = middle.astype(F32)
    squares_mid = split2(jnp.sum(middle_wide * middle_wide, axis=1, keepdims=True))
    units = jnp.dot(
        (middle_wide * ln2_mine).astype(BF), ffn[:, :1536], preferred_element_type=F32
    ).astype(BF)
    squares_mid = jnp.pad(jnp.concatenate(squares_mid, axis=1), ((0, 0), (0, 126)))
    units = spread(jnp.concatenate([units, squares_mid], axis=1), "y", 4)
    units = jnp.sum(units.astype(F32), axis=0)
    scale_mid = lax.rsqrt((units[:, 1536:1537] + units[:, 1537:1538]) / width + EPSILON)
    act = (jax.nn.silu(units[:, :768] * scale_mid) * (units[:, 768:1536] * scale_mid)).astype(BF)
    down = lax.dot_general(act, ffn[:, 1536:2304], contract, preferred_element_type=F32)
    down = jnp.transpose(down.astype(BF).reshape(2, 12, 4, 128), (2, 0, 1, 3)).reshape(8, 12, 128)
    down = jnp.sum(swap(down, ("x", "c")).astype(F32), axis=0)
    middle_mine = lax.dynamic_slice(middle, (c * 12, x * 128), (12, 128))
    following = (middle_mine.astype(F32) + down).astype(BF)

    half = spread(following, "z", 16).reshape(16, 2, 6, 128)
    half = jnp.swapaxes(half, 0, 1).reshape(192, 128)
    half = spread(half, ("y", "x"), 16)
    other = lax.ppermute(half, "c", [(0, 1), (1, 0)])
    core = c.reshape(1)
    own_logits, own_spot = head(core, inv_temp, half, last_all, head_weight)
    other_logits, spots = head(core, inv_temp, other, last_all, head_weight, own_spot)

    def in_order(mine_part, other_part):
        return jnp.concatenate(
            [jnp.where(c == 0, mine_part, other_part), jnp.where(c == 0, other_part, mine_part)], axis=0
        )

    def own_columns(tiles):
        return lax.dynamic_slice(tiles, (y * 4 + z // 4, 0, 0), (1, 192, 128)).reshape(192, 128)

    own = in_order(own_columns(half), own_columns(other))
    next_hidden = lax.dynamic_slice(own, (0, z % 4 * 32), (384, 32))
    spots = swap(spots, ("y", "x", "c"))
    top = jnp.max(spots, axis=0)
    spot = top + jnp.log(jnp.sum(jnp.exp(spots - top), axis=0))
    spots = spread(spot, "z", 16)
    top = jnp.max(spots, axis=0)
    spot = top + jnp.log(jnp.sum(jnp.exp(spots - top), axis=0))
    spot = spot.reshape(2, 256)[:, :192].reshape(384, 1)
    logprobs = in_order(own_logits, other_logits) - spot

    return logprobs, next_hidden, updated_keys, updated_values


def solution(mesh):
    grid = Mesh(mesh.devices.reshape(16, 4, 4, 2), ("z", "y", "x", "c"))
    seq, tp = ("z", "y"), ("x", "c")
    in_specs = (
        P(None, seq), P(seq), P(seq, tp), P(seq, tp), P(seq, tp), P(seq, tp), P(), P(),
        P(tp, seq), P(seq), P(seq, tp), P(seq, tp), P(tp, seq), P(seq),
        P(None, seq + tp), P(), P(None, seq, tp), P(None, seq, tp), P(), P(), P(),
    )
    out_specs = (P(None, seq + tp), P(None, seq), P(None, seq, tp), P(None, seq, tp))
    return jax.shard_map(on_device, mesh=grid, in_specs=in_specs, out_specs=out_specs, check_vma=False)
```

```python
import jax
import jax.numpy as jnp
from jax import lax
from jax.experimental import pallas as pl
from jax.experimental.pallas import tpu as pltpu
from jax.sharding import Mesh, PartitionSpec as P

EPSILON = 1e-06
ROPE_BASE = 1000000.0
NEGATIVE = -1e30
BF = jnp.bfloat16
F32 = jnp.float32


def ancestry(parents):
    node_count = parents.shape[-1]
    node_ids = jnp.arange(node_count, dtype=jnp.int32)
    reachable = (parents[..., :, None] == node_ids[None, :]).astype(BF)
    reachable = jnp.maximum(reachable, jnp.eye(node_count, dtype=BF))
    for turn in range((node_count - 1).bit_length()):
        reachable = jnp.minimum(
            jnp.einsum("rij,rjk->rik", reachable, reachable, preferred_element_type=F32), 1.0
        ).astype(BF)
    return reachable.astype(F32)


def head_norm(values, gain):
    meansq = jnp.mean(values * values, axis=-1, keepdims=True)
    return values * lax.rsqrt(meansq + EPSILON) * gain


def rotate(values, cosine, sine):
    half = values.shape[-1] // 2
    low, high = values[..., :half], values[..., half:]
    return jnp.concatenate([low * cosine - high * sine, high * cosine + low * sine], axis=-1)


def swap(values, axis):
    return lax.all_to_all(values, axis, 0, 0, tiled=True)


def spread(values, axis, count):
    return swap(jnp.broadcast_to(values[None], (count,) + values.shape), axis)


def split2(values):
    high = lax.reduce_precision(values, 8, 7)
    return high.astype(BF), (values - high).astype(BF)


def pack_kernel(hidden_ref, ln1_ref, ln2_ref, last_ref, wq_ref, wk_ref, wv_ref, wg_ref, out_ref):
    lane = lax.broadcasted_iota(jnp.int32, (1, 512), 1)
    first = lane // 128
    local = lane - first * 128
    token = jnp.where(local < 96, first * 96 + local, -1)
    chosen = lax.broadcasted_iota(jnp.int32, (384, 512), 0) == token
    moved = jnp.dot(
        hidden_ref[...], jnp.where(chosen, 1.0, 0.0).astype(BF), preferred_element_type=F32
    )
    diagonal = lax.broadcasted_iota(jnp.int32, (32, 32), 0) == lax.broadcasted_iota(jnp.int32, (32, 32), 1)
    lane = lax.broadcasted_iota(jnp.int32, (32, 128), 1)
    extra = jnp.zeros((32, 128), F32)
    for which, gain_ref in enumerate((ln1_ref, ln2_ref, last_ref)):
        rest = jnp.sum(jnp.where(diagonal, gain_ref[...], 0.0), axis=1, keepdims=True)
        for digit in range(3):
            part = rest.astype(BF).astype(F32)
            extra = jnp.where(lane == 96 + which * 3 + digit, part, extra)
            rest = rest - part
    for y in range(4):
        out_ref[y, :, 0:256] = wq_ref[...]
        out_ref[y, :, 256:384] = wk_ref[...]
        out_ref[y, :, 384:512] = wv_ref[...]
        out_ref[y, :, 512:768] = wg_ref[...]
        out_ref[y, :, 768:896] = (moved[:, y * 128 : y * 128 + 128] + extra).astype(BF)


def head_kernel(core_ref, temp_ref, tiles_ref, gain_ref, weight_ref, *refs, flip, width):
    logits_ref, spot_ref = refs[-2:]
    rows = tiles_ref.shape[1]
    squares = jnp.zeros((rows, 128), F32)
    for column in range(16):
        tile = tiles_ref[column % 4 * 4 + column // 4].astype(F32)
        squares = squares + tile * tile
    scale = lax.rsqrt(jnp.sum(squares, axis=1, keepdims=True) / width + EPSILON)
    total = jnp.zeros((rows, 256), F32)
    for pair in range(8):
        sides, rights = [], []
        for column in (2 * pair, 2 * pair + 1):
            for quarter in range(4):
                start = (column // 4 * 4 + quarter) * 128 + column % 4 * 32
                rights.append(weight_ref[start : start + 32, :])
            tile = tiles_ref[column % 4 * 4 + column // 4].astype(F32)
            sides.append((tile * scale * gain_ref[column : column + 1, :]).astype(BF))
        total = total + jnp.dot(
            jnp.concatenate(sides, axis=1),
            jnp.concatenate(rights, axis=0),
            preferred_element_type=F32,
        )
    part = core_ref[0] if not flip else 1 - core_ref[0]
    row = lax.broadcasted_iota(jnp.int32, (rows, 1), 0)
    temps = jnp.zeros((rows, 1), F32)
    for request in range(4):
        here = (row >= request * 48) & (row < request * 48 + 48)
        temps = jnp.where(here, temp_ref[part * 4 + request], temps)
    logits = total * temps
    logits_ref[...] = logits
    top = jnp.max(logits, axis=1, keepdims=True)
    spot = top + jnp.log(jnp.sum(jnp.exp(logits - top), axis=1, keepdims=True))
    across = lax.broadcasted_iota(jnp.int32, (rows, 256), 0) == lax.broadcasted_iota(jnp.int32, (rows, 256), 1)
    mine = jnp.sum(jnp.where(across, spot, 0.0), axis=0, keepdims=True)
    if not flip:
        spot_ref[...] = mine
    else:
        first = refs[0][...]
        low, high = jnp.where(part == 1, first, mine), jnp.where(part == 1, mine, first)
        for copy in range(spot_ref.shape[0]):
            spot_ref[copy, :, 0:256] = low
            spot_ref[copy, :, 256:512] = high


def head(core, temps, tiles, gains, weight, first=None):
    rows = tiles.shape[1]
    flip = first is not None
    vmem, smem = pl.BlockSpec(memory_space=pltpu.VMEM), pl.BlockSpec(memory_space=pltpu.SMEM)
    extra = (first,) if flip else ()
    return pl.pallas_call(
        lambda *refs: head_kernel(*refs, flip=flip, width=2048),
        out_shape=(
            jax.ShapeDtypeStruct((rows, 256), F32),
            jax.ShapeDtypeStruct((32, 1, 512) if flip else (1, 256), F32),
        ),
        in_specs=[smem, smem, vmem, vmem, vmem] + [vmem] * len(extra),
        out_specs=(vmem, vmem),
        cost_estimate=pl.CostEstimate(
            flops=2 * rows * 2048 * 256, bytes_accessed=2 * 2048 * (rows + 256), transcendentals=rows * 256
        ),
        name="head_flip" if flip else "head_own",
    )(core, temps, tiles, gains, weight, *extra)


def pack_state(peak, mass, weighted):
    count = peak.shape[0]
    mass_high, mass_low = split2(mass)
    stats = jnp.stack([peak.astype(BF), mass_high, mass_low], axis=1).reshape(count, 6, 6)
    stats = jnp.pad(stats, ((0, 0), (0, 0), (0, 122)))
    return jnp.concatenate([weighted.astype(BF).reshape(count, 12, 128), stats], axis=1)


def merge_state(packed):
    count = packed.shape[0]
    weighted = packed[:, :12].reshape(count, 2, 6, 128).astype(F32)
    stats = packed[:, 12:, :6].astype(F32).reshape(count, 3, 2, 6)
    peaks, masses = stats[:, 0], stats[:, 1] + stats[:, 2]
    factor = jnp.exp(peaks - jnp.max(peaks, axis=0))
    return jnp.sum(masses * factor, axis=0), jnp.sum(weighted * factor[..., None], axis=0)


def on_device(
    hidden, ln1_gain, wq, wk, wv, wg, q_gain, key_gain, wo, ln2_gain, w_gate, w_up, w_down,
    last_gain, head_weight, inv_temp, key_cache, value_cache, lengths, parents, accepted,
):
    z, y, x, c = (lax.axis_index(name) for name in ("z", "y", "x", "c"))
    seq = z * 4 + y
    requests, tree = parents.shape
    slot_count = key_cache.shape[1]
    width = 2048


    ffn = jnp.concatenate([w_gate, w_up, w_down.T, wo.T], axis=1)
    ffn = lax.all_gather(ffn, "z", axis=0, tiled=True)
    vmem = pl.BlockSpec(memory_space=pltpu.VMEM)
    pieces = pl.pallas_call(
        pack_kernel,
        out_shape=jax.ShapeDtypeStruct((4, 32, 896), BF),
        in_specs=[vmem] * 8,
        out_specs=vmem,
        name="pack",
    )(hidden.T, *(gain.reshape(1, 32) for gain in (ln1_gain, ln2_gain, last_gain)), wq, wk, wv, wg)
    mine = swap(pieces, "y").reshape(128, 896)
    proj, side = mine[:, :768], mine[:, 768:]
    side_wide = side.astype(F32)
    ln1_row = side_wide[:, 96:97] + side_wide[:, 97:98] + side_wide[:, 98:99]
    scaled = (side_wide * ln1_row).astype(BF)
    partial = lax.dot_general(scaled, proj, (((0,), (0,)), ((), ())), preferred_element_type=F32)
    partial = partial[:96].astype(BF)

    def by_tile(values):
        split = values.reshape(16, 6, values.shape[1] // 128, 128)
        return jnp.swapaxes(split, 1, 2).reshape(16, -1, 128)

    sent = by_tile(jnp.concatenate([partial[:, :512], side.T[:96]], axis=1))
    caches = jnp.stack([key_cache, value_cache])
    parts = [
        lax.dynamic_slice(caches, (0, (y ^ shift) * 2, 0, 0), (2, 2, slot_count, 128))
        for shift in range(4)
    ]
    sent, parts = lax.optimization_barrier((sent, parts))
    got = swap(sent, "z")
    for shift in range(1, 4):
        parts[shift] = lax.ppermute(parts[shift], "y", [(i, i ^ shift) for i in range(4)])
    sums = jnp.sum(got[:, :24].astype(F32), axis=0).reshape(4, 6, 128)
    rows = got[:, 24:]
    rows_wide = rows.astype(F32)
    squares = jnp.sum(rows_wide * rows_wide, axis=(0, 2))
    scale1 = lax.rsqrt(squares / width + EPSILON)[:, None]
    sums = sums * scale1

    links = ancestry(parents)
    depth = jnp.sum((links > 0.5).astype(jnp.int32), axis=-1) - 1
    target = lengths[:, None] + depth
    first = y * 96 + z * 6
    my_places = lax.dynamic_slice(target.reshape(-1), (first,), (6,))
    inverse = ROPE_BASE ** (-jnp.arange(64, dtype=F32) / 64)
    angles = my_places.astype(F32)[:, None] * inverse[None, :]
    cosine, sine = jnp.cos(angles), jnp.sin(angles)
    query = rotate(head_norm(sums[:2], q_gain), cosine, sine) * 128 ** (-0.5)
    new_key = rotate(head_norm(sums[2], key_gain), cosine, sine)
    block = jnp.concatenate(
        [
            query.reshape(12, 128), new_key, sums[3],
            side[:, 99:105].T.astype(F32), jnp.zeros((2, 128), F32),
        ],
        axis=0,
    ).astype(BF)
    block, parts[2] = lax.optimization_barrier((block, parts[2]))
    gathered, moved = lax.optimization_barrier((spread(block, "z", 16), jnp.concatenate(parts, axis=2)))
    gain_all = gathered[:, 24:30].astype(F32)
    ln2_mine = gain_all[:, 0] + gain_all[:, 1] + gain_all[:, 2]
    ln2_mine = lax.dynamic_slice(ln2_mine, (0, y * 32), (16, 32)).reshape(1, 512)
    last_all = gain_all[:, 3] + gain_all[:, 4] + gain_all[:, 5]
    last_all = jnp.swapaxes(last_all.reshape(4, 4, 4, 32), 1, 2).reshape(16, 128)
    spot96 = jnp.arange(96, dtype=jnp.int32)
    origin = jnp.arange(4, dtype=jnp.int32)[:, None] * 6 + (spot96 // 6 * 24 + spot96 % 6)[None, :]
    gather = (origin.reshape(384, 1) == jnp.arange(384, dtype=jnp.int32)[None, :]).astype(BF)
    tokens = jnp.dot(gather, gathered[:, :24].reshape(384, 128), preferred_element_type=F32).astype(BF)
    queries = tokens[:192].reshape(2, 2, tree, 128)
    tree_keys = tokens[192:288].reshape(2, tree, 128)
    tree_values = tokens[288:].reshape(2, tree, 128)

    keys, values = moved[0], moved[1]
    my_lengths = lax.dynamic_slice(lengths, (2 * y,), (2,))
    my_links = lax.dynamic_slice(links, (2 * y, 0, 0), (2, tree, tree))
    source = (y ^ jnp.arange(4, dtype=jnp.int32)) + z * 4
    row_slots = (source[:, None] * slot_count + jnp.arange(slot_count, dtype=jnp.int32)).reshape(-1)
    valid_slot = (row_slots[None, :] < my_lengths[:, None])[:, None, None, :]
    valid_node = ((my_links > 0.5) & (z == 0))[:, None, :, :]
    scores = jnp.einsum("grid,rcd->rgic", queries, keys, preferred_element_type=F32)
    tree_scores = jnp.einsum("grid,rjd->rgij", queries, tree_keys, preferred_element_type=F32)
    peak = jnp.maximum(
        jnp.max(jnp.where(valid_slot, scores, NEGATIVE), axis=-1),
        jnp.max(jnp.where(valid_node, tree_scores, NEGATIVE), axis=-1),
    )
    peak = lax.reduce_precision(peak, 8, 7)
    weights = jnp.where(valid_slot, jnp.exp(scores - peak[..., None]), 0.0)
    tree_weights = jnp.where(valid_node, jnp.exp(tree_scores - peak[..., None]), 0.0)
    mass = jnp.sum(weights, axis=-1) + jnp.sum(tree_weights, axis=-1)
    weighted = jnp.einsum(
        "rgic,rcd->rgid", weights.astype(BF), values, preferred_element_type=F32
    ) + jnp.einsum("rgij,rjd->rgid", tree_weights.astype(BF), tree_values, preferred_element_type=F32)

    def by_z(values):
        rest = values.shape[3:]
        return jnp.swapaxes(values.reshape((2, 2, 8, 6) + rest), 1, 2).reshape((16, 2, 6) + rest)

    outgoing = pack_state(by_z(peak), by_z(mass), by_z(weighted))
    outgoing = jnp.concatenate([outgoing, by_tile(partial[:, 512:])], axis=1)
    arrived, last_all = lax.optimization_barrier((swap(outgoing, "z"), last_all))
    mass, weighted = merge_state(arrived[:, :18])
    gate = jnp.sum(arrived[:, 18:].astype(F32), axis=0).reshape(2, 6, 128)
    gated = weighted / mass[..., None] * jax.nn.sigmoid(gate * scale1)
    gated = gated.astype(BF).reshape(12, 128)
    residual = jnp.transpose(rows.reshape(4, 4, 6, 4, 32), (3, 0, 2, 1, 4)).reshape(4, 24, 128)
    same = jnp.concatenate([gated, tokens[192:]], axis=0)
    both = swap(jnp.concatenate([residual, jnp.broadcast_to(same[None], (4, 204, 128))], axis=1), "y")
    hidden_rows = jnp.swapaxes(both[:, :24].reshape(4, 4, 6, 128), 1, 2).reshape(24, 512)
    gated = jnp.swapaxes(both[:, 24:36].reshape(4, 2, 6, 128), 0, 1).reshape(2, 24, 128)

    contract = (((1,), (1,)), ((), ()))
    attn = lax.dot_general(
        jnp.concatenate([gated[0], gated[1]], axis=1),
        ffn[:, 2304:],
        contract,
        preferred_element_type=F32,
    )
    attn = jnp.broadcast_to(attn.astype(BF)[None], (8, 24, 512))
    attn, fresh = lax.optimization_barrier((attn, both[:, 36:]))
    tree_keys = fresh[:, :96].reshape(requests, tree, 128)
    tree_values = fresh[:, 96:].reshape(requests, tree, 128)

    slot_ids = seq * slot_count + jnp.arange(slot_count, dtype=jnp.int32)
    accepted_rows = links[jnp.arange(requests), accepted]
    placed = (slot_ids[None, :, None] == target[:, None, :]).astype(F32) * accepted_rows[:, None, :]
    hits = (jnp.sum(placed, axis=2) > 0.5)[:, :, None]
    placed = placed.astype(BF)
    moved_keys = jnp.einsum("rca,rae->rce", placed, tree_keys, preferred_element_type=F32).astype(BF)
    moved_values = jnp.einsum("rca,rae->rce", placed, tree_values, preferred_element_type=F32).astype(BF)
    updated_keys = jnp.where(hits, moved_keys, key_cache)
    updated_values = jnp.where(hits, moved_values, value_cache)

    attn, updated_keys, updated_values = lax.optimization_barrier(
        (swap(attn, ("x", "c")), updated_keys, updated_values)
    )
    attn = jnp.sum(attn.astype(F32), axis=0)
    middle = (hidden_rows.astype(F32) + attn).astype(BF)
    middle_wide = middle.astype(F32)
    squares_mid = split2(jnp.sum(middle_wide * middle_wide, axis=1, keepdims=True))
    units = jnp.dot(
        (middle_wide * ln2_mine).astype(BF), ffn[:, :1536], preferred_element_type=F32
    ).astype(BF)
    squares_mid = jnp.pad(jnp.concatenate(squares_mid, axis=1), ((0, 0), (0, 126)))
    units = spread(jnp.concatenate([units, squares_mid], axis=1), "y", 4)
    units = jnp.sum(units.astype(F32), axis=0)
    scale_mid = lax.rsqrt((units[:, 1536:1537] + units[:, 1537:1538]) / width + EPSILON)
    act = (jax.nn.silu(units[:, :768] * scale_mid) * (units[:, 768:1536] * scale_mid)).astype(BF)
    down = lax.dot_general(act, ffn[:, 1536:2304], contract, preferred_element_type=F32)
    down = jnp.transpose(down.astype(BF).reshape(2, 12, 4, 128), (2, 0, 1, 3)).reshape(8, 12, 128)
    down = jnp.sum(swap(down, ("x", "c")).astype(F32), axis=0)
    middle_mine = lax.dynamic_slice(middle, (c * 12, x * 128), (12, 128))
    following = (middle_mine.astype(F32) + down).astype(BF)

    half = spread(following, "z", 16).reshape(16, 2, 6, 128)
    half = jnp.swapaxes(half, 0, 1).reshape(192, 128)
    half = spread(half, ("y", "x"), 16)
    other = lax.ppermute(half, "c", [(0, 1), (1, 0)])
    core = c.reshape(1)
    own_logits, own_spot = head(core, inv_temp, half, last_all, head_weight)
    other_logits, spots = head(core, inv_temp, other, last_all, head_weight, own_spot)

    def in_order(mine_part, other_part):
        return jnp.concatenate(
            [jnp.where(c == 0, mine_part, other_part), jnp.where(c == 0, other_part, mine_part)], axis=0
        )

    def own_columns(tiles):
        return lax.dynamic_slice(tiles, (y * 4 + z // 4, 0, 0), (1, 192, 128)).reshape(192, 128)

    own = in_order(own_columns(half), own_columns(other))
    next_hidden = lax.dynamic_slice(own, (0, z % 4 * 32), (384, 32))
    spots = swap(spots, ("y", "x", "c"))
    top = jnp.max(spots, axis=0)
    spot = top + jnp.log(jnp.sum(jnp.exp(spots - top), axis=0))
    spots = spread(spot, "z", 16)
    top = jnp.max(spots, axis=0)
    spot = top + jnp.log(jnp.sum(jnp.exp(spots - top), axis=0))
    spot = spot.reshape(2, 256)[:, :192].reshape(384, 1)
    logprobs = in_order(own_logits, other_logits) - spot

    return logprobs, next_hidden, updated_keys, updated_values


def solution(mesh):
    grid = Mesh(mesh.devices.reshape(16, 4, 4, 2), ("z", "y", "x", "c"))
    seq, tp = ("z", "y"), ("x", "c")
    in_specs = (
        P(None, seq), P(seq), P(seq, tp), P(seq, tp), P(seq, tp), P(seq, tp), P(), P(),
        P(tp, seq), P(seq), P(seq, tp), P(seq, tp), P(tp, seq), P(seq),
        P(None, seq + tp), P(), P(None, seq, tp), P(None, seq, tp), P(), P(), P(),
    )
    out_specs = (P(None, seq + tp), P(None, seq), P(None, seq, tp), P(None, seq, tp))
    return jax.shard_map(on_device, mesh=grid, in_specs=in_specs, out_specs=out_specs, check_vma=False)
```

```python
import jax
import jax.numpy as jnp
from jax import lax
from jax.experimental import pallas as pl
from jax.experimental.pallas import tpu as pltpu
from jax.sharding import Mesh, PartitionSpec as P

EPSILON = 1e-06
ROPE_BASE = 1000000.0
NEGATIVE = -1e30
BF = jnp.bfloat16
F32 = jnp.float32


def ancestry(parents):
    node_count = parents.shape[-1]
    node_ids = jnp.arange(node_count, dtype=jnp.int32)
    reachable = (parents[..., :, None] == node_ids[None, :]).astype(BF)
    reachable = jnp.maximum(reachable, jnp.eye(node_count, dtype=BF))
    for turn in range((node_count - 1).bit_length()):
        reachable = jnp.minimum(
            jnp.einsum("rij,rjk->rik", reachable, reachable, preferred_element_type=F32), 1.0
        ).astype(BF)
    return reachable.astype(F32)


def head_norm(values, gain):
    meansq = jnp.mean(values * values, axis=-1, keepdims=True)
    return values * lax.rsqrt(meansq + EPSILON) * gain


def rotate(values, cosine, sine):
    half = values.shape[-1] // 2
    low, high = values[..., :half], values[..., half:]
    return jnp.concatenate([low * cosine - high * sine, high * cosine + low * sine], axis=-1)


def swap(values, axis):
    return lax.all_to_all(values, axis, 0, 0, tiled=True)


def spread(values, axis, count):
    return swap(jnp.broadcast_to(values[None], (count,) + values.shape), axis)


def split2(values):
    high = lax.reduce_precision(values, 8, 7)
    return high.astype(BF), (values - high).astype(BF)


def pack_kernel(hidden_ref, ln1_ref, ln2_ref, last_ref, wq_ref, wk_ref, wv_ref, wg_ref, out_ref):
    lane = lax.broadcasted_iota(jnp.int32, (1, 512), 1)
    first = lane // 128
    local = lane - first * 128
    token = jnp.where(local < 96, first * 96 + local, -1)
    chosen = lax.broadcasted_iota(jnp.int32, (384, 512), 0) == token
    moved = jnp.dot(
        hidden_ref[...], jnp.where(chosen, 1.0, 0.0).astype(BF), preferred_element_type=F32
    )
    diagonal = lax.broadcasted_iota(jnp.int32, (32, 32), 0) == lax.broadcasted_iota(jnp.int32, (32, 32), 1)
    lane = lax.broadcasted_iota(jnp.int32, (32, 128), 1)
    extra = jnp.zeros((32, 128), F32)
    for which, gain_ref in enumerate((ln1_ref, ln2_ref, last_ref)):
        rest = jnp.sum(jnp.where(diagonal, gain_ref[...], 0.0), axis=1, keepdims=True)
        for digit in range(3):
            part = rest.astype(BF).astype(F32)
            extra = jnp.where(lane == 96 + which * 3 + digit, part, extra)
            rest = rest - part
    for y in range(4):
        out_ref[y, :, 0:256] = wq_ref[...]
        out_ref[y, :, 256:384] = wk_ref[...]
        out_ref[y, :, 384:512] = wv_ref[...]
        out_ref[y, :, 512:768] = wg_ref[...]
        out_ref[y, :, 768:896] = (moved[:, y * 128 : y * 128 + 128] + extra).astype(BF)


def head_kernel(core_ref, temp_ref, tiles_ref, gain_ref, weight_ref, *refs, flip, width):
    logits_ref, spot_ref = refs[-2:]
    rows = tiles_ref.shape[1]
    squares = jnp.zeros((rows, 128), F32)
    for column in range(16):
        tile = tiles_ref[column % 4 * 4 + column // 4].astype(F32)
        squares = squares + tile * tile
    scale = lax.rsqrt(jnp.sum(squares, axis=1, keepdims=True) / width + EPSILON)
    total = jnp.zeros((rows, 256), F32)
    for pair in range(8):
        sides, rights = [], []
        for column in (2 * pair, 2 * pair + 1):
            for quarter in range(4):
                start = (column // 4 * 4 + quarter) * 128 + column % 4 * 32
                rights.append(weight_ref[start : start + 32, :])
            tile = tiles_ref[column % 4 * 4 + column // 4].astype(F32)
            sides.append((tile * scale * gain_ref[column : column + 1, :]).astype(BF))
        total = total + jnp.dot(
            jnp.concatenate(sides, axis=1),
            jnp.concatenate(rights, axis=0),
            preferred_element_type=F32,
        )
    part = core_ref[0] if not flip else 1 - core_ref[0]
    row = lax.broadcasted_iota(jnp.int32, (rows, 1), 0)
    temps = jnp.zeros((rows, 1), F32)
    for request in range(4):
        here = (row >= request * 48) & (row < request * 48 + 48)
        temps = jnp.where(here, temp_ref[part * 4 + request], temps)
    logits = total * temps
    logits_ref[...] = logits
    top = jnp.max(logits, axis=1, keepdims=True)
    spot = top + jnp.log(jnp.sum(jnp.exp(logits - top), axis=1, keepdims=True))
    across = lax.broadcasted_iota(jnp.int32, (rows, 256), 0) == lax.broadcasted_iota(jnp.int32, (rows, 256), 1)
    mine = jnp.sum(jnp.where(across, spot, 0.0), axis=0, keepdims=True)
    if not flip:
        spot_ref[...] = mine
    else:
        first = refs[0][...]
        low, high = jnp.where(part == 1, first, mine), jnp.where(part == 1, mine, first)
        for copy in range(spot_ref.shape[0]):
            spot_ref[copy, :, 0:256] = low
            spot_ref[copy, :, 256:512] = high


def head(core, temps, tiles, gains, weight, first=None):
    rows = tiles.shape[1]
    flip = first is not None
    vmem, smem = pl.BlockSpec(memory_space=pltpu.VMEM), pl.BlockSpec(memory_space=pltpu.SMEM)
    extra = (first,) if flip else ()
    return pl.pallas_call(
        lambda *refs: head_kernel(*refs, flip=flip, width=2048),
        out_shape=(
            jax.ShapeDtypeStruct((rows, 256), F32),
            jax.ShapeDtypeStruct((8, 1, 512) if flip else (1, 256), F32),
        ),
        in_specs=[smem, smem, vmem, vmem, vmem] + [vmem] * len(extra),
        out_specs=(vmem, vmem),
        cost_estimate=pl.CostEstimate(
            flops=2 * rows * 2048 * 256, bytes_accessed=2 * 2048 * (rows + 256), transcendentals=rows * 256
        ),
        name="head_flip" if flip else "head_own",
    )(core, temps, tiles, gains, weight, *extra)


def pack_state(peak, mass, weighted):
    count = peak.shape[0]
    mass_high, mass_low = split2(mass)
    stats = jnp.stack([peak.astype(BF), mass_high, mass_low], axis=1).reshape(count, 6, 6)
    stats = jnp.pad(stats, ((0, 0), (0, 0), (0, 122)))
    return jnp.concatenate([weighted.astype(BF).reshape(count, 12, 128), stats], axis=1)


def merge_state(packed):
    count = packed.shape[0]
    weighted = packed[:, :12].reshape(count, 2, 6, 128).astype(F32)
    stats = packed[:, 12:, :6].astype(F32).reshape(count, 3, 2, 6)
    peaks, masses = stats[:, 0], stats[:, 1] + stats[:, 2]
    factor = jnp.exp(peaks - jnp.max(peaks, axis=0))
    return jnp.sum(masses * factor, axis=0), jnp.sum(weighted * factor[..., None], axis=0)


def on_device(
    hidden, ln1_gain, wq, wk, wv, wg, q_gain, key_gain, wo, ln2_gain, w_gate, w_up, w_down,
    last_gain, head_weight, inv_temp, key_cache, value_cache, lengths, parents, accepted,
):
    z, y, x, c = (lax.axis_index(name) for name in ("z", "y", "x", "c"))
    seq = z * 4 + y
    requests, tree = parents.shape
    slot_count = key_cache.shape[1]
    width = 2048


    ffn = jnp.concatenate([w_gate, w_up, w_down.T, wo.T], axis=1)
    ffn = lax.all_gather(ffn, "z", axis=0, tiled=True)
    vmem = pl.BlockSpec(memory_space=pltpu.VMEM)
    pieces = pl.pallas_call(
        pack_kernel,
        out_shape=jax.ShapeDtypeStruct((4, 32, 896), BF),
        in_specs=[vmem] * 8,
        out_specs=vmem,
        name="pack",
    )(hidden.T, *(gain.reshape(1, 32) for gain in (ln1_gain, ln2_gain, last_gain)), wq, wk, wv, wg)
    mine = swap(pieces, "y").reshape(128, 896)
    proj, side = mine[:, :768], mine[:, 768:]
    side_wide = side.astype(F32)
    ln1_row = side_wide[:, 96:97] + side_wide[:, 97:98] + side_wide[:, 98:99]
    scaled = (side_wide * ln1_row).astype(BF)
    partial = lax.dot_general(scaled, proj, (((0,), (0,)), ((), ())), preferred_element_type=F32)
    partial = partial[:96].astype(BF)

    def by_tile(values):
        split = values.reshape(16, 6, values.shape[1] // 128, 128)
        return jnp.swapaxes(split, 1, 2).reshape(16, -1, 128)

    sent = by_tile(jnp.concatenate([partial[:, :512], side.T[:96]], axis=1))
    caches = jnp.stack([key_cache, value_cache])
    parts = [
        lax.dynamic_slice(caches, (0, (y ^ shift) * 2, 0, 0), (2, 2, slot_count, 128))
        for shift in range(4)
    ]
    sent, parts = lax.optimization_barrier((sent, parts))
    got = swap(sent, "z")
    for shift in range(1, 4):
        parts[shift] = lax.ppermute(parts[shift], "y", [(i, i ^ shift) for i in range(4)])
    sums = jnp.sum(got[:, :24].astype(F32), axis=0).reshape(4, 6, 128)
    rows = got[:, 24:]
    rows_wide = rows.astype(F32)
    squares = jnp.sum(rows_wide * rows_wide, axis=(0, 2))
    scale1 = lax.rsqrt(squares / width + EPSILON)[:, None]
    sums = sums * scale1

    links = ancestry(parents)
    depth = jnp.sum((links > 0.5).astype(jnp.int32), axis=-1) - 1
    target = lengths[:, None] + depth
    first = y * 96 + z * 6
    my_places = lax.dynamic_slice(target.reshape(-1), (first,), (6,))
    inverse = ROPE_BASE ** (-jnp.arange(64, dtype=F32) / 64)
    angles = my_places.astype(F32)[:, None] * inverse[None, :]
    cosine, sine = jnp.cos(angles), jnp.sin(angles)
    query = rotate(head_norm(sums[:2], q_gain), cosine, sine) * 128 ** (-0.5)
    new_key = rotate(head_norm(sums[2], key_gain), cosine, sine)
    block = jnp.concatenate(
        [
            query.reshape(12, 128), new_key, sums[3],
            side[:, 99:105].T.astype(F32), jnp.zeros((2, 128), F32),
        ],
        axis=0,
    ).astype(BF)
    block, parts[1], parts[3] = lax.optimization_barrier((block, parts[1], parts[3]))
    gathered, moved = lax.optimization_barrier((spread(block, "z", 16), jnp.concatenate(parts, axis=2)))
    gain_all = gathered[:, 24:30].astype(F32)
    ln2_mine = gain_all[:, 0] + gain_all[:, 1] + gain_all[:, 2]
    ln2_mine = lax.dynamic_slice(ln2_mine, (0, y * 32), (16, 32)).reshape(1, 512)
    last_all = gain_all[:, 3] + gain_all[:, 4] + gain_all[:, 5]
    last_all = jnp.swapaxes(last_all.reshape(4, 4, 4, 32), 1, 2).reshape(16, 128)
    spot96 = jnp.arange(96, dtype=jnp.int32)
    origin = jnp.arange(4, dtype=jnp.int32)[:, None] * 6 + (spot96 // 6 * 24 + spot96 % 6)[None, :]
    gather = (origin.reshape(384, 1) == jnp.arange(384, dtype=jnp.int32)[None, :]).astype(BF)
    tokens = jnp.dot(gather, gathered[:, :24].reshape(384, 128), preferred_element_type=F32).astype(BF)
    queries = tokens[:192].reshape(2, 2, tree, 128)
    tree_keys = tokens[192:288].reshape(2, tree, 128)
    tree_values = tokens[288:].reshape(2, tree, 128)

    keys, values = moved[0], moved[1]
    my_lengths = lax.dynamic_slice(lengths, (2 * y,), (2,))
    my_links = lax.dynamic_slice(links, (2 * y, 0, 0), (2, tree, tree))
    source = (y ^ jnp.arange(4, dtype=jnp.int32)) + z * 4
    row_slots = (source[:, None] * slot_count + jnp.arange(slot_count, dtype=jnp.int32)).reshape(-1)
    valid_slot = (row_slots[None, :] < my_lengths[:, None])[:, None, None, :]
    valid_node = ((my_links > 0.5) & (z == 0))[:, None, :, :]
    scores = jnp.einsum("grid,rcd->rgic", queries, keys, preferred_element_type=F32)
    tree_scores = jnp.einsum("grid,rjd->rgij", queries, tree_keys, preferred_element_type=F32)
    peak = jnp.maximum(
        jnp.max(jnp.where(valid_slot, scores, NEGATIVE), axis=-1),
        jnp.max(jnp.where(valid_node, tree_scores, NEGATIVE), axis=-1),
    )
    peak = lax.reduce_precision(peak, 8, 7)
    weights = jnp.where(valid_slot, jnp.exp(scores - peak[..., None]), 0.0)
    tree_weights = jnp.where(valid_node, jnp.exp(tree_scores - peak[..., None]), 0.0)
    mass = jnp.sum(weights, axis=-1) + jnp.sum(tree_weights, axis=-1)
    weighted = jnp.einsum(
        "rgic,rcd->rgid", weights.astype(BF), values, preferred_element_type=F32
    ) + jnp.einsum("rgij,rjd->rgid", tree_weights.astype(BF), tree_values, preferred_element_type=F32)

    def by_z(values):
        rest = values.shape[3:]
        return jnp.swapaxes(values.reshape((2, 2, 8, 6) + rest), 1, 2).reshape((16, 2, 6) + rest)

    outgoing = pack_state(by_z(peak), by_z(mass), by_z(weighted))
    outgoing = jnp.concatenate([outgoing, by_tile(partial[:, 512:])], axis=1)
    arrived, last_all = lax.optimization_barrier((swap(outgoing, "z"), last_all))
    mass, weighted = merge_state(arrived[:, :18])
    gate = jnp.sum(arrived[:, 18:].astype(F32), axis=0).reshape(2, 6, 128)
    gated = weighted / mass[..., None] * jax.nn.sigmoid(gate * scale1)
    gated = gated.astype(BF).reshape(12, 128)
    residual = jnp.transpose(rows.reshape(4, 4, 6, 4, 32), (3, 0, 2, 1, 4)).reshape(4, 24, 128)
    same = jnp.concatenate([gated, tokens[192:]], axis=0)
    both = swap(jnp.concatenate([residual, jnp.broadcast_to(same[None], (4, 204, 128))], axis=1), "y")
    both, ffn = lax.optimization_barrier((both, ffn))
    hidden_rows = jnp.swapaxes(both[:, :24].reshape(4, 4, 6, 128), 1, 2).reshape(24, 512)
    gated = jnp.swapaxes(both[:, 24:36].reshape(4, 2, 6, 128), 0, 1).reshape(2, 24, 128)

    contract = (((1,), (1,)), ((), ()))
    attn = lax.dot_general(
        jnp.concatenate([gated[0], gated[1]], axis=1),
        ffn[:, 2304:],
        contract,
        preferred_element_type=F32,
    )
    attn = jnp.broadcast_to(attn.astype(BF)[None], (8, 24, 512))
    attn, fresh = lax.optimization_barrier((attn, both[:, 36:]))
    tree_keys = fresh[:, :96].reshape(requests, tree, 128)
    tree_values = fresh[:, 96:].reshape(requests, tree, 128)

    slot_ids = seq * slot_count + jnp.arange(slot_count, dtype=jnp.int32)
    accepted_rows = links[jnp.arange(requests), accepted]
    placed = (slot_ids[None, :, None] == target[:, None, :]).astype(F32) * accepted_rows[:, None, :]
    hits = (jnp.sum(placed, axis=2) > 0.5)[:, :, None]
    placed = placed.astype(BF)
    moved_keys = jnp.einsum("rca,rae->rce", placed, tree_keys, preferred_element_type=F32).astype(BF)
    moved_values = jnp.einsum("rca,rae->rce", placed, tree_values, preferred_element_type=F32).astype(BF)
    updated_keys = jnp.where(hits, moved_keys, key_cache)
    updated_values = jnp.where(hits, moved_values, value_cache)

    attn, updated_keys, updated_values = lax.optimization_barrier(
        (swap(attn, ("x", "c")), updated_keys, updated_values)
    )
    attn = jnp.sum(attn.astype(F32), axis=0)
    middle = (hidden_rows.astype(F32) + attn).astype(BF)
    middle_wide = middle.astype(F32)
    squares_mid = split2(jnp.sum(middle_wide * middle_wide, axis=1, keepdims=True))
    units = jnp.dot(
        (middle_wide * ln2_mine).astype(BF), ffn[:, :1536], preferred_element_type=F32
    ).astype(BF)
    squares_mid = jnp.pad(jnp.concatenate(squares_mid, axis=1), ((0, 0), (0, 126)))
    units = spread(jnp.concatenate([units, squares_mid], axis=1), "y", 4)
    units = jnp.sum(units.astype(F32), axis=0)
    scale_mid = lax.rsqrt((units[:, 1536:1537] + units[:, 1537:1538]) / width + EPSILON)
    act = (jax.nn.silu(units[:, :768] * scale_mid) * (units[:, 768:1536] * scale_mid)).astype(BF)
    down = lax.dot_general(act, ffn[:, 1536:2304], contract, preferred_element_type=F32)
    down = jnp.transpose(down.astype(BF).reshape(2, 12, 4, 128), (2, 0, 1, 3)).reshape(8, 12, 128)
    down = jnp.sum(swap(down, ("x", "c")).astype(F32), axis=0)
    middle_mine = lax.dynamic_slice(middle, (c * 12, x * 128), (12, 128))
    following = (middle_mine.astype(F32) + down).astype(BF)

    half = spread(following, "z", 16).reshape(16, 2, 6, 128)
    half = jnp.swapaxes(half, 0, 1).reshape(192, 128)
    half = spread(half, ("y", "x"), 16)
    other = lax.ppermute(half, "c", [(0, 1), (1, 0)])
    core = c.reshape(1)
    own_logits, own_spot = head(core, inv_temp, half, last_all, head_weight)
    other_logits, spots = head(core, inv_temp, other, last_all, head_weight, own_spot)

    def in_order(mine_part, other_part):
        return jnp.concatenate(
            [jnp.where(c == 0, mine_part, other_part), jnp.where(c == 0, other_part, mine_part)], axis=0
        )

    def own_columns(tiles):
        return lax.dynamic_slice(tiles, (y * 4 + z // 4, 0, 0), (1, 192, 128)).reshape(192, 128)

    own = in_order(own_columns(half), own_columns(other))
    next_hidden = lax.dynamic_slice(own, (0, z % 4 * 32), (384, 32))
    spots = swap(spots, ("x", "c"))
    top = jnp.max(spots, axis=0)
    spot = top + jnp.log(jnp.sum(jnp.exp(spots - top), axis=0))
    spots = spread(spot, ("z", "y"), 64)
    top = jnp.max(spots, axis=0)
    spot = top + jnp.log(jnp.sum(jnp.exp(spots - top), axis=0))
    spot = spot.reshape(2, 256)[:, :192].reshape(384, 1)
    logprobs = in_order(own_logits, other_logits) - spot

    return logprobs, next_hidden, updated_keys, updated_values


def solution(mesh):
    grid = Mesh(mesh.devices.reshape(16, 4, 4, 2), ("z", "y", "x", "c"))
    seq, tp = ("z", "y"), ("x", "c")
    in_specs = (
        P(None, seq), P(seq), P(seq, tp), P(seq, tp), P(seq, tp), P(seq, tp), P(), P(),
        P(tp, seq), P(seq), P(seq, tp), P(seq, tp), P(tp, seq), P(seq),
        P(None, seq + tp), P(), P(None, seq, tp), P(None, seq, tp), P(), P(), P(),
    )
    out_specs = (P(None, seq + tp), P(None, seq), P(None, seq, tp), P(None, seq, tp))
    return jax.shard_map(on_device, mesh=grid, in_specs=in_specs, out_specs=out_specs, check_vma=False)
```

```python
import jax
import jax.numpy as jnp
from jax import lax
from jax.experimental import pallas as pl
from jax.experimental.pallas import tpu as pltpu
from jax.sharding import Mesh, PartitionSpec as P

EPSILON = 1e-06
ROPE_BASE = 1000000.0
NEGATIVE = -1e30
BF = jnp.bfloat16
F32 = jnp.float32


def ancestry(parents):
    node_count = parents.shape[-1]
    node_ids = jnp.arange(node_count, dtype=jnp.int32)
    reachable = (parents[..., :, None] == node_ids[None, :]).astype(BF)
    reachable = jnp.maximum(reachable, jnp.eye(node_count, dtype=BF))
    for turn in range((node_count - 1).bit_length()):
        reachable = jnp.minimum(
            jnp.einsum("rij,rjk->rik", reachable, reachable, preferred_element_type=F32), 1.0
        ).astype(BF)
    return reachable.astype(F32)


def head_norm(values, gain):
    meansq = jnp.mean(values * values, axis=-1, keepdims=True)
    return values * lax.rsqrt(meansq + EPSILON) * gain


def rotate(values, cosine, sine):
    half = values.shape[-1] // 2
    low, high = values[..., :half], values[..., half:]
    return jnp.concatenate([low * cosine - high * sine, high * cosine + low * sine], axis=-1)


def swap(values, axis):
    return lax.all_to_all(values, axis, 0, 0, tiled=True)


def spread(values, axis, count):
    return swap(jnp.broadcast_to(values[None], (count,) + values.shape), axis)


def split2(values):
    high = lax.reduce_precision(values, 8, 7)
    return high.astype(BF), (values - high).astype(BF)


def pack_kernel(
    hidden_ref, ln1_ref, ln2_ref, last_ref, wq_ref, wk_ref, wv_ref, wg_ref,
    gate_ref, up_ref, down_ref, wo_ref, out_ref, joined_ref,
):
    joined_ref[:, 0:768] = gate_ref[...]
    joined_ref[:, 768:1536] = up_ref[...]
    joined_ref[:, 1536:2304] = down_ref[...]
    joined_ref[:, 2304:2560] = wo_ref[...]
    lane = lax.broadcasted_iota(jnp.int32, (1, 512), 1)
    first = lane // 128
    local = lane - first * 128
    token = jnp.where(local < 96, first * 96 + local, -1)
    chosen = lax.broadcasted_iota(jnp.int32, (384, 512), 0) == token
    moved = jnp.dot(
        hidden_ref[...], jnp.where(chosen, 1.0, 0.0).astype(BF), preferred_element_type=F32
    )
    diagonal = lax.broadcasted_iota(jnp.int32, (32, 32), 0) == lax.broadcasted_iota(jnp.int32, (32, 32), 1)
    lane = lax.broadcasted_iota(jnp.int32, (32, 128), 1)
    extra = jnp.zeros((32, 128), F32)
    for which, gain_ref in enumerate((ln1_ref, ln2_ref, last_ref)):
        rest = jnp.sum(jnp.where(diagonal, gain_ref[...], 0.0), axis=1, keepdims=True)
        for digit in range(3):
            part = rest.astype(BF).astype(F32)
            extra = jnp.where(lane == 96 + which * 3 + digit, part, extra)
            rest = rest - part
    for y in range(4):
        out_ref[y, :, 0:256] = wq_ref[...]
        out_ref[y, :, 256:384] = wk_ref[...]
        out_ref[y, :, 384:512] = wv_ref[...]
        out_ref[y, :, 512:768] = wg_ref[...]
        out_ref[y, :, 768:896] = (moved[:, y * 128 : y * 128 + 128] + extra).astype(BF)


def head_kernel(core_ref, temp_ref, tiles_ref, gain_ref, weight_ref, *refs, flip, width):
    logits_ref, spot_ref = refs[-2:]
    rows = tiles_ref.shape[1]
    squares = jnp.zeros((rows, 128), F32)
    for column in range(16):
        tile = tiles_ref[column % 4 * 4 + column // 4].astype(F32)
        squares = squares + tile * tile
    scale = lax.rsqrt(jnp.sum(squares, axis=1, keepdims=True) / width + EPSILON)
    total = jnp.zeros((rows, 256), F32)
    for pair in range(8):
        sides, rights = [], []
        for column in (2 * pair, 2 * pair + 1):
            for quarter in range(4):
                start = (column // 4 * 4 + quarter) * 128 + column % 4 * 32
                rights.append(weight_ref[start : start + 32, :])
            tile = tiles_ref[column % 4 * 4 + column // 4].astype(F32)
            sides.append((tile * scale * gain_ref[column : column + 1, :]).astype(BF))
        total = total + jnp.dot(
            jnp.concatenate(sides, axis=1),
            jnp.concatenate(rights, axis=0),
            preferred_element_type=F32,
        )
    part = core_ref[0] if not flip else 1 - core_ref[0]
    row = lax.broadcasted_iota(jnp.int32, (rows, 1), 0)
    temps = jnp.zeros((rows, 1), F32)
    for request in range(4):
        here = (row >= request * 48) & (row < request * 48 + 48)
        temps = jnp.where(here, temp_ref[part * 4 + request], temps)
    logits = total * temps
    logits_ref[...] = logits
    top = jnp.max(logits, axis=1, keepdims=True)
    spot = top + jnp.log(jnp.sum(jnp.exp(logits - top), axis=1, keepdims=True))
    across = lax.broadcasted_iota(jnp.int32, (rows, 256), 0) == lax.broadcasted_iota(jnp.int32, (rows, 256), 1)
    mine = jnp.sum(jnp.where(across, spot, 0.0), axis=0, keepdims=True)
    if not flip:
        spot_ref[...] = mine
    else:
        first = refs[0][...]
        low, high = jnp.where(part == 1, first, mine), jnp.where(part == 1, mine, first)
        for copy in range(spot_ref.shape[0]):
            spot_ref[copy, :, 0:256] = low
            spot_ref[copy, :, 256:512] = high


def head(core, temps, tiles, gains, weight, first=None):
    rows = tiles.shape[1]
    flip = first is not None
    vmem, smem = pl.BlockSpec(memory_space=pltpu.VMEM), pl.BlockSpec(memory_space=pltpu.SMEM)
    extra = (first,) if flip else ()
    return pl.pallas_call(
        lambda *refs: head_kernel(*refs, flip=flip, width=2048),
        out_shape=(
            jax.ShapeDtypeStruct((rows, 256), F32),
            jax.ShapeDtypeStruct((32, 1, 512) if flip else (1, 256), F32),
        ),
        in_specs=[smem, smem, vmem, vmem, vmem] + [vmem] * len(extra),
        out_specs=(vmem, vmem),
        cost_estimate=pl.CostEstimate(
            flops=2 * rows * 2048 * 256, bytes_accessed=2 * 2048 * (rows + 256), transcendentals=rows * 256
        ),
        name="head_flip" if flip else "head_own",
    )(core, temps, tiles, gains, weight, *extra)


def pack_state(peak, mass, weighted):
    count = peak.shape[0]
    mass_high, mass_low = split2(mass)
    stats = jnp.stack([peak.astype(BF), mass_high, mass_low], axis=1).reshape(count, 6, 6)
    stats = jnp.pad(stats, ((0, 0), (0, 0), (0, 122)))
    return jnp.concatenate([weighted.astype(BF).reshape(count, 12, 128), stats], axis=1)


def merge_state(packed):
    count = packed.shape[0]
    weighted = packed[:, :12].reshape(count, 2, 6, 128).astype(F32)
    stats = packed[:, 12:, :6].astype(F32).reshape(count, 3, 2, 6)
    peaks, masses = stats[:, 0], stats[:, 1] + stats[:, 2]
    factor = jnp.exp(peaks - jnp.max(peaks, axis=0))
    return jnp.sum(masses * factor, axis=0), jnp.sum(weighted * factor[..., None], axis=0)


def on_device(
    hidden, ln1_gain, wq, wk, wv, wg, q_gain, key_gain, wo, ln2_gain, w_gate, w_up, w_down,
    last_gain, head_weight, inv_temp, key_cache, value_cache, lengths, parents, accepted,
):
    z, y, x, c = (lax.axis_index(name) for name in ("z", "y", "x", "c"))
    seq = z * 4 + y
    requests, tree = parents.shape
    slot_count = key_cache.shape[1]
    width = 2048


    vmem = pl.BlockSpec(memory_space=pltpu.VMEM)
    pieces, ffn = pl.pallas_call(
        pack_kernel,
        out_shape=(jax.ShapeDtypeStruct((4, 32, 896), BF), jax.ShapeDtypeStruct((32, 2560), BF)),
        in_specs=[vmem] * 12,
        out_specs=(vmem, vmem),
        name="pack",
    )(
        hidden.T, *(gain.reshape(1, 32) for gain in (ln1_gain, ln2_gain, last_gain)), wq, wk, wv, wg,
        w_gate, w_up, w_down.T, wo.T,
    )
    ffn = lax.all_gather(ffn, "z", axis=0, tiled=True)
    mine = swap(pieces, "y").reshape(128, 896)
    proj, side = mine[:, :768], mine[:, 768:]
    side_wide = side.astype(F32)
    ln1_row = side_wide[:, 96:97] + side_wide[:, 97:98] + side_wide[:, 98:99]
    scaled = (side_wide * ln1_row).astype(BF)
    partial = lax.dot_general(scaled, proj, (((0,), (0,)), ((), ())), preferred_element_type=F32)
    partial = partial[:96].astype(BF)

    def by_tile(values):
        split = values.reshape(16, 6, values.shape[1] // 128, 128)
        return jnp.swapaxes(split, 1, 2).reshape(16, -1, 128)

    sent = by_tile(jnp.concatenate([partial[:, :512], side.T[:96]], axis=1))
    caches = jnp.stack([key_cache, value_cache])
    parts = [
        lax.dynamic_slice(caches, (0, (y ^ shift) * 2, 0, 0), (2, 2, slot_count, 128))
        for shift in range(4)
    ]
    sent, parts = lax.optimization_barrier((sent, parts))
    got = swap(sent, "z")
    for shift in range(1, 4):
        parts[shift] = lax.ppermute(parts[shift], "y", [(i, i ^ shift) for i in range(4)])
    sums = jnp.sum(got[:, :24].astype(F32), axis=0).reshape(4, 6, 128)
    rows = got[:, 24:]
    rows_wide = rows.astype(F32)
    squares = jnp.sum(rows_wide * rows_wide, axis=(0, 2))
    scale1 = lax.rsqrt(squares / width + EPSILON)[:, None]
    sums = sums * scale1

    links = ancestry(parents)
    depth = jnp.sum((links > 0.5).astype(jnp.int32), axis=-1) - 1
    target = lengths[:, None] + depth
    first = y * 96 + z * 6
    my_places = lax.dynamic_slice(target.reshape(-1), (first,), (6,))
    inverse = ROPE_BASE ** (-jnp.arange(64, dtype=F32) / 64)
    angles = my_places.astype(F32)[:, None] * inverse[None, :]
    cosine, sine = jnp.cos(angles), jnp.sin(angles)
    query = rotate(head_norm(sums[:2], q_gain), cosine, sine) * 128 ** (-0.5)
    new_key = rotate(head_norm(sums[2], key_gain), cosine, sine)
    block = jnp.concatenate(
        [
            query.reshape(12, 128), new_key, sums[3],
            side[:, 99:105].T.astype(F32), jnp.zeros((2, 128), F32),
        ],
        axis=0,
    ).astype(BF)
    block, parts[1], parts[3] = lax.optimization_barrier((block, parts[1], parts[3]))
    gathered, moved = lax.optimization_barrier((spread(block, "z", 16), jnp.concatenate(parts, axis=2)))
    gain_all = gathered[:, 24:30].astype(F32)
    ln2_mine = gain_all[:, 0] + gain_all[:, 1] + gain_all[:, 2]
    ln2_mine = lax.dynamic_slice(ln2_mine, (0, y * 32), (16, 32)).reshape(1, 512)
    last_all = gain_all[:, 3] + gain_all[:, 4] + gain_all[:, 5]
    last_all = jnp.swapaxes(last_all.reshape(4, 4, 4, 32), 1, 2).reshape(16, 128)
    spot96 = jnp.arange(96, dtype=jnp.int32)
    origin = jnp.arange(4, dtype=jnp.int32)[:, None] * 6 + (spot96 // 6 * 24 + spot96 % 6)[None, :]
    gather = (origin.reshape(384, 1) == jnp.arange(384, dtype=jnp.int32)[None, :]).astype(BF)
    tokens = jnp.dot(gather, gathered[:, :24].reshape(384, 128), preferred_element_type=F32).astype(BF)
    queries = tokens[:192].reshape(2, 2, tree, 128)
    tree_keys = tokens[192:288].reshape(2, tree, 128)
    tree_values = tokens[288:].reshape(2, tree, 128)

    keys, values = moved[0], moved[1]
    my_lengths = lax.dynamic_slice(lengths, (2 * y,), (2,))
    my_links = lax.dynamic_slice(links, (2 * y, 0, 0), (2, tree, tree))
    source = (y ^ jnp.arange(4, dtype=jnp.int32)) + z * 4
    row_slots = (source[:, None] * slot_count + jnp.arange(slot_count, dtype=jnp.int32)).reshape(-1)
    valid_slot = (row_slots[None, :] < my_lengths[:, None])[:, None, None, :]
    valid_node = ((my_links > 0.5) & (z == 0))[:, None, :, :]
    scores = jnp.einsum("grid,rcd->rgic", queries, keys, preferred_element_type=F32)
    tree_scores = jnp.einsum("grid,rjd->rgij", queries, tree_keys, preferred_element_type=F32)
    peak = jnp.maximum(
        jnp.max(jnp.where(valid_slot, scores, NEGATIVE), axis=-1),
        jnp.max(jnp.where(valid_node, tree_scores, NEGATIVE), axis=-1),
    )
    peak = lax.reduce_precision(peak, 8, 7)
    weights = jnp.where(valid_slot, jnp.exp(scores - peak[..., None]), 0.0)
    tree_weights = jnp.where(valid_node, jnp.exp(tree_scores - peak[..., None]), 0.0)
    mass = jnp.sum(weights, axis=-1) + jnp.sum(tree_weights, axis=-1)
    weighted = jnp.einsum(
        "rgic,rcd->rgid", weights.astype(BF), values, preferred_element_type=F32
    ) + jnp.einsum("rgij,rjd->rgid", tree_weights.astype(BF), tree_values, preferred_element_type=F32)

    def by_z(values):
        rest = values.shape[3:]
        return jnp.swapaxes(values.reshape((2, 2, 8, 6) + rest), 1, 2).reshape((16, 2, 6) + rest)

    outgoing = pack_state(by_z(peak), by_z(mass), by_z(weighted))
    outgoing = jnp.concatenate([outgoing, by_tile(partial[:, 512:])], axis=1)
    arrived, last_all = lax.optimization_barrier((swap(outgoing, "z"), last_all))
    mass, weighted = merge_state(arrived[:, :18])
    gate = jnp.sum(arrived[:, 18:].astype(F32), axis=0).reshape(2, 6, 128)
    gated = weighted / mass[..., None] * jax.nn.sigmoid(gate * scale1)
    gated = gated.astype(BF).reshape(12, 128)
    residual = jnp.transpose(rows.reshape(4, 4, 6, 4, 32), (3, 0, 2, 1, 4)).reshape(4, 24, 128)
    same = jnp.concatenate([gated, tokens[192:]], axis=0)
    both = swap(jnp.concatenate([residual, jnp.broadcast_to(same[None], (4, 204, 128))], axis=1), "y")
    hidden_rows = jnp.swapaxes(both[:, :24].reshape(4, 4, 6, 128), 1, 2).reshape(24, 512)
    gated = jnp.swapaxes(both[:, 24:36].reshape(4, 2, 6, 128), 0, 1).reshape(2, 24, 128)

    contract = (((1,), (1,)), ((), ()))
    attn = lax.dot_general(
        jnp.concatenate([gated[0], gated[1]], axis=1),
        ffn[:, 2304:],
        contract,
        preferred_element_type=F32,
    )
    attn = jnp.broadcast_to(attn.astype(BF)[None], (8, 24, 512))
    attn, fresh = lax.optimization_barrier((attn, both[:, 36:]))
    tree_keys = fresh[:, :96].reshape(requests, tree, 128)
    tree_values = fresh[:, 96:].reshape(requests, tree, 128)

    slot_ids = seq * slot_count + jnp.arange(slot_count, dtype=jnp.int32)
    accepted_rows = links[jnp.arange(requests), accepted]
    placed = (slot_ids[None, :, None] == target[:, None, :]).astype(F32) * accepted_rows[:, None, :]
    hits = (jnp.sum(placed, axis=2) > 0.5)[:, :, None]
    placed = placed.astype(BF)
    moved_keys = jnp.einsum("rca,rae->rce", placed, tree_keys, preferred_element_type=F32).astype(BF)
    moved_values = jnp.einsum("rca,rae->rce", placed, tree_values, preferred_element_type=F32).astype(BF)
    updated_keys = jnp.where(hits, moved_keys, key_cache)
    updated_values = jnp.where(hits, moved_values, value_cache)

    attn, updated_keys, updated_values = lax.optimization_barrier(
        (swap(attn, ("x", "c")), updated_keys, updated_values)
    )
    attn = jnp.sum(attn.astype(F32), axis=0)
    middle = (hidden_rows.astype(F32) + attn).astype(BF)
    middle_wide = middle.astype(F32)
    squares_mid = split2(jnp.sum(middle_wide * middle_wide, axis=1, keepdims=True))
    units = jnp.dot(
        (middle_wide * ln2_mine).astype(BF), ffn[:, :1536], preferred_element_type=F32
    ).astype(BF)
    squares_mid = jnp.pad(jnp.concatenate(squares_mid, axis=1), ((0, 0), (0, 126)))
    units = spread(jnp.concatenate([units, squares_mid], axis=1), "y", 4)
    units = jnp.sum(units.astype(F32), axis=0)
    scale_mid = lax.rsqrt((units[:, 1536:1537] + units[:, 1537:1538]) / width + EPSILON)
    act = (jax.nn.silu(units[:, :768] * scale_mid) * (units[:, 768:1536] * scale_mid)).astype(BF)
    down = lax.dot_general(act, ffn[:, 1536:2304], contract, preferred_element_type=F32)
    down = jnp.transpose(down.astype(BF).reshape(2, 12, 4, 128), (2, 0, 1, 3)).reshape(8, 12, 128)
    down = jnp.sum(swap(down, ("x", "c")).astype(F32), axis=0)
    middle_mine = lax.dynamic_slice(middle, (c * 12, x * 128), (12, 128))
    following = (middle_mine.astype(F32) + down).astype(BF)

    half = spread(following, "z", 16).reshape(16, 2, 6, 128)
    half = jnp.swapaxes(half, 0, 1).reshape(192, 128)
    half = spread(half, ("y", "x"), 16)
    other = lax.ppermute(half, "c", [(0, 1), (1, 0)])
    core = c.reshape(1)
    own_logits, own_spot = head(core, inv_temp, half, last_all, head_weight)
    other_logits, spots = head(core, inv_temp, other, last_all, head_weight, own_spot)

    def in_order(mine_part, other_part):
        return jnp.concatenate(
            [jnp.where(c == 0, mine_part, other_part), jnp.where(c == 0, other_part, mine_part)], axis=0
        )

    def own_columns(tiles):
        return lax.dynamic_slice(tiles, (y * 4 + z // 4, 0, 0), (1, 192, 128)).reshape(192, 128)

    own = in_order(own_columns(half), own_columns(other))
    next_hidden = lax.dynamic_slice(own, (0, z % 4 * 32), (384, 32))
    spots = swap(spots, ("y", "x", "c"))
    top = jnp.max(spots, axis=0)
    spot = top + jnp.log(jnp.sum(jnp.exp(spots - top), axis=0))
    spots = spread(spot, "z", 16)
    top = jnp.max(spots, axis=0)
    spot = top + jnp.log(jnp.sum(jnp.exp(spots - top), axis=0))
    spot = spot.reshape(2, 256)[:, :192].reshape(384, 1)
    logprobs = in_order(own_logits, other_logits) - spot

    return logprobs, next_hidden, updated_keys, updated_values


def solution(mesh):
    grid = Mesh(mesh.devices.reshape(16, 4, 4, 2), ("z", "y", "x", "c"))
    seq, tp = ("z", "y"), ("x", "c")
    in_specs = (
        P(None, seq), P(seq), P(seq, tp), P(seq, tp), P(seq, tp), P(seq, tp), P(), P(),
        P(tp, seq), P(seq), P(seq, tp), P(seq, tp), P(tp, seq), P(seq),
        P(None, seq + tp), P(), P(None, seq, tp), P(None, seq, tp), P(), P(), P(),
    )
    out_specs = (P(None, seq + tp), P(None, seq), P(None, seq, tp), P(None, seq, tp))
    return jax.shard_map(on_device, mesh=grid, in_specs=in_specs, out_specs=out_specs, check_vma=False)
```

```python
import jax
import jax.numpy as jnp
from jax import lax
from jax.experimental import pallas as pl
from jax.experimental.pallas import tpu as pltpu
from jax.sharding import Mesh, PartitionSpec as P

EPSILON = 1e-06
ROPE_BASE = 1000000.0
NEGATIVE = -1e30
BF = jnp.bfloat16
F32 = jnp.float32


def ancestry(parents):
    node_count = parents.shape[-1]
    node_ids = jnp.arange(node_count, dtype=jnp.int32)
    reachable = (parents[..., :, None] == node_ids[None, :]).astype(BF)
    reachable = jnp.maximum(reachable, jnp.eye(node_count, dtype=BF))
    for turn in range((node_count - 1).bit_length()):
        reachable = jnp.minimum(
            jnp.einsum("rij,rjk->rik", reachable, reachable, preferred_element_type=F32), 1.0
        ).astype(BF)
    return reachable.astype(F32)


def head_norm(values, gain):
    meansq = jnp.mean(values * values, axis=-1, keepdims=True)
    return values * lax.rsqrt(meansq + EPSILON) * gain


def rotate(values, cosine, sine):
    half = values.shape[-1] // 2
    low, high = values[..., :half], values[..., half:]
    return jnp.concatenate([low * cosine - high * sine, high * cosine + low * sine], axis=-1)


def swap(values, axis):
    return lax.all_to_all(values, axis, 0, 0, tiled=True)


def spread(values, axis, count):
    return swap(jnp.broadcast_to(values[None], (count,) + values.shape), axis)


def split2(values):
    high = lax.reduce_precision(values, 8, 7)
    return high.astype(BF), (values - high).astype(BF)


def pack_kernel(
    hidden_ref, ln1_ref, ln2_ref, last_ref, wq_ref, wk_ref, wv_ref, wg_ref,
    gate_ref, up_ref, down_ref, wo_ref, out_ref, joined_ref,
):
    joined_ref[:, 0:768] = gate_ref[...]
    joined_ref[:, 768:1536] = up_ref[...]
    joined_ref[:, 1536:2304] = down_ref[...]
    joined_ref[:, 2304:2560] = wo_ref[...]
    lane = lax.broadcasted_iota(jnp.int32, (1, 512), 1)
    first = lane // 128
    local = lane - first * 128
    token = jnp.where(local < 96, first * 96 + local, -1)
    chosen = lax.broadcasted_iota(jnp.int32, (384, 512), 0) == token
    moved = jnp.dot(
        hidden_ref[...], jnp.where(chosen, 1.0, 0.0).astype(BF), preferred_element_type=F32
    )
    diagonal = lax.broadcasted_iota(jnp.int32, (32, 32), 0) == lax.broadcasted_iota(jnp.int32, (32, 32), 1)
    lane = lax.broadcasted_iota(jnp.int32, (32, 128), 1)
    extra = jnp.zeros((32, 128), F32)
    for which, gain_ref in enumerate((ln1_ref, ln2_ref, last_ref)):
        rest = jnp.sum(jnp.where(diagonal, gain_ref[...], 0.0), axis=1, keepdims=True)
        for digit in range(3):
            part = rest.astype(BF).astype(F32)
            extra = jnp.where(lane == 96 + which * 3 + digit, part, extra)
            rest = rest - part
    for y in range(4):
        out_ref[y, :, 0:256] = wq_ref[...]
        out_ref[y, :, 256:384] = wk_ref[...]
        out_ref[y, :, 384:512] = wv_ref[...]
        out_ref[y, :, 512:768] = wg_ref[...]
        out_ref[y, :, 768:896] = (moved[:, y * 128 : y * 128 + 128] + extra).astype(BF)


def head_kernel(core_ref, temp_ref, tiles_ref, gain_ref, weight_ref, *refs, flip, width):
    logits_ref, spot_ref = refs[-2:]
    rows = tiles_ref.shape[1]
    squares = jnp.zeros((rows, 128), F32)
    for column in range(16):
        tile = tiles_ref[column % 4 * 4 + column // 4].astype(F32)
        squares = squares + tile * tile
    scale = lax.rsqrt(jnp.sum(squares, axis=1, keepdims=True) / width + EPSILON)
    total = jnp.zeros((rows, 256), F32)
    for pair in range(8):
        sides, rights = [], []
        for column in (2 * pair, 2 * pair + 1):
            for quarter in range(4):
                start = (column // 4 * 4 + quarter) * 128 + column % 4 * 32
                rights.append(weight_ref[start : start + 32, :])
            tile = tiles_ref[column % 4 * 4 + column // 4].astype(F32)
            sides.append((tile * scale * gain_ref[column : column + 1, :]).astype(BF))
        total = total + jnp.dot(
            jnp.concatenate(sides, axis=1),
            jnp.concatenate(rights, axis=0),
            preferred_element_type=F32,
        )
    part = core_ref[0] if not flip else 1 - core_ref[0]
    row = lax.broadcasted_iota(jnp.int32, (rows, 1), 0)
    temps = jnp.zeros((rows, 1), F32)
    for request in range(4):
        here = (row >= request * 48) & (row < request * 48 + 48)
        temps = jnp.where(here, temp_ref[part * 4 + request], temps)
    logits = total * temps
    logits_ref[...] = logits
    top = jnp.max(logits, axis=1, keepdims=True)
    spot = top + jnp.log(jnp.sum(jnp.exp(logits - top), axis=1, keepdims=True))
    across = lax.broadcasted_iota(jnp.int32, (rows, 256), 0) == lax.broadcasted_iota(jnp.int32, (rows, 256), 1)
    mine = jnp.sum(jnp.where(across, spot, 0.0), axis=0, keepdims=True)
    if not flip:
        spot_ref[...] = mine
    else:
        first = refs[0][...]
        low, high = jnp.where(part == 1, first, mine), jnp.where(part == 1, mine, first)
        for copy in range(spot_ref.shape[0]):
            spot_ref[copy, :, 0:256] = low
            spot_ref[copy, :, 256:512] = high


def head(core, temps, tiles, gains, weight, first=None):
    rows = tiles.shape[1]
    flip = first is not None
    vmem, smem = pl.BlockSpec(memory_space=pltpu.VMEM), pl.BlockSpec(memory_space=pltpu.SMEM)
    extra = (first,) if flip else ()
    return pl.pallas_call(
        lambda *refs: head_kernel(*refs, flip=flip, width=2048),
        out_shape=(
            jax.ShapeDtypeStruct((rows, 256), F32),
            jax.ShapeDtypeStruct((32, 1, 512) if flip else (1, 256), F32),
        ),
        in_specs=[smem, smem, vmem, vmem, vmem] + [vmem] * len(extra),
        out_specs=(vmem, vmem),
        cost_estimate=pl.CostEstimate(
            flops=2 * rows * 2048 * 256, bytes_accessed=2 * 2048 * (rows + 256), transcendentals=rows * 256
        ),
        name="head_flip" if flip else "head_own",
    )(core, temps, tiles, gains, weight, *extra)


def pack_state(peak, mass, weighted):
    count = peak.shape[0]
    mass_high, mass_low = split2(mass)
    stats = jnp.stack([peak.astype(BF), mass_high, mass_low], axis=1).reshape(count, 6, 6)
    stats = jnp.pad(stats, ((0, 0), (0, 0), (0, 122)))
    return jnp.concatenate([weighted.astype(BF).reshape(count, 12, 128), stats], axis=1)


def merge_state(packed):
    count = packed.shape[0]
    weighted = packed[:, :12].reshape(count, 2, 6, 128).astype(F32)
    stats = packed[:, 12:, :6].astype(F32).reshape(count, 3, 2, 6)
    peaks, masses = stats[:, 0], stats[:, 1] + stats[:, 2]
    factor = jnp.exp(peaks - jnp.max(peaks, axis=0))
    return jnp.sum(masses * factor, axis=0), jnp.sum(weighted * factor[..., None], axis=0)


def on_device(
    hidden, ln1_gain, wq, wk, wv, wg, q_gain, key_gain, wo, ln2_gain, w_gate, w_up, w_down,
    last_gain, head_weight, inv_temp, key_cache, value_cache, lengths, parents, accepted,
):
    z, y, x, c = (lax.axis_index(name) for name in ("z", "y", "x", "c"))
    seq = z * 4 + y
    requests, tree = parents.shape
    slot_count = key_cache.shape[1]
    width = 2048


    vmem = pl.BlockSpec(memory_space=pltpu.VMEM)
    pieces, ffn = pl.pallas_call(
        pack_kernel,
        out_shape=(jax.ShapeDtypeStruct((4, 32, 896), BF), jax.ShapeDtypeStruct((32, 2560), BF)),
        in_specs=[vmem] * 12,
        out_specs=(vmem, vmem),
        name="pack",
    )(
        hidden.T, *(gain.reshape(1, 32) for gain in (ln1_gain, ln2_gain, last_gain)), wq, wk, wv, wg,
        w_gate, w_up, w_down.T, wo.T,
    )
    ffn = lax.all_gather(ffn, "z", axis=0, tiled=True)
    mine = swap(pieces, "y").reshape(128, 896)
    proj, side = mine[:, :768], mine[:, 768:]
    side_wide = side.astype(F32)
    ln1_row = side_wide[:, 96:97] + side_wide[:, 97:98] + side_wide[:, 98:99]
    scaled = (side_wide * ln1_row).astype(BF)
    partial = lax.dot_general(scaled, proj, (((0,), (0,)), ((), ())), preferred_element_type=F32)
    partial = partial[:96].astype(BF)

    def by_tile(values):
        split = values.reshape(16, 6, values.shape[1] // 128, 128)
        return jnp.swapaxes(split, 1, 2).reshape(16, -1, 128)

    sent = by_tile(jnp.concatenate([partial[:, :512], side.T[:96]], axis=1))
    caches = jnp.stack([key_cache, value_cache])
    parts = [
        lax.dynamic_slice(caches, (0, (y ^ shift) * 2, 0, 0), (2, 2, slot_count, 128))
        for shift in range(4)
    ]
    sent, parts = lax.optimization_barrier((sent, parts))
    got = swap(sent, "z")
    for shift in range(1, 4):
        parts[shift] = lax.ppermute(parts[shift], "y", [(i, i ^ shift) for i in range(4)])
    sums = jnp.sum(got[:, :24].astype(F32), axis=0).reshape(4, 6, 128)
    rows = got[:, 24:]
    rows_wide = rows.astype(F32)
    squares = jnp.sum(rows_wide * rows_wide, axis=(0, 2))
    scale1 = lax.rsqrt(squares / width + EPSILON)[:, None]
    sums = sums * scale1

    links = ancestry(parents)
    depth = jnp.sum((links > 0.5).astype(jnp.int32), axis=-1) - 1
    target = lengths[:, None] + depth
    first = y * 96 + z * 6
    my_places = lax.dynamic_slice(target.reshape(-1), (first,), (6,))
    inverse = ROPE_BASE ** (-jnp.arange(64, dtype=F32) / 64)
    angles = my_places.astype(F32)[:, None] * inverse[None, :]
    cosine, sine = jnp.cos(angles), jnp.sin(angles)
    query = rotate(head_norm(sums[:2], q_gain), cosine, sine) * 128 ** (-0.5)
    new_key = rotate(head_norm(sums[2], key_gain), cosine, sine)
    block = jnp.concatenate(
        [
            query.reshape(12, 128), new_key, sums[3],
            side[:, 99:105].T.astype(F32), jnp.zeros((2, 128), F32),
        ],
        axis=0,
    ).astype(BF)
    block, parts[1], parts[3] = lax.optimization_barrier((block, parts[1], parts[3]))
    gathered, moved = lax.optimization_barrier((spread(block, "z", 16), jnp.concatenate(parts, axis=2)))
    gain_all = gathered[:, 24:30].astype(F32)
    ln2_mine = gain_all[:, 0] + gain_all[:, 1] + gain_all[:, 2]
    ln2_mine = lax.dynamic_slice(ln2_mine, (0, y * 32), (16, 32)).reshape(1, 512)
    last_all = gain_all[:, 3] + gain_all[:, 4] + gain_all[:, 5]
    last_all = jnp.swapaxes(last_all.reshape(4, 4, 4, 32), 1, 2).reshape(16, 128)
    spot96 = jnp.arange(96, dtype=jnp.int32)
    origin = jnp.arange(4, dtype=jnp.int32)[:, None] * 6 + (spot96 // 6 * 24 + spot96 % 6)[None, :]
    gather = (origin.reshape(384, 1) == jnp.arange(384, dtype=jnp.int32)[None, :]).astype(BF)
    tokens = jnp.dot(gather, gathered[:, :24].reshape(384, 128), preferred_element_type=F32).astype(BF)
    queries = tokens[:192].reshape(2, 2, tree, 128)
    tree_keys = tokens[192:288].reshape(2, tree, 128)
    tree_values = tokens[288:].reshape(2, tree, 128)

    keys, values = moved[0], moved[1]
    my_lengths = lax.dynamic_slice(lengths, (2 * y,), (2,))
    my_links = lax.dynamic_slice(links, (2 * y, 0, 0), (2, tree, tree))
    source = (y ^ jnp.arange(4, dtype=jnp.int32)) + z * 4
    row_slots = (source[:, None] * slot_count + jnp.arange(slot_count, dtype=jnp.int32)).reshape(-1)
    valid_slot = (row_slots[None, :] < my_lengths[:, None])[:, None, None, :]
    valid_node = ((my_links > 0.5) & (z == 0))[:, None, :, :]
    scores = jnp.einsum("grid,rcd->rgic", queries, keys, preferred_element_type=F32)
    tree_scores = jnp.einsum("grid,rjd->rgij", queries, tree_keys, preferred_element_type=F32)
    peak = jnp.maximum(
        jnp.max(jnp.where(valid_slot, scores, NEGATIVE), axis=-1),
        jnp.max(jnp.where(valid_node, tree_scores, NEGATIVE), axis=-1),
    )
    peak = lax.reduce_precision(peak, 8, 7)
    weights = jnp.where(valid_slot, jnp.exp(scores - peak[..., None]), 0.0)
    tree_weights = jnp.where(valid_node, jnp.exp(tree_scores - peak[..., None]), 0.0)
    mass = jnp.sum(weights, axis=-1) + jnp.sum(tree_weights, axis=-1)
    weighted = jnp.einsum(
        "rgic,rcd->rgid", weights.astype(BF), values, preferred_element_type=F32
    ) + jnp.einsum("rgij,rjd->rgid", tree_weights.astype(BF), tree_values, preferred_element_type=F32)

    def by_z(values):
        rest = values.shape[3:]
        return jnp.swapaxes(values.reshape((2, 2, 8, 6) + rest), 1, 2).reshape((16, 2, 6) + rest)

    outgoing = pack_state(by_z(peak), by_z(mass), by_z(weighted))
    outgoing = jnp.concatenate([outgoing, by_tile(partial[:, 512:])], axis=1)
    arrived, last_all = lax.optimization_barrier((swap(outgoing, "z"), last_all))
    mass, weighted = merge_state(arrived[:, :18])
    gate = jnp.sum(arrived[:, 18:].astype(F32), axis=0).reshape(2, 6, 128)
    gated = weighted / mass[..., None] * jax.nn.sigmoid(gate * scale1)
    gated = gated.astype(BF).reshape(12, 128)
    residual = jnp.transpose(rows.reshape(4, 4, 6, 4, 32), (3, 0, 2, 1, 4)).reshape(4, 24, 128)
    same = jnp.concatenate([gated, tokens[192:]], axis=0)
    both = swap(jnp.concatenate([residual, jnp.broadcast_to(same[None], (4, 204, 128))], axis=1), "y")
    hidden_rows = jnp.swapaxes(both[:, :24].reshape(4, 4, 6, 128), 1, 2).reshape(24, 512)
    gated = jnp.swapaxes(both[:, 24:36].reshape(4, 2, 6, 128), 0, 1).reshape(2, 24, 128)

    contract = (((1,), (1,)), ((), ()))
    repeated = jnp.broadcast_to(jnp.concatenate([gated[0], gated[1]], axis=1)[None], (8, 24, 256))
    repeated = lax.optimization_barrier(repeated.reshape(192, 256))
    attn = lax.dot_general(
        repeated,
        ffn[:, 2304:],
        contract,
        preferred_element_type=F32,
    )
    attn = attn.astype(BF).reshape(8, 24, 512)
    attn, fresh = lax.optimization_barrier((attn, both[:, 36:]))
    tree_keys = fresh[:, :96].reshape(requests, tree, 128)
    tree_values = fresh[:, 96:].reshape(requests, tree, 128)

    slot_ids = seq * slot_count + jnp.arange(slot_count, dtype=jnp.int32)
    accepted_rows = links[jnp.arange(requests), accepted]
    placed = (slot_ids[None, :, None] == target[:, None, :]).astype(F32) * accepted_rows[:, None, :]
    hits = (jnp.sum(placed, axis=2) > 0.5)[:, :, None]
    placed = placed.astype(BF)
    moved_keys = jnp.einsum("rca,rae->rce", placed, tree_keys, preferred_element_type=F32).astype(BF)
    moved_values = jnp.einsum("rca,rae->rce", placed, tree_values, preferred_element_type=F32).astype(BF)
    updated_keys = jnp.where(hits, moved_keys, key_cache)
    updated_values = jnp.where(hits, moved_values, value_cache)

    attn, updated_keys, updated_values = lax.optimization_barrier(
        (swap(attn, ("x", "c")), updated_keys, updated_values)
    )
    attn = jnp.sum(attn.astype(F32), axis=0)
    middle = (hidden_rows.astype(F32) + attn).astype(BF)
    middle_wide = middle.astype(F32)
    squares_mid = split2(jnp.sum(middle_wide * middle_wide, axis=1, keepdims=True))
    units = jnp.dot(
        (middle_wide * ln2_mine).astype(BF), ffn[:, :1536], preferred_element_type=F32
    ).astype(BF)
    squares_mid = jnp.pad(jnp.concatenate(squares_mid, axis=1), ((0, 0), (0, 126)))
    units = spread(jnp.concatenate([units, squares_mid], axis=1), "y", 4)
    units = jnp.sum(units.astype(F32), axis=0)
    scale_mid = lax.rsqrt((units[:, 1536:1537] + units[:, 1537:1538]) / width + EPSILON)
    act = (jax.nn.silu(units[:, :768] * scale_mid) * (units[:, 768:1536] * scale_mid)).astype(BF)
    down = lax.dot_general(act, ffn[:, 1536:2304], contract, preferred_element_type=F32)
    down = jnp.transpose(down.astype(BF).reshape(2, 12, 4, 128), (2, 0, 1, 3)).reshape(8, 12, 128)
    down = jnp.sum(swap(down, ("x", "c")).astype(F32), axis=0)
    middle_mine = lax.dynamic_slice(middle, (c * 12, x * 128), (12, 128))
    following = (middle_mine.astype(F32) + down).astype(BF)

    half = spread(following, "z", 16).reshape(16, 2, 6, 128)
    half = jnp.swapaxes(half, 0, 1).reshape(192, 128)
    half = spread(half, ("y", "x"), 16)
    other = lax.ppermute(half, "c", [(0, 1), (1, 0)])
    core = c.reshape(1)
    own_logits, own_spot = head(core, inv_temp, half, last_all, head_weight)
    other_logits, spots = head(core, inv_temp, other, last_all, head_weight, own_spot)

    def in_order(mine_part, other_part):
        return jnp.concatenate(
            [jnp.where(c == 0, mine_part, other_part), jnp.where(c == 0, other_part, mine_part)], axis=0
        )

    def own_columns(tiles):
        return lax.dynamic_slice(tiles, (y * 4 + z // 4, 0, 0), (1, 192, 128)).reshape(192, 128)

    own = in_order(own_columns(half), own_columns(other))
    next_hidden = lax.dynamic_slice(own, (0, z % 4 * 32), (384, 32))
    spots = swap(spots, ("y", "x", "c"))
    top = jnp.max(spots, axis=0)
    spot = top + jnp.log(jnp.sum(jnp.exp(spots - top), axis=0))
    spots = spread(spot, "z", 16)
    top = jnp.max(spots, axis=0)
    spot = top + jnp.log(jnp.sum(jnp.exp(spots - top), axis=0))
    spot = spot.reshape(2, 256)[:, :192].reshape(384, 1)
    logprobs = in_order(own_logits, other_logits) - spot

    return logprobs, next_hidden, updated_keys, updated_values


def solution(mesh):
    grid = Mesh(mesh.devices.reshape(16, 4, 4, 2), ("z", "y", "x", "c"))
    seq, tp = ("z", "y"), ("x", "c")
    in_specs = (
        P(None, seq), P(seq), P(seq, tp), P(seq, tp), P(seq, tp), P(seq, tp), P(), P(),
        P(tp, seq), P(seq), P(seq, tp), P(seq, tp), P(tp, seq), P(seq),
        P(None, seq + tp), P(), P(None, seq, tp), P(None, seq, tp), P(), P(), P(),
    )
    out_specs = (P(None, seq + tp), P(None, seq), P(None, seq, tp), P(None, seq, tp))
    return jax.shard_map(on_device, mesh=grid, in_specs=in_specs, out_specs=out_specs, check_vma=False)
```
